32 devices in a mesh: dp: 4 (over x, core), mp: 8 (over z, y).
Axes of the slice: x: 2, y: 2, z: 4, core: 2. Of those that a mesh axis runs over, the one named last changes fastest.
Arguments:
- layer_input: bfloat16 [8192, 2048], P(('dp', 'mp')), may hold values from -6 to 6
- cotangent: bfloat16 [8192, 2048], P(('dp', 'mp')), may hold values from -6 to 6
- segment_ids: int32 [8192], P('dp'), may hold values from 0 to 11, as said below
- token_valid: int32 [8192], P('dp'), may hold values from 0 to 1, as said below
- norm_attn: bfloat16 [2048], replicated, may hold values from 0.099609375 to 1.8984375
- norm_mlp: bfloat16 [2048], replicated, may hold values from 0.099609375 to 1.8984375
- base_qkv: bfloat16 [3, 2048, 2048], P(None, None, 'mp'), may hold values from -0.125 to 0.125
- base_attn_out: bfloat16 [2048, 2048], P('mp'), may hold values from -0.125 to 0.125
- base_gate_up: bfloat16 [2, 2048, 5632], P(None, None, 'mp'), may hold values from -0.125 to 0.125
- base_down: bfloat16 [5632, 2048], P('mp'), may hold values from -0.078125 to 0.078125
- rank_in_attn: float32 [4, 2048, 16], P(None, ('dp', 'mp')), may hold values from -0.125 to 0.125
- rank_out_attn: float32 [4, 16, 2048], P(None, None, ('dp', 'mp')), may hold values from -0.36 to 0.36
- magnitude_qkv: float32 [3, 2048], P(None, ('dp', 'mp')), may hold values from 0.7 to 1.4
- magnitude_out: float32 [2048], P(('dp', 'mp')), may hold values from 3 to 12
- rank_in_mlp: float32 [2, 2048, 16], P(None, ('dp', 'mp')), may hold values from -0.125 to 0.125
- rank_out_mlp: float32 [2, 16, 5632], P(None, None, ('dp', 'mp')), may hold values from -0.36 to 0.36
- magnitude_mlp: float32 [2, 5632], P(None, ('dp', 'mp')), may hold values from 0.7 to 1.4
- rank_in_down: float32 [5632, 16], P(('dp', 'mp')), may hold values from -0.078125 to 0.078125
- rank_out_down: float32 [16, 2048], P(None, ('dp', 'mp')), may hold values from -0.36 to 0.36
- magnitude_down: float32 [2048], P(('dp', 'mp')), may hold values from 1 to 3
Outputs:
- layer_output: bfloat16 [8192, 2048], P(('dp', 'mp'))
- input_grad: float32 [8192, 2048], P(('dp', 'mp'))
- grad_rank_in_attn: float32 [4, 2048, 16], P(None, ('dp', 'mp'))
- grad_rank_out_attn: float32 [4, 16, 2048], P(None, None, ('dp', 'mp'))
- grad_magnitude_qkv: float32 [3, 2048], P(None, ('dp', 'mp'))
- grad_magnitude_out: float32 [2048], P(('dp', 'mp'))
- grad_rank_in_mlp: float32 [2, 2048, 16], P(None, ('dp', 'mp'))
- grad_rank_out_mlp: float32 [2, 16, 5632], P(None, None, ('dp', 'mp'))
- grad_magnitude_mlp: float32 [2, 5632], P(None, ('dp', 'mp'))
- grad_rank_in_down: float32 [5632, 16], P(('dp', 'mp'))
- grad_rank_out_down: float32 [16, 2048], P(None, ('dp', 'mp'))
- grad_magnitude_down: float32 [2048], P(('dp', 'mp'))
The draws below stay inside these ranges and needn't reach their ends.
Inputs may be any that keep to these rules, and one draw needn't show every extreme that they name: `segment_ids`: ids never decrease along a row of 2048 tokens (each segment is one contiguous run), and no two rows share an id. `token_valid`: padding forms a tail of each row of 2048 tokens.
All inputs are finite; a program needn't handle non-finite values.
Results may differ from the reference program's by a relative error of at most 0.024.
Values may be sent and summed in bfloat16 or wider, within the bound.
No kernel may reach another device: no remote copies, remote signals or barrier semaphores. Data moves between devices by JAX's collectives and lax.ppermute only.
A program may use at most 320 MiB of HBM per device.

```python
import math
from functools import partial
import jax
import jax.numpy as jnp
from jax import lax

D = 2048
H = 16
HD = 128
FF = 5632
R = 16
ALPHA = 32
S = 2048
TOKENS = 8192


def row_layout(key):
    row_count = TOKENS // S
    base_key = jax.random.fold_in(key, 11)
    first_key, second_key, third_key = jax.random.split(base_key, 3)
    opening = jax.random.randint(first_key, (row_count, 1), 1, S // 32 + 1)
    closing_gap = jax.random.randint(second_key, (row_count, 1), S // 64 + 1, S // 16)
    padding = 1 + jax.random.randint(third_key, (row_count, 1), 0, 1 << 20) % (closing_gap - 1)
    position = jnp.arange(S, dtype=jnp.int32)[None, :]
    closing = S - closing_gap
    segment = (position >= opening).astype(jnp.int32) + (position >= closing).astype(jnp.int32) + 3 * jnp.arange(row_count, dtype=jnp.int32)[:, None]
    valid = (position < S - padding).astype(jnp.int32)
    return (segment.reshape(TOKENS), valid.reshape(TOKENS))


def draw_segment_ids(key, part):
    return row_layout(key)[0]


def draw_token_valid(key, part):
    return row_layout(key)[1]


def level_of(stream_key, dims, shards, low, top_value):
    def one(dim, blocks):
        draws = jax.random.uniform(jax.random.fold_in(jax.random.fold_in(stream_key, 6), dim), (blocks,), jnp.float32, low / len(shards), top_value / len(shards))
        return jnp.repeat(jnp.exp(draws), dims[dim] // blocks).reshape((-1,) + (1,) * (len(dims) - dim - 1))

    loudness = one(*shards[0])
    for cut in shards[1:]:
        loudness = loudness * one(*cut)
    return loudness


def normal_values(rng, shape, scale, bound, pieces=(), kind=jnp.bfloat16):
    entries = jax.random.normal(rng, shape, jnp.float32) * scale
    if len(pieces) > 0:
        entries = level_of(rng, shape, pieces, -0.22, 0.18) * entries
    return jnp.clip(entries, min=-bound, max=bound).astype(kind)


def setup_inputs(seed: int = 0) -> dict:
    seeds = jax.random.split(jax.random.key(seed), 21)
    layer_input = normal_values(seeds[0], (TOKENS, D), 1.0, 6.0, ((0, 32),))
    cotangent = normal_values(seeds[1], (TOKENS, D), 1.0, 6.0, ((0, 32),))
    segment_ids = draw_segment_ids(jax.random.fold_in(seeds[20], 71), 0)
    token_valid = draw_token_valid(jax.random.fold_in(seeds[20], 71), 0)
    norm_attn = jnp.clip(1.0 + 0.18 * jax.random.normal(seeds[4], (D,), jnp.float32), 0.099609375, 1.8984375).astype(jnp.bfloat16)
    norm_mlp = jnp.clip(1.0 + 0.18 * jax.random.normal(seeds[5], (D,), jnp.float32), 0.099609375, 1.8984375).astype(jnp.bfloat16)
    base_qkv = normal_values(seeds[6], (3, D, D), D ** -0.5, 0.125, ((2, 8),))
    base_attn_out = normal_values(seeds[7], (D, D), D ** -0.5, 0.125, ((0, 8),))
    base_gate_up = normal_values(seeds[8], (2, D, FF), D ** -0.5, 0.125, ((2, 8),))
    base_down = normal_values(seeds[9], (FF, D), FF ** -0.5, 0.078125, ((0, 8),))
    rank_in_attn = normal_values(seeds[10], (4, D, R), D ** -0.5, 0.125, ((1, 32),), jnp.float32)
    rank_out_attn = normal_values(seeds[11], (4, R, D), 0.06, 0.36, ((2, 32),), jnp.float32)
    magnitude_qkv = jnp.clip(jnp.exp(math.log(1.4) - 0.6931472 * jax.random.uniform(seeds[12], (3, D), jnp.float32) ** level_of(seeds[12], (3, D), ((1, 32),), -0.2, 0.2)), 0.7, 1.4)
    magnitude_out = jnp.clip(jnp.exp(math.log(12.0) - 1.3862944 * jax.random.uniform(seeds[13], (D,), jnp.float32) ** level_of(seeds[13], (D,), ((0, 32),), -0.2, 0.2)), 3.0, 12.0)
    rank_in_mlp = normal_values(seeds[14], (2, D, R), D ** -0.5, 0.125, ((1, 32),), jnp.float32)
    rank_out_mlp = normal_values(seeds[15], (2, R, FF), 0.06, 0.36, ((2, 32),), jnp.float32)
    magnitude_mlp = jnp.clip(jnp.exp(math.log(1.4) - 0.6931472 * jax.random.uniform(seeds[16], (2, FF), jnp.float32) ** level_of(seeds[16], (2, FF), ((1, 32),), -0.2, 0.2)), 0.7, 1.4)
    rank_in_down = normal_values(seeds[17], (FF, R), FF ** -0.5, 0.078125, ((0, 32),), jnp.float32)
    rank_out_down = normal_values(seeds[18], (R, D), 0.06, 0.36, ((1, 32),), jnp.float32)
    magnitude_down = jnp.clip(jnp.exp(math.log(3.0) - 1.0986123 * jax.random.uniform(seeds[19], (D,), jnp.float32) ** level_of(seeds[19], (D,), ((0, 32),), -0.2, 0.2)), 1.0, 3.0)
    return {"layer_input": layer_input, "cotangent": cotangent, "segment_ids": segment_ids, "token_valid": token_valid, "norm_attn": norm_attn, "norm_mlp": norm_mlp, "base_qkv": base_qkv, "base_attn_out": base_attn_out, "base_gate_up": base_gate_up, "base_down": base_down, "rank_in_attn": rank_in_attn, "rank_out_attn": rank_out_attn, "magnitude_qkv": magnitude_qkv, "magnitude_out": magnitude_out, "rank_in_mlp": rank_in_mlp, "rank_out_mlp": rank_out_mlp, "magnitude_mlp": magnitude_mlp, "rank_in_down": rank_in_down, "rank_out_down": rank_out_down, "magnitude_down": magnitude_down}


EXACT = lax.Precision.HIGHEST
EPSILON = 1e-05
ROPE_BASE = 10000.0

@jax.custom_vjp
def low(v):
    return lax.optimization_barrier(v.astype(jnp.bfloat16)).astype(jnp.float32)

@jax.custom_vjp
def low_back(v):
    return v

def low_keep(v):
    return (low(v), None)

def low_pass(kept, grad):
    return (grad,)

def back_keep(v):
    return (v, None)

def back_low(kept, grad):
    return (low(grad),)
low.defvjp(low_keep, low_pass)
low_back.defvjp(back_keep, back_low)

def matmul(left, right):
    return jnp.dot(left, right, precision=EXACT)

def positions_of(segments):
    total_len = segments.shape[0]
    steps_idx = jnp.arange(total_len, dtype=jnp.int32)
    earlier = jnp.concatenate([segments[:1] - 1, segments[:-1]])
    begins = (steps_idx % S == 0) | (segments != earlier)
    first_idx = lax.cummax(jnp.where(begins, steps_idx, 0), axis=0)
    return steps_idx - first_idx

def rotary_tables(positions):
    half_width = HD // 2
    inverse_freq = ROPE_BASE ** (-(2.0 * jnp.arange(half_width, dtype=jnp.float32)) / HD)
    angle = positions.astype(jnp.float32)[:, None] * inverse_freq[None, :]
    return (jnp.cos(angle)[:, None, :], jnp.sin(angle)[:, None, :])

def rotate(values, cosine, sine):
    half_width = values.shape[-1] // 2
    first_half = values[..., :half_width]
    second_half = values[..., half_width:]
    return jnp.concatenate([first_half * cosine - second_half * sine, second_half * cosine + first_half * sine], axis=-1)

def rms_normed(values, gain):
    inverse = lax.rsqrt(lax.optimization_barrier(jnp.mean(values * values, axis=-1, keepdims=True)) + EPSILON)
    return values * inverse * gain

def dora(base, rank_in, rank_out, magnitude):
    merged = base + ALPHA / R * matmul(low(rank_in), low(rank_out))
    norms = jnp.sqrt(lax.optimization_barrier(jnp.sum(merged * merged, axis=0)))
    return (low(merged), low(magnitude) / norms)

def row_attention(inputs):
    queries, key_heads, value_heads, segments, valid = inputs
    scores = low_back(jnp.einsum('qhd,khd->hqk', queries, key_heads, precision=EXACT))
    position = jnp.arange(S, dtype=jnp.int32)
    allowed = (segments[:, None] == segments[None, :]) & (position[None, :] <= position[:, None]) & ((valid[None, :] == 1) | (position[:, None] == position[None, :]))
    attn_weights = jax.nn.softmax(jnp.where(allowed[None], scores, -1e+30), axis=-1)
    return jnp.einsum('hqk,khd->qhd', low(attn_weights), value_heads, precision=EXACT)

def forward(layer_input, rank_in_attn, rank_out_attn, magnitude_qkv, magnitude_out, rank_in_mlp, rank_out_mlp, magnitude_mlp, rank_in_down, rank_out_down, magnitude_down, frozen=None):
    norm_attn, norm_mlp, base_qkv, base_attn_out, base_gate_up, base_down, cosine, sine, segment_ids, token_valid = frozen
    normed_one = low(rms_normed(layer_input, norm_attn))
    projected = []
    for member in range(3):
        merged, column_scale = dora(base_qkv[member], rank_in_attn[member], rank_out_attn[member], magnitude_qkv[member])
        projected.append(low_back(matmul(normed_one, merged)) * column_scale)
    heads_shape = (TOKENS, H, HD)
    queries = low(rotate(projected[0].reshape(heads_shape), cosine, sine) * HD ** (-0.5))
    key_heads = low(rotate(projected[1].reshape(heads_shape), cosine, sine))
    value_heads = low(projected[2].reshape(heads_shape))
    rows_shape = (TOKENS // S, S, H, HD)
    attended = lax.map(jax.checkpoint(row_attention), (queries.reshape(rows_shape), key_heads.reshape(rows_shape), value_heads.reshape(rows_shape), segment_ids.reshape(TOKENS // S, S), token_valid.reshape(TOKENS // S, S)))
    attended = low(low_back(attended.reshape(TOKENS, D)))
    merged, column_scale = dora(base_attn_out, rank_in_attn[3], rank_out_attn[3], magnitude_out)
    residual = layer_input + low_back(matmul(attended, merged)) * column_scale
    normed_two = low(rms_normed(residual, norm_mlp))
    gate_merged, gate_scale = dora(base_gate_up[0], rank_in_mlp[0], rank_out_mlp[0], magnitude_mlp[0])
    up_merged, up_scale = dora(base_gate_up[1], rank_in_mlp[1], rank_out_mlp[1], magnitude_mlp[1])
    gate = low_back(matmul(normed_two, gate_merged)) * gate_scale
    upward = low_back(matmul(normed_two, up_merged)) * up_scale
    hidden = low(jax.nn.silu(gate) * upward)
    down_merged, down_scale = dora(base_down, rank_in_down, rank_out_down, magnitude_down)
    return residual + low_back(matmul(hidden, down_merged)) * down_scale

def reference(layer_input, cotangent, segment_ids, token_valid, norm_attn, norm_mlp, base_qkv, base_attn_out, base_gate_up, base_down, rank_in_attn, rank_out_attn, magnitude_qkv, magnitude_out, rank_in_mlp, rank_out_mlp, magnitude_mlp, rank_in_down, rank_out_down, magnitude_down):
    positions = positions_of(segment_ids)
    cosine, sine = rotary_tables(positions)
    frozen = (norm_attn.astype(jnp.float32), norm_mlp.astype(jnp.float32), base_qkv.astype(jnp.float32), base_attn_out.astype(jnp.float32), base_gate_up.astype(jnp.float32), base_down.astype(jnp.float32), cosine, sine, segment_ids, token_valid)
    output, pullback = jax.vjp(partial(forward, frozen=frozen), layer_input.astype(jnp.float32), rank_in_attn, rank_out_attn, magnitude_qkv, magnitude_out, rank_in_mlp, rank_out_mlp, magnitude_mlp, rank_in_down, rank_out_down, magnitude_down)
    grads = pullback(cotangent.astype(jnp.float32))
    return (output.astype(jnp.bfloat16), grads[0], grads[1], grads[2], grads[3], grads[4], grads[5], grads[6], grads[7], grads[8], grads[9], grads[10])
```

```python
import functools

import jax
import jax.numpy as jnp
import numpy as np
from jax import lax
from jax.experimental import pallas as pl
from jax.experimental.pallas import tpu as pltpu
from jax.sharding import Mesh
from jax.sharding import PartitionSpec as P

HD = 128
R = 16
ALPHA = 32
FACTOR = ALPHA / R
EPSILON = 1e-05
ROPE_BASE = 10000.0
BF16 = jnp.bfloat16
F32 = jnp.float32
NEG = -1e30
AXES = ("x", "c", "zh", "zl", "y")
VM = pl.BlockSpec(memory_space=pltpu.VMEM)
SM = pl.BlockSpec(memory_space=pltpu.SMEM)


def mm(left, right, lc=1, rc=0, precision=None):
    return lax.dot_general(
        left,
        right,
        (((lc,), (rc,)), ((), ())),
        preferred_element_type=F32,
        precision=precision,
    )


def params(mib=58):
    return pltpu.CompilerParams(vmem_limit_bytes=mib * 1024 * 1024)


def cost(flops, nbytes, trans=0):
    return pl.CostEstimate(
        flops=int(flops), bytes_accessed=int(nbytes), transcendentals=int(trans)
    )


def pack_kernel(a_w, f_w, a1, b1, mq, mo, a2, b2, mm_, a3, b3, md, out):
    out[...] = jnp.zeros(out.shape, out.dtype)

    def turned(block):
        width = block.shape[0]
        eye = (
            lax.broadcasted_iota(jnp.int32, (width, width), 0)
            == lax.broadcasted_iota(jnp.int32, (width, width), 1)
        ).astype(BF16)
        return mm(block.astype(BF16), eye, 0, 0).astype(BF16)

    for p in range(4):
        out[0, :R, p * a_w : (p + 1) * a_w] = turned(a1[p])
    for p in range(2):
        out[0, :R, (4 + p) * a_w : (5 + p) * a_w] = turned(a2[p])
    at = 6 * a_w
    out[0, :R, at : at + f_w] = turned(a3[...])
    at += f_w
    for p in range(4):
        out[0, :R, at : at + a_w] = b1[p].astype(BF16)
        at += a_w
    for p in range(2):
        out[0, :R, at : at + f_w] = b2[p].astype(BF16)
        at += f_w
    out[0, :R, at : at + a_w] = b3[...].astype(BF16)
    at = 0
    for p in range(3):
        out[0, R : R + 1, at : at + a_w] = mq[p : p + 1, :].astype(BF16)
        at += a_w
    out[0, R : R + 1, at : at + a_w] = mo[...].astype(BF16)
    at += a_w
    for p in range(2):
        out[0, R : R + 1, at : at + f_w] = mm_[p : p + 1, :].astype(BF16)
        at += f_w
    out[0, R : R + 1, at : at + a_w] = md[...].astype(BF16)


def unpack_kernel(
    a_w, f_w, dp, order, where_, g, at_qkv, at_gu, at_o, at_d, at_o0, at_d0,
    b_qkv, b_gu, b_o, b_d, m_qkv, m_o, m_gu, m_d,
):
    n = g.shape[0]
    b_at = 6 * a_w + f_w
    for d in range(n):
        s = order[d]
        lo, hi = d * a_w, (d + 1) * a_w
        for p in range(3):
            at_qkv[p * R : (p + 1) * R, lo:hi] = g[s, :R, p * a_w : (p + 1) * a_w]
        for p in range(2):
            at_gu[p, :, lo:hi] = g[s, :R, (4 + p) * a_w : (5 + p) * a_w]
        b_o[:, lo:hi] = g[s, :R, b_at + 3 * a_w : b_at + 4 * a_w]
        end = b_at + 4 * a_w + 2 * f_w
        b_d[:, lo:hi] = g[s, :R, end : end + a_w]
        m_o[:, lo:hi] = g[s, R : R + 1, 3 * a_w : 4 * a_w].astype(F32)
        end = 4 * a_w + 2 * f_w
        m_d[:, lo:hi] = g[s, R : R + 1, end : end + a_w].astype(F32)
    for i in range(dp):
        s = order[where_[0] * dp + i]
        lo, hi = i * a_w, (i + 1) * a_w
        flo, fhi = i * f_w, (i + 1) * f_w
        at_o[:, lo:hi] = g[s, :R, 3 * a_w : 4 * a_w]
        at_d[:, flo:fhi] = g[s, :R, 6 * a_w : 6 * a_w + f_w]
        for p in range(3):
            b_qkv[p, :, lo:hi] = g[s, :R, b_at + p * a_w : b_at + (p + 1) * a_w]
            m_qkv[p, :, lo:hi] = g[s, R : R + 1, p * a_w : (p + 1) * a_w].astype(F32)
        for p in range(2):
            e = b_at + 4 * a_w + p * f_w
            b_gu[p, :, flo:fhi] = g[s, :R, e : e + f_w]
            e = 4 * a_w + p * f_w
            m_gu[p, :, flo:fhi] = g[s, R : R + 1, e : e + f_w].astype(F32)
        s = order[where_[1] * dp + i]
        at_o0[:, lo:hi] = g[s, :R, 3 * a_w : 4 * a_w]
        at_d0[:, flo:fhi] = g[s, :R, 6 * a_w : 6 * a_w + f_w]


def pack_grads_kernel(
    a_w, f_w, dp, order, where_, ga_full, gb_full, m_full, ga_attn, ga_d, gb_qkv, gb_gu,
    m_qkv, m_gu, out
):
    n = out.shape[0]
    out[...] = jnp.zeros(out.shape, out.dtype)
    b_at = 6 * a_w + f_w
    dt = out.dtype
    for d in range(n):
        s = order[d]
        lo, hi = d * a_w, (d + 1) * a_w
        for i, p in enumerate((0, 1, 2, 4, 5)):
            out[s, :R, p * a_w : (p + 1) * a_w] = ga_full[i * R : (i + 1) * R, lo:hi].astype(dt)
        out[s, :R, b_at + 3 * a_w : b_at + 4 * a_w] = gb_full[:R, lo:hi].astype(dt)
        end = b_at + 4 * a_w + 2 * f_w
        out[s, :R, end : end + a_w] = gb_full[R:, lo:hi].astype(dt)
        out[s, R : R + 1, 3 * a_w : 4 * a_w] = m_full[0:1, lo:hi].astype(dt)
        end = 4 * a_w + 2 * f_w
        out[s, R : R + 1, end : end + a_w] = m_full[1:2, lo:hi].astype(dt)
    for i in range(dp):
        s = order[where_[0] * dp + i]
        lo, hi = i * a_w, (i + 1) * a_w
        flo, fhi = i * f_w, (i + 1) * f_w
        out[s, :R, 3 * a_w : 4 * a_w] = ga_attn[:, lo:hi].astype(dt)
        out[s, :R, 6 * a_w : 6 * a_w + f_w] = ga_d[:, flo:fhi].astype(dt)
        for p in range(3):
            out[s, :R, b_at + p * a_w : b_at + (p + 1) * a_w] = gb_qkv[p, :, lo:hi].astype(dt)
            out[s, R : R + 1, p * a_w : (p + 1) * a_w] = m_qkv[p, :, lo:hi].astype(dt)
        for p in range(2):
            e = b_at + 4 * a_w + p * f_w
            out[s, :R, e : e + f_w] = gb_gu[p, :, flo:fhi].astype(dt)
            e = 4 * a_w + p * f_w
            out[s, R : R + 1, e : e + f_w] = m_gu[p, :, flo:fhi].astype(dt)


def merge_cols_kernel(x_parts, flags, own, *refs):
    parts = refs[:x_parts]
    at, b, vb, ssq = refs[x_parts:]
    h = pl.program_id(2)
    k = lax.rem(h - flags[1] + x_parts, x_parts)
    w = parts[0][0]
    for i in range(1, x_parts):
        w = jnp.where(k == i, parts[i][0], w)
    w = jnp.where(flags[0] == 1, own[0], w)
    v = w.astype(F32) + FACTOR * mm(at[...], b[0], 0, 0)
    vb[...] = v.astype(BF16)

    @pl.when(h == 0)
    def _():
        ssq[...] = jnp.zeros_like(ssq)

    ssq[...] += jnp.sum(v * v, axis=0, keepdims=True)


def merge_qkv(flags, own, parts, at_qkv, b_qkv):
    members, rows, width = own.shape
    heads = width // HD
    xs = len(parts)
    part_rows = rows // xs
    spec = pl.BlockSpec((1, part_rows, HD), lambda p, h, t, f: (p, 0, h))
    return pl.pallas_call(
        functools.partial(merge_cols_kernel, xs),
        grid_spec=pltpu.PrefetchScalarGridSpec(
            num_scalar_prefetch=1,
            grid=(members, heads, xs),
            in_specs=[pl.BlockSpec((1, part_rows, HD), lambda p, h, t, f: (p, t, h))]
            + [spec] * xs
            + [
                pl.BlockSpec((R, part_rows), lambda p, h, t, f: (p, t)),
                pl.BlockSpec((1, R, HD), lambda p, h, t, f: (p, 0, h)),
            ],
            out_specs=[
                pl.BlockSpec((part_rows, HD), lambda p, h, t, f: (t, h * members + p)),
                pl.BlockSpec((1, HD), lambda p, h, t, f: (0, h * members + p)),
            ],
        ),
        out_shape=[
            jax.ShapeDtypeStruct((rows, members * width), BF16),
            jax.ShapeDtypeStruct((1, members * width), F32),
        ],
        compiler_params=params(),
        cost_estimate=cost(2 * rows * width * members * 256, 4 * members * rows * width * 2),
    )(flags, own, *parts, at_qkv, b_qkv)


def merge_gu_kernel(x_parts, flags, own, *refs):
    parts = refs[:x_parts]
    at, b, vb, ssq = refs[x_parts:]
    h = pl.program_id(1)
    k = lax.rem(h - flags[1] + x_parts, x_parts)
    w = parts[0][0]
    for i in range(1, x_parts):
        w = jnp.where(k == i, parts[i][0], w)
    w = jnp.where(flags[0] == 1, own[0], w)
    v = w.astype(F32) + FACTOR * mm(at[0], b[0], 0, 0)
    vb[0] = v.astype(BF16)

    @pl.when(h == 0)
    def _():
        ssq[...] = jnp.zeros_like(ssq)

    ssq[0] += jnp.sum(v * v, axis=0, keepdims=True)


def merge_gu(flags, own, parts, at_gu, b_gu):
    members, rows, width = own.shape
    xs = len(parts)
    part_rows = rows // xs
    return pl.pallas_call(
        functools.partial(merge_gu_kernel, xs),
        grid_spec=pltpu.PrefetchScalarGridSpec(
            num_scalar_prefetch=1,
            grid=(members, xs),
            in_specs=[pl.BlockSpec((1, part_rows, width), lambda p, t, f: (p, t, 0))]
            + [pl.BlockSpec((1, part_rows, width), lambda p, t, f: (p, 0, 0))] * xs
            + [
                pl.BlockSpec((1, R, part_rows), lambda p, t, f: (p, 0, t)),
                pl.BlockSpec((1, R, width), lambda p, t, f: (p, 0, 0)),
            ],
            out_specs=[
                pl.BlockSpec((1, part_rows, width), lambda p, t, f: (p, t, 0)),
                pl.BlockSpec((1, 1, width), lambda p, t, f: (p, 0, 0)),
            ],
        ),
        out_shape=[
            jax.ShapeDtypeStruct((members, rows, width), BF16),
            jax.ShapeDtypeStruct((members, 1, width), F32),
        ],
        compiler_params=params(),
        cost_estimate=cost(2 * rows * width * members * 256, 4 * members * rows * width * 2),
    )(flags, own, *parts, at_gu, b_gu)


def merge_rows_kernel(x_parts, flags, own, *refs):
    parts = refs[:x_parts]
    at, b, vb = refs[x_parts:]
    k = lax.rem(pl.program_id(0) - flags[1] + x_parts, x_parts)
    w = parts[0][...]
    for i in range(1, x_parts):
        w = jnp.where(k == i, parts[i][...], w)
    w = jnp.where(flags[0] == 1, own[...], w)
    v = w.astype(F32) + FACTOR * mm(at[...], b[...], 0, 0)
    vb[...] = v.astype(BF16)


def merge_rows(flags, own, parts, at, b):
    rows, width = own.shape
    xs = len(parts)
    part = width // xs
    return pl.pallas_call(
        functools.partial(merge_rows_kernel, xs),
        grid_spec=pltpu.PrefetchScalarGridSpec(
            num_scalar_prefetch=1,
            grid=(xs,),
            in_specs=[pl.BlockSpec((rows, part), lambda t, f: (0, t))]
            + [pl.BlockSpec((rows, part), lambda t, f: (0, 0))] * xs
            + [
                pl.BlockSpec((R, rows), lambda t, f: (0, 0)),
                pl.BlockSpec((R, part), lambda t, f: (0, t)),
            ],
            out_specs=pl.BlockSpec((rows, part), lambda t, f: (0, t)),
        ),
        out_shape=jax.ShapeDtypeStruct((rows, width), BF16),
        compiler_params=params(),
        cost_estimate=cost(2 * rows * width * 256, 4 * rows * width * 2),
    )(flags, own, *parts, at, b)


def qkv_kernel(rows, blk, *refs):
    count = len(rows)
    xs = refs[:count]
    w, scale, cos0, cos1, sin0, sin1, out = refs[count:]
    cos = jnp.concatenate([cos0[...], cos1[...]], axis=0)
    sin = jnp.concatenate([sin0[...], sin1[...]], axis=0)
    at = 0
    for x, r in zip(xs, rows):
        z = mm(x[...], w[...]) * scale[...]
        co, si = cos[at : at + r], sin[at : at + r]
        q = z[:, :HD]
        k = z[:, HD : 2 * HD]
        q = (q * co + pltpu.roll(q, HD // 2, 1) * si) * HD ** (-0.5)
        k = k * co + pltpu.roll(k, HD // 2, 1) * si
        out[at : at + r, :HD] = q.astype(BF16)
        out[at : at + r, HD : 2 * HD] = k.astype(BF16)
        out[at : at + r, 2 * HD :] = z[:, 2 * HD :].astype(BF16)
        at += r


def qkv_chunk(blk, chunk, pieces, w, scale, cos, sin):
    rows = [p.shape[0] for p in pieces]
    total = sum(rows)
    tokens = total // 2
    depth, width = w.shape
    heads = width // (3 * HD)

    def table(k):
        return pl.BlockSpec((tokens, HD), lambda h, b: (b[2 * chunk + k], 0))

    return pl.pallas_call(
        functools.partial(qkv_kernel, rows),
        grid_spec=pltpu.PrefetchScalarGridSpec(
            num_scalar_prefetch=1,
            grid=(heads,),
            in_specs=[pl.BlockSpec((r, depth), lambda h, b: (0, 0)) for r in rows]
            + [
                pl.BlockSpec((depth, 3 * HD), lambda h, b: (0, h)),
                pl.BlockSpec((1, 3 * HD), lambda h, b: (0, h)),
                table(0),
                table(1),
                table(0),
                table(1),
            ],
            out_specs=pl.BlockSpec((total, 3 * HD), lambda h, b: (0, h)),
        ),
        out_shape=jax.ShapeDtypeStruct((total, width), BF16),
        compiler_params=params(),
        cost_estimate=cost(2 * total * depth * width, 2 * (depth * width + total * depth)),
    )(blk, *pieces, w, scale, cos, cos, sin, sin)


def masked(scores, low, first_key, first_query, valid_count):
    keys = first_key + lax.broadcasted_iota(jnp.int32, scores.shape, 0)
    queries = first_query + lax.broadcasted_iota(jnp.int32, (1, scores.shape[1]), 1)
    high = jnp.minimum(queries, valid_count - 1)
    allowed = ((keys >= low) & (keys <= high)) | (keys == queries)
    return jnp.where(allowed, scores, NEG)


def attn_fwd_kernel(n_chunks, tokens, bq, info, *refs):
    chunks = refs[:n_chunks]
    low, qkv_abs, att_abs, att_slot, lse, m_sc, l_sc, acc = refs[n_chunks:]
    i = pl.program_id(1)
    last = pl.num_programs(1) - 1
    slots = 2 * n_chunks
    valid_count = info[slots]

    @pl.when(i == 0)
    def _():
        for s in range(slots):
            start = pl.multiple_of(info[s] * tokens, tokens)
            qkv_abs[pl.ds(start, tokens), :] = chunks[s // 2][
                (s % 2) * tokens : (s % 2 + 1) * tokens, :
            ]

    q0 = pl.multiple_of(i * bq, bq)
    q = qkv_abs[pl.ds(q0, bq), :HD]
    lo = low[:, pl.ds(q0, bq)]
    m_sc[...] = jnp.full(m_sc.shape, NEG, F32)
    l_sc[...] = jnp.zeros_like(l_sc)
    acc[...] = jnp.zeros_like(acc)

    def step(j, carry):
        k0 = pl.multiple_of(j * bq, bq)
        k = qkv_abs[pl.ds(k0, bq), HD : 2 * HD]
        v = qkv_abs[pl.ds(k0, bq), 2 * HD :]
        s = masked(mm(k, q, 1, 1), lo, k0, q0, valid_count)
        m_old = m_sc[...]
        m_new = jnp.maximum(m_old, jnp.max(s, axis=0, keepdims=True))
        p = jnp.exp(s - m_new)
        alpha = jnp.exp(m_old - m_new)
        m_sc[...] = m_new
        l_sc[...] = l_sc[...] * alpha + jnp.sum(p, axis=0, keepdims=True)
        acc[...] = acc[...] * alpha + mm(v, p.astype(BF16), 0, 0)
        return carry

    lax.fori_loop(info[slots + 1 + i], i + 1, step, 0)
    total = l_sc[...]
    lse[0, :, pl.ds(q0, bq)] = m_sc[...] + jnp.log(total)
    att_abs[pl.ds(q0, bq), :] = (acc[...] / total).T.astype(BF16)

    @pl.when(i == last)
    def _():
        for s in range(slots):
            start = pl.multiple_of(info[s] * tokens, tokens)
            att_slot[s * tokens : (s + 1) * tokens, :] = att_abs[pl.ds(start, tokens), :]


def attn_fwd(info, chunks, low, tokens, bq):
    rows, width = chunks[0].shape
    heads = width // (3 * HD)
    seq = rows * len(chunks)
    n_blocks = seq // bq
    whole = pl.BlockSpec((seq, HD), lambda h, i, f: (0, h))
    return pl.pallas_call(
        functools.partial(attn_fwd_kernel, len(chunks), tokens, bq),
        grid_spec=pltpu.PrefetchScalarGridSpec(
            num_scalar_prefetch=1,
            grid=(heads, n_blocks),
            in_specs=[pl.BlockSpec((rows, 3 * HD), lambda h, i, f: (0, h))] * len(chunks)
            + [pl.BlockSpec((1, seq), lambda h, i, f: (0, 0))],
            out_specs=[
                pl.BlockSpec((seq, 3 * HD), lambda h, i, f: (0, h)),
                whole,
                whole,
                pl.BlockSpec((1, 1, seq), lambda h, i, f: (h, 0, 0)),
            ],
            scratch_shapes=[
                pltpu.VMEM((1, bq), F32),
                pltpu.VMEM((1, bq), F32),
                pltpu.VMEM((HD, bq), F32),
            ],
        ),
        out_shape=[
            jax.ShapeDtypeStruct((seq, width), BF16),
            jax.ShapeDtypeStruct((seq, heads * HD), BF16),
            jax.ShapeDtypeStruct((seq, heads * HD), BF16),
            jax.ShapeDtypeStruct((heads, 1, seq), F32),
        ],
        compiler_params=params(),
        cost_estimate=cost(
            4 * heads * seq * seq * HD, 2 * seq * width * 3, heads * seq * seq // 2
        ),
    )(info, *chunks, low)


def attn_bwd_kernel(
    n_chunks, tokens, bq, info, qkv, *refs
):
    dos = refs[:n_chunks]
    att, lse, low, cos, sin, scale, dz, dc, do_abs, delta, dq, dk, dv = refs[n_chunks:]
    slots = 2 * n_chunks
    valid_count = info[slots]
    seq = qkv.shape[0]
    n_blocks = seq // bq
    for s in range(slots):
        start = pl.multiple_of(info[s] * tokens, tokens)
        do_abs[pl.ds(start, tokens), :] = dos[s // 2][(s % 2) * tokens : (s % 2 + 1) * tokens, :]
    ones = jnp.ones((8, HD), F32)
    for i in range(n_blocks):
        r = slice(i * bq, (i + 1) * bq)
        prod = do_abs[r, :].astype(F32) * att[r, :].astype(F32)
        delta[:, r] = mm(ones, prod, 1, 1, lax.Precision.HIGHEST)[:1]
    dq[...] = jnp.zeros_like(dq)

    def outer(j, carry):
        k0 = pl.multiple_of(j * bq, bq)
        k = qkv[pl.ds(k0, bq), HD : 2 * HD]
        v = qkv[pl.ds(k0, bq), 2 * HD :]
        krow = pl.ds(k0, bq)
        dk[krow, :] = jnp.zeros((bq, HD), F32)
        dv[krow, :] = jnp.zeros((bq, HD), F32)

        def inner(i, c):
            @pl.when(info[slots + 1 + i] <= j)
            def _():
                q0 = pl.multiple_of(i * bq, bq)
                qrow = pl.ds(q0, bq)
                q = qkv[qrow, :HD]
                do = do_abs[qrow, :]
                s = masked(mm(k, q, 1, 1), low[:, qrow], k0, q0, valid_count)
                p = jnp.exp(s - lse[0, :, qrow])
                dp = mm(v, do, 1, 1)
                ds = (p * (dp - delta[:, qrow])).astype(BF16)
                dv[krow, :] += mm(p.astype(BF16), do)
                dk[krow, :] += mm(ds, q)
                dq[qrow, :] += mm(ds, k, 0, 0)

            return c

        return lax.fori_loop(j, n_blocks, inner, carry)

    lax.fori_loop(0, n_blocks, outer, 0)
    dcq = jnp.zeros((1, HD), F32)
    dck = jnp.zeros((1, HD), F32)
    dcv = jnp.zeros((1, HD), F32)
    half = HD // 2
    for s in range(slots):
        rows = pl.ds(pl.multiple_of(info[s] * tokens, tokens), tokens)
        co, si = cos[rows, :], sin[rows, :]
        out = slice(s * tokens, (s + 1) * tokens)

        def back(u):
            return u * co - pltpu.roll(u, half, 1) * si

        gq = back(dq[rows, :]) * HD ** (-0.5)
        gk = back(dk[rows, :])
        gv = dv[rows, :]
        q = back(qkv[rows, :HD].astype(F32)) * HD**0.5
        k = back(qkv[rows, HD : 2 * HD].astype(F32))
        v = qkv[rows, 2 * HD :].astype(F32)
        dcq += jnp.sum(gq * q, axis=0, keepdims=True)
        dck += jnp.sum(gk * k, axis=0, keepdims=True)
        dcv += jnp.sum(gv * v, axis=0, keepdims=True)
        dz[out, :HD] = (gq * scale[:, :HD]).astype(BF16)
        dz[out, HD : 2 * HD] = (gk * scale[:, HD : 2 * HD]).astype(BF16)
        dz[out, 2 * HD :] = (gv * scale[:, 2 * HD :]).astype(BF16)
    dc[:, :HD] = dcq / scale[:, :HD]
    dc[:, HD : 2 * HD] = dck / scale[:, HD : 2 * HD]
    dc[:, 2 * HD :] = dcv / scale[:, 2 * HD :]


def attn_bwd(info, qkv_abs, do_chunks, att_abs, lse, low, cos, sin, scale, tokens, bq):
    seq, width = qkv_abs.shape
    heads = width // (3 * HD)
    rows = do_chunks[0].shape[0]
    once = lambda h, f: (0, 0)
    head = lambda h, f: (0, h)
    return pl.pallas_call(
        functools.partial(attn_bwd_kernel, len(do_chunks), tokens, bq),
        grid_spec=pltpu.PrefetchScalarGridSpec(
            num_scalar_prefetch=1,
            grid=(heads,),
            in_specs=[pl.BlockSpec((seq, 3 * HD), head)]
            + [pl.BlockSpec((rows, HD), head)] * len(do_chunks)
            + [
                pl.BlockSpec((seq, HD), head),
                pl.BlockSpec((1, 1, seq), lambda h, f: (h, 0, 0)),
                pl.BlockSpec((1, seq), once),
                pl.BlockSpec((seq, HD), once),
                pl.BlockSpec((seq, HD), once),
                pl.BlockSpec((1, 3 * HD), head),
            ],
            out_specs=[
                pl.BlockSpec((seq, 3 * HD), head),
                pl.BlockSpec((1, 3 * HD), head),
            ],
            scratch_shapes=[
                pltpu.VMEM((seq, HD), BF16),
                pltpu.VMEM((1, seq), F32),
                pltpu.VMEM((seq, HD), F32),
                pltpu.VMEM((seq, HD), F32),
                pltpu.VMEM((seq, HD), F32),
            ],
        ),
        out_shape=[
            jax.ShapeDtypeStruct((seq, width), BF16),
            jax.ShapeDtypeStruct((1, width), F32),
        ],
        compiler_params=params(),
        cost_estimate=cost(
            10 * heads * seq * seq * HD, 2 * seq * width * 4, heads * seq * seq // 2
        ),
    )(info, qkv_abs, *do_chunks, att_abs, lse, low, cos, sin, scale)


def mlp_kernel(rows, *refs):
    count = len(rows)
    xs = refs[:count]
    dhid, w, scale, hid, dz, dx_own, dx_mate, dc = refs[count:]
    tokens = dx_own.shape[0]
    sum_gate = jnp.zeros(scale.shape[1:], F32)
    sum_up = jnp.zeros(scale.shape[1:], F32)
    at = 0
    for x, r in zip(xs, rows):
        part = slice(at, at + r)
        xv = x[...]
        zg = mm(xv, w[0])
        zu = mm(xv, w[1])
        gate = zg * scale[0]
        up = zu * scale[1]
        s = 1.0 / (1.0 + jnp.exp(-gate))
        act = gate * s
        hid[part, :] = (act * up).astype(BF16)
        d = dhid[part, :].astype(F32)
        dgate = d * up * s * (1.0 + gate * (1.0 - s))
        dup = d * act
        sum_gate += jnp.sum(dgate * zg, axis=0, keepdims=True)
        sum_up += jnp.sum(dup * zu, axis=0, keepdims=True)
        dzg = (dgate * scale[0]).astype(BF16)
        dzu = (dup * scale[1]).astype(BF16)
        dz[0, part, :] = dzg
        dz[1, part, :] = dzu
        dx = (mm(dzg, w[0], 1, 1) + mm(dzu, w[1], 1, 1)).astype(BF16)
        if at < tokens:
            dx_own[part, :] = dx
        else:
            dx_mate[at - tokens : at - tokens + r, :] = dx
        at += r
    dc[0] = sum_gate
    dc[1] = sum_up


def mlp_chunk(pieces, dhid, w, scale):
    rows = [p.shape[0] for p in pieces]
    total = sum(rows)
    _, depth, width = w.shape
    half = jax.ShapeDtypeStruct((total // 2, depth), BF16)
    return pl.pallas_call(
        functools.partial(mlp_kernel, rows),
        in_specs=[VM] * (len(pieces) + 3),
        out_specs=[VM] * 5,
        out_shape=[
            jax.ShapeDtypeStruct((total, width), BF16),
            jax.ShapeDtypeStruct((2, total, width), BF16),
            half,
            half,
            jax.ShapeDtypeStruct((2, 1, width), F32),
        ],
        compiler_params=params(),
        cost_estimate=cost(
            8 * total * depth * width, 4 * depth * width + 4 * total * depth, total * width
        ),
    )(*pieces, dhid, w, scale)


def rank_kernel(nx, nd, spans, *refs):
    xs = refs[:nx]
    ds = refs[nx : nx + nd]
    at, b, v, s, ga, gb = refs[nx + nd :]
    ga_sum = None
    gb_sum = None
    for xi, xa, di, da, r in spans:
        x = xs[xi][xa : xa + r, :]
        d = ds[di][da : da + r, :]
        u = mm(d, b[...], 1, 1).astype(BF16)
        t = mm(x, at[...], 1, 1).astype(BF16)
        a_part = mm(u, x, 0, 0)
        b_part = mm(t, d, 0, 0)
        ga_sum = a_part if ga_sum is None else ga_sum + a_part
        gb_sum = b_part if gb_sum is None else gb_sum + b_part
    sv = s[...]
    sb = (b[...].astype(F32) * sv).astype(BF16)
    ga[...] = FACTOR * (ga_sum - mm(sb, v[...], 1, 1))
    gb[...] = FACTOR * (gb_sum - mm(at[...], v[...]) * sv)


def rank_grads(xs, ds, at, b, v, s):
    spans = []
    xi = xa = di = da = 0
    while xi < len(xs):
        r = min(xs[xi].shape[0] - xa, ds[di].shape[0] - da)
        spans.append((xi, xa, di, da, r))
        xa += r
        da += r
        if xa == xs[xi].shape[0]:
            xi, xa = xi + 1, 0
        if da == ds[di].shape[0]:
            di, da = di + 1, 0
    total = sum(x.shape[0] for x in xs)
    rank, n_in = at.shape
    n_out = b.shape[1]
    return pl.pallas_call(
        functools.partial(rank_kernel, len(xs), len(ds), tuple(spans)),
        in_specs=[VM] * (len(xs) + len(ds) + 4),
        out_specs=[VM] * 2,
        out_shape=[
            jax.ShapeDtypeStruct((rank, n_in), F32),
            jax.ShapeDtypeStruct((rank, n_out), F32),
        ],
        compiler_params=params(),
        cost_estimate=cost(
            4 * total * (n_in + n_out) * 256, 2 * (total * (n_in + n_out) + n_in * n_out)
        ),
    )(*xs, *ds, at, b, v, s)


def norm_forward(values):
    inverse = lax.rsqrt(jnp.mean(values * values, axis=-1, keepdims=True) + EPSILON)
    return values * inverse, inverse


def norm_backward(grad_normed, unit_vals, inverse, gain):
    scaled = grad_normed * gain
    return inverse * (scaled - unit_vals * jnp.mean(scaled * unit_vals, axis=-1, keepdims=True))


def after(value, *others):
    return lax.optimization_barrier((value,) + others)[0]


def on_device(
    sizes,
    layer_input,
    cotangent,
    segment_ids,
    token_valid,
    norm_attn,
    norm_mlp,
    base_qkv,
    base_attn_out,
    base_gate_up,
    base_down,
    rank_in_attn,
    rank_out_attn,
    magnitude_qkv,
    magnitude_out,
    rank_in_mlp,
    rank_out_mlp,
    magnitude_mlp,
    rank_in_down,
    rank_out_down,
    magnitude_down,
):
    X, C, ZH, ZL, Y = (sizes[a] for a in AXES)
    ix, ic, izh, izl, iy = (lax.axis_index(a) for a in AXES)
    dp, mp = X * C, ZH * ZL * Y
    n_dev = dp * mp
    tokens, model = layer_input.shape
    seq = segment_ids.shape[0]
    width = base_qkv.shape[2]
    hidden = base_gate_up.shape[2]
    heads = width // HD
    a_w = rank_in_attn.shape[1]
    f_w = rank_in_down.shape[0]
    used = 11 * a_w + 3 * f_w
    packed_w = -(-used // 128) * 128
    bq = min(512, seq)
    stay = ic == izh

    def from_offset(a, axis, k):
        n = sizes[axis]
        return lax.ppermute(a, axis, [(s, (s - k) % n) for s in range(n)])

    def to_offset(a, axis, k):
        n = sizes[axis]
        return lax.ppermute(a, axis, [(s, (s + k) % n) for s in range(n)])

    def mate(a):
        return from_offset(a, "c", 1)

    offsets = [(dz, dy) for dz in range(ZL) for dy in range(Y)]

    def chips(a, off, sign):
        dz, dy = off
        perm = []
        for z in range(ZL):
            for y in range(Y):
                perm.append((z * Y + y, (z + sign * dz) % ZL * Y + (y + sign * dy) % Y))
        return lax.ppermute(a, ("zl", "y"), perm)

    def swap_rows(a):
        return lax.ppermute(a, ("c", "zh"), [(1, 2), (2, 1)])

    def gather_square(a):
        if ZL == 2 and Y == 2:
            half = a.shape[0] // 2
            py, pz = chips(a, (0, 1), -1), chips(a, (1, 0), -1)
            d0 = chips(pz[:half], (0, 1), -1)
            d1 = chips(py[half:], (1, 0), -1)
            lists = [[a], [py], [pz], [d0, d1]]
        else:
            lists = [[a]] + [[chips(a, o, -1)] for o in offsets[1:]]
        return [pieces + [mate(p) for p in pieces] for pieces in lists]

    def scatter_square(parts):
        total = None
        for o in list(range(len(offsets)))[::-1]:
            own, other = parts[o]
            got = mate(other)
            block = own.astype(F32) + got.astype(F32)
            if o:
                block = chips(block.astype(BF16), offsets[o], 1).astype(F32)
            total = block if total is None else total + block
        return total

    def square_sum(a):
        total = a
        for axis in ("c", "zl", "y"):
            total = sum((from_offset(total, axis, k) for k in range(1, sizes[axis])), total)
        return total

    d = np.arange(n_dev)
    d_dp, d_mp = d // mp, d % mp

    def digit(values, own, n):
        return (jnp.asarray(values, jnp.int32) - own + n) % n

    order = digit(d_dp % 2, ic, C)
    order = order * X + digit(d_dp // 2, ix, X)
    order = order * Y + digit(d_mp % Y, iy, Y)
    order = order * ZL + digit(d_mp // Y % ZL, izl, ZL)
    order = order * ZH + digit(d_mp // (Y * ZL), izh, ZH)
    shard = (ic * ZL + izl) * Y + iy
    shard_here = (izh * ZL + izl) * Y + iy
    where_ = jnp.stack([shard, shard_here]).astype(jnp.int32)
    flags = jnp.stack([stay.astype(jnp.int32), ix]).astype(jnp.int32)
    slots = []
    for dz, dy in offsets:
        for k in range(2):
            slots.append(((ic + k) % 2 * ZL + (izl + dz) % ZL) * Y + (iy + dy) % Y)
    blk = jnp.stack(slots).astype(jnp.int32)

    packed = pl.pallas_call(
        functools.partial(pack_kernel, a_w, f_w),
        in_specs=[VM] * 10,
        out_specs=VM,
        out_shape=jax.ShapeDtypeStruct((1, R + 1, packed_w), BF16),
    )(
        rank_in_attn,
        rank_out_attn,
        magnitude_qkv,
        magnitude_out[None],
        rank_in_mlp,
        rank_out_mlp,
        magnitude_mlp,
        rank_in_down,
        rank_out_down,
        magnitude_down[None],
    )

    moved_input = swap_rows(layer_input)
    gathered = packed
    for axis in ("zh", "zl", "y", "x", "c"):
        gathered = jnp.concatenate(
            [gathered] + [from_offset(gathered, axis, k) for k in range(1, sizes[axis])], axis=0
        )

    def sds(shape, dtype=BF16):
        return jax.ShapeDtypeStruct(shape, dtype)

    (
        at_qkv, at_gu, at_o, at_d, at_o0, at_d0, b_qkv, b_gu, b_o, b_d, m_qkv, m_o, m_gu, m_d,
    ) = pl.pallas_call(
        functools.partial(unpack_kernel, a_w, f_w, dp),
        in_specs=[SM, SM, VM],
        out_specs=[VM] * 14,
        out_shape=[
            sds((3 * R, model)),
            sds((2, R, model)),
            sds((R, width)),
            sds((R, hidden)),
            sds((R, width)),
            sds((R, hidden)),
            sds((3, R, width)),
            sds((2, R, hidden)),
            sds((R, model)),
            sds((R, model)),
            sds((3, 1, width), F32),
            sds((1, model), F32),
            sds((2, 1, hidden), F32),
            sds((1, model), F32),
        ],
    )(order, where_, gathered)

    def fetch(w, axis):
        part = w.shape[axis] // X
        mine = lax.dynamic_slice_in_dim(w, ix * part, part, axis)
        mine = lax.ppermute(mine, ("c", "zh"), [(0, 1), (3, 2)])
        parts = [mine]
        for k in range(1, X):
            perm = []
            for x in range(X):
                for cz in (1, 2):
                    perm.append((x * 4 + cz, (x - k) % X * 4 + cz))
            parts.append(lax.ppermute(mine, ("x", "c", "zh"), perm))
        return parts

    parts_qkv = fetch(base_qkv, 1)
    local_input = jnp.where(stay, layer_input, moved_input)
    parts_o = fetch(after(base_attn_out, local_input), 1)
    moved_cot = swap_rows(after(cotangent, local_input))
    parts_gu = fetch(after(base_gate_up, parts_qkv[-1]), 1)
    parts_d = fetch(after(base_down, parts_qkv[-1]), 1)
    local_cot = jnp.where(stay, cotangent, moved_cot)

    gain_one = norm_attn.astype(F32)
    gain_two = norm_mlp.astype(F32)
    input_full = local_input.astype(F32)
    unit_one, inverse_one = norm_forward(input_full)
    normed_one = (unit_one * gain_one).astype(BF16)
    one = gather_square(normed_one)

    seg_mate = mate(segment_ids)
    valid_mate = mate(token_valid)
    segments = jnp.where(stay, segment_ids, seg_mate)
    valid = jnp.where(stay, token_valid, valid_mate)
    steps = jnp.arange(seq, dtype=jnp.int32)
    earlier = jnp.concatenate([segments[:1] - 1, segments[:-1]])
    first = lax.cummax(jnp.where(segments != earlier, steps, 0), axis=0)
    low = first[None]
    positions = steps - first
    frequency = ROPE_BASE ** (-(2.0 * jnp.arange(HD // 2, dtype=F32)) / HD)
    angle = positions.astype(F32)[:, None] * frequency[None, :]
    cos_half, sin_half = jnp.cos(angle), jnp.sin(angle)
    cos = jnp.concatenate([cos_half, cos_half], axis=1)
    sin = jnp.concatenate([-sin_half, sin_half], axis=1)
    info = jnp.concatenate([blk, jnp.sum(valid)[None].astype(jnp.int32), first[::bq] // bq])

    v_qkv, square_qkv = merge_qkv(flags, base_qkv, parts_qkv, at_qkv, b_qkv)
    norms_qkv = jnp.sqrt(square_qkv)

    def head_major(a):
        k = a.shape[1]
        return a.reshape(3, k, heads, HD).transpose(1, 2, 0, 3).reshape(k, 3 * width)

    mags_qkv = head_major(m_qkv)
    scale_qkv = mags_qkv / norms_qkv

    def rows_square(base, at0, b):
        v = base.astype(F32) + FACTOR * mm(at0, b, 0, 0)
        return jnp.sum(v * v, axis=0)

    squares = jnp.stack(
        [rows_square(base_attn_out, at_o0, b_o), rows_square(base_down, at_d0, b_d)]
    )
    for axis in ("zh", "zl", "y"):
        squares = sum((from_offset(squares, axis, k) for k in range(1, sizes[axis])), squares)
    norms_rows = jnp.sqrt(squares)
    norms_o, norms_d = norms_rows[0:1], norms_rows[1:2]
    scale_o = m_o / norms_o
    scale_d = m_d / norms_d

    qkv = [
        qkv_chunk(blk, o, one[o], v_qkv, scale_qkv, cos, sin) for o in range(len(offsets))
    ]
    qkv_abs, att_abs, att_slot, lse = attn_fwd(info, qkv, low, tokens, bq)
    v_o = merge_rows(flags, base_attn_out, parts_o, at_o, b_o)

    def slot(a, o, k):
        at = (2 * o + k) * tokens
        return lax.slice_in_dim(a, at, at + tokens, axis=0)

    parts = [
        tuple(mm(slot(att_slot, o, k), v_o).astype(BF16) for k in range(2))
        for o in range(len(offsets))
    ]
    summed_out = scatter_square(parts)
    residual = input_full + summed_out * scale_o
    unit_two, inverse_two = norm_forward(residual)
    normed_two = (unit_two * gain_two).astype(BF16)
    two = gather_square(normed_two)

    v_gu, square_gu = merge_gu(flags, base_gate_up, parts_gu, at_gu, b_gu)
    norms_gu = jnp.sqrt(square_gu)
    scale_gu = m_gu / norms_gu
    v_d = merge_rows(flags, base_down, parts_d, at_d, b_d)
    grad_output = local_cot.astype(F32)
    low_down = (grad_output * scale_d).astype(BF16)
    down = gather_square(after(low_down, qkv[-1]))
    hid, dz_gu, parts, dc_gu = [], [], [], 0.0
    for o in range(len(offsets)):
        dhid = jnp.concatenate([mm(p, v_d, 1, 1) for p in down[o]], axis=0)
        h, dz, own, other, dc = mlp_chunk(two[o], dhid, v_gu, scale_gu)
        hid.append(h)
        dz_gu.append(dz)
        parts.append((own, other))
        dc_gu = dc_gu + dc
    grad_normed_two = scatter_square(parts)
    grad_residual = grad_output + norm_backward(grad_normed_two, unit_two, inverse_two, gain_two)
    low_out = (grad_residual * scale_o).astype(BF16)
    out = gather_square(low_out)

    do_chunks = [
        jnp.concatenate([mm(p, v_o, 1, 1).astype(BF16) for p in out[o]], axis=0)
        for o in range(len(offsets))
    ]
    dz_qkv, dc_qkv = attn_bwd(
        info, qkv_abs, do_chunks, att_abs, lse, low, cos, sin, scale_qkv, tokens, bq
    )

    parts = [
        tuple(
            mm(lax.slice_in_dim(h, k * tokens, (k + 1) * tokens, axis=0), v_d).astype(BF16)
            for k in range(2)
        )
        for h in [after(h, low_out) for h in hid]
    ]
    summed_down = scatter_square(parts)
    output_here = (residual + summed_down * scale_d).astype(BF16)
    layer_output = jnp.where(stay, output_here, swap_rows(output_here))

    col_own = jnp.stack(
        [
            jnp.sum(grad_residual * summed_out, axis=0),
            jnp.sum(grad_output * summed_down, axis=0),
        ]
    )
    col_row = square_sum(col_own)

    parts = [
        tuple(mm(slot(dz_qkv, o, k), v_qkv, 1, 1).astype(BF16) for k in range(2))
        for o in range(len(offsets))
    ]
    grad_normed_one = scatter_square(parts)
    grad_here = grad_residual + norm_backward(grad_normed_one, unit_one, inverse_one, gain_one)
    input_grad = jnp.where(stay, grad_here, swap_rows(grad_here.astype(BF16)).astype(F32))

    def flat(lists):
        return [p for pieces in lists for p in pieces]

    def shrink(col, mags, norms):
        return col * mags / (norms * norms * norms)

    ga_gu, gb_gu = [], []
    s_gu = shrink(dc_gu, m_gu, norms_gu)
    for p in range(2):
        ga, gb = rank_grads(
            flat(two), [dz[p] for dz in dz_gu], at_gu[p], b_gu[p], v_gu[p], s_gu[p]
        )
        ga_gu.append(ga)
        gb_gu.append(gb)
    ga_o, gb_o = rank_grads(
        [att_slot], flat(out), at_o, b_o, v_o, shrink(col_row[0:1], m_o, norms_o)
    )
    ga_d, gb_d = rank_grads(
        hid, flat(down), at_d, b_d, v_d, shrink(col_row[1:2], m_d, norms_d)
    )
    b_blocks = jnp.concatenate(
        [
            head_major(jnp.stack([b_qkv[q] if q == p else jnp.zeros_like(b_qkv[q]) for q in range(3)]))
            for p in range(3)
        ],
        axis=0,
    )
    ga_qkv, gb_all = rank_grads(
        flat(one), [dz_qkv], at_qkv, b_blocks, v_qkv, shrink(dc_qkv, mags_qkv, norms_qkv)
    )
    gb_qkv = jnp.stack(
        [
            gb_all[p * R : (p + 1) * R].reshape(R, heads, 3, HD)[:, :, p].reshape(R, width)
            for p in range(3)
        ]
    )
    mag_qkv = (dc_qkv / norms_qkv).reshape(heads, 3, HD).transpose(1, 0, 2).reshape(3, 1, width)
    mag_full = jnp.concatenate([col_own[0:1] / norms_o, col_own[1:2] / norms_d], axis=0)

    grads = pl.pallas_call(
        functools.partial(pack_grads_kernel, a_w, f_w, dp),
        in_specs=[SM, SM] + [VM] * 9,
        out_specs=VM,
        out_shape=jax.ShapeDtypeStruct((n_dev, R + 1, packed_w), F32),
    )(
        order,
        where_,
        jnp.concatenate([ga_qkv] + ga_gu, axis=0),
        jnp.concatenate([gb_o, gb_d], axis=0),
        mag_full,
        ga_o,
        ga_d,
        gb_qkv,
        jnp.stack(gb_gu),
        mag_qkv,
        dc_gu / norms_gu,
    )
    for axis in ("c", "x", "y", "zl", "zh"):
        m = grads.shape[0] // sizes[axis]
        grads = sum(
            (to_offset(grads[k * m : (k + 1) * m], axis, k) for k in range(1, sizes[axis])),
            grads[:m],
        )
    g = grads[0]
    gm = g[R]
    g = g[:R]

    def cols(start, count, w):
        return g[:, start : start + count * w].reshape(R, count, w)

    grad_in_attn = cols(0, 4, a_w).transpose(1, 2, 0)
    grad_in_mlp = cols(4 * a_w, 2, a_w).transpose(1, 2, 0)
    grad_in_down = g[:, 6 * a_w : 6 * a_w + f_w].T
    b_at = 6 * a_w + f_w
    grad_out_attn = cols(b_at, 4, a_w).transpose(1, 0, 2)
    grad_out_mlp = cols(b_at + 4 * a_w, 2, f_w).transpose(1, 0, 2)
    grad_out_down = g[:, b_at + 4 * a_w + 2 * f_w : used]
    grad_mag_qkv = gm[: 3 * a_w].reshape(3, a_w)
    grad_mag_out = gm[3 * a_w : 4 * a_w]
    grad_mag_mlp = gm[4 * a_w : 4 * a_w + 2 * f_w].reshape(2, f_w)
    grad_mag_down = gm[4 * a_w + 2 * f_w : 5 * a_w + 2 * f_w]
    return (
        layer_output,
        input_grad,
        grad_in_attn,
        grad_out_attn,
        grad_mag_qkv,
        grad_mag_out,
        grad_in_mlp,
        grad_out_mlp,
        grad_mag_mlp,
        grad_in_down,
        grad_out_down,
        grad_mag_down,
    )


def solution(mesh):
    dp, mp = mesh.shape["dp"], mesh.shape["mp"]
    shape = (dp // 2, 2, 2, 2, mp // 4)
    fine = Mesh(mesh.devices.reshape(shape), AXES)
    rows, cols = ("x", "c"), ("zh", "zl", "y")
    both = rows + cols
    return jax.shard_map(
        functools.partial(on_device, dict(zip(AXES, shape))),
        mesh=fine,
        in_specs=(
            P(both, None),
            P(both, None),
            P(rows),
            P(rows),
            P(),
            P(),
            P(None, None, cols),
            P(cols, None),
            P(None, None, cols),
            P(cols, None),
            P(None, both, None),
            P(None, None, both),
            P(None, both),
            P(both),
            P(None, both, None),
            P(None, None, both),
            P(None, both),
            P(both, None),
            P(None, both),
            P(both),
        ),
        out_specs=(
            P(both, None),
            P(both, None),
            P(None, both, None),
            P(None, None, both),
            P(None, both),
            P(both),
            P(None, both, None),
            P(None, None, both),
            P(None, both),
            P(both, None),
            P(None, both),
            P(both),
        ),
        check_vma=False,
    )
```

```python
import functools

import jax
import jax.numpy as jnp
import numpy as np
from jax import lax
from jax.experimental import pallas as pl
from jax.experimental.pallas import tpu as pltpu
from jax.sharding import Mesh
from jax.sharding import PartitionSpec as P

HD = 128
R = 16
ALPHA = 32
FACTOR = ALPHA / R
EPSILON = 1e-05
ROPE_BASE = 10000.0
BF16 = jnp.bfloat16
F32 = jnp.float32
NEG = -1e30
AXES = ("x", "c", "zh", "zl", "y")
VM = pl.BlockSpec(memory_space=pltpu.VMEM)
SM = pl.BlockSpec(memory_space=pltpu.SMEM)


def mm(left, right, lc=1, rc=0, precision=None):
    return lax.dot_general(
        left,
        right,
        (((lc,), (rc,)), ((), ())),
        preferred_element_type=F32,
        precision=precision,
    )


def params(mib=58):
    return pltpu.CompilerParams(vmem_limit_bytes=mib * 1024 * 1024)


def cost(flops, nbytes, trans=0):
    scale = 1000
    return pl.CostEstimate(
        flops=int(flops) // scale,
        bytes_accessed=int(nbytes) // scale,
        transcendentals=int(trans) // scale,
    )


class Shift:
    def __init__(self, ref, at):
        self.ref, self.at = ref, at

    def __getitem__(self, i):
        return self.ref[self.at + i]


def pack_kernel(a_w, f_w, a1, b1, mq, mo, a2, b2, mm_, a3, b3, md, out):
    out[...] = jnp.zeros(out.shape, out.dtype)
    at = 0
    for ref, count, w in ((a1, 4, a_w), (a2, 2, a_w), (a3, 1, f_w), (b1, 4, a_w), (b2, 2, f_w), (b3, 1, a_w)):
        for p in range(count):
            out[0, :R, at : at + w] = ref[p].astype(BF16)
            at += w
    at = 0
    for ref, count, w in ((mq, 3, a_w), (mo, 1, a_w), (mm_, 2, f_w), (md, 1, a_w)):
        for p in range(count):
            out[0, R : R + 1, at : at + w] = ref[p : p + 1, :].astype(BF16)
            at += w


def unpack_grads_kernel(a_w, f_w, g, a1, b1, mq, mo, a2, b2, mm_, a3, b3, md):
    at = 0
    for ref, count, w in ((a1, 4, a_w), (a2, 2, a_w), (a3, 1, f_w), (b1, 4, a_w), (b2, 2, f_w), (b3, 1, a_w)):
        for p in range(count):
            ref[p] = g[0, :R, at : at + w]
            at += w
    at = 0
    for ref, count, w in ((mq, 3, a_w), (mo, 1, a_w), (mm_, 2, f_w), (md, 1, a_w)):
        for p in range(count):
            ref[p : p + 1, :] = g[0, R : R + 1, at : at + w]
            at += w


def unpack_kernel(
    a_w, f_w, dp, table, g, at_qkv, at_gu, at_o, at_d, at_o0, at_d0,
    b_qkv, b_blocks, b_gu, b_o, b_d, m_qkv, m_o, m_gu, m_d,
):
    b_blocks[...] = jnp.zeros(b_blocks.shape, b_blocks.dtype)
    n = g.shape[0]
    order, where_ = Shift(table, 0), Shift(table, n)
    b_at = 6 * a_w + f_w
    for d in range(n):
        s = order[d]
        lo, hi = d * a_w, (d + 1) * a_w
        for p in range(3):
            at_qkv[p * R : (p + 1) * R, lo:hi] = g[s, :R, p * a_w : (p + 1) * a_w]
        for p in range(2):
            at_gu[p, :, lo:hi] = g[s, :R, (4 + p) * a_w : (5 + p) * a_w]
        b_o[:, lo:hi] = g[s, :R, b_at + 3 * a_w : b_at + 4 * a_w]
        end = b_at + 4 * a_w + 2 * f_w
        b_d[:, lo:hi] = g[s, :R, end : end + a_w]
        m_o[:, lo:hi] = g[s, R : R + 1, 3 * a_w : 4 * a_w].astype(F32)
        end = 4 * a_w + 2 * f_w
        m_d[:, lo:hi] = g[s, R : R + 1, end : end + a_w].astype(F32)
    for i in range(dp):
        s = order[where_[0] * dp + i]
        lo, hi = i * a_w, (i + 1) * a_w
        flo, fhi = i * f_w, (i + 1) * f_w
        at_o[:, lo:hi] = g[s, :R, 3 * a_w : 4 * a_w]
        at_d[:, flo:fhi] = g[s, :R, 6 * a_w : 6 * a_w + f_w]
        for p in range(3):
            b_qkv[p, :, lo:hi] = g[s, :R, b_at + p * a_w : b_at + (p + 1) * a_w]
            for h, at in pieces_of(lo, hi):
                head, inner = divmod(h, HD)
                to = (head * 3 + p) * HD + inner
                w = at[1] - at[0]
                src = p * a_w + at[0]
                b_blocks[p * R : (p + 1) * R, to : to + w] = g[s, :R, b_at + src : b_at + src + w]
                m_qkv[:, to : to + w] = g[s, R : R + 1, src : src + w].astype(F32)
        for p in range(2):
            e = b_at + 4 * a_w + p * f_w
            b_gu[p, :, flo:fhi] = g[s, :R, e : e + f_w]
            e = 4 * a_w + p * f_w
            m_gu[p, :, flo:fhi] = g[s, R : R + 1, e : e + f_w].astype(F32)
        s = order[where_[1] * dp + i]
        at_o0[:, lo:hi] = g[s, :R, 3 * a_w : 4 * a_w]
        at_d0[:, flo:fhi] = g[s, :R, 6 * a_w : 6 * a_w + f_w]


def pieces_of(lo, hi):
    found = []
    at = lo
    while at < hi:
        end = min(hi, (at // HD + 1) * HD)
        found.append((at, (at - lo, end - lo)))
        at = end
    return found


def pack_grads_kernel(
    a_w, f_w, dp, table, ga_qkv, ga_gu, gb_o, gb_d, m_full, ga_attn, ga_d, gb_all, gb_gu,
    m_qkv, m_gu, out
):
    n = out.shape[0]
    order, where_ = Shift(table, 0), Shift(table, n)
    heads = m_qkv.shape[1] // (3 * HD)
    out[...] = jnp.zeros(out.shape, out.dtype)
    b_at = 6 * a_w + f_w
    dt = out.dtype
    for d in range(n):
        s = order[d]
        lo, hi = d * a_w, (d + 1) * a_w
        for p in range(3):
            out[s, :R, p * a_w : (p + 1) * a_w] = ga_qkv[p * R : (p + 1) * R, lo:hi].astype(dt)
        for p in range(2):
            e = (4 + p) * a_w
            out[s, :R, e : e + a_w] = ga_gu[p * R : (p + 1) * R, lo:hi].astype(dt)
        out[s, :R, b_at + 3 * a_w : b_at + 4 * a_w] = gb_o[:, lo:hi].astype(dt)
        end = b_at + 4 * a_w + 2 * f_w
        out[s, :R, end : end + a_w] = gb_d[:, lo:hi].astype(dt)
        out[s, R : R + 1, 3 * a_w : 4 * a_w] = m_full[0:1, lo:hi].astype(dt)
        end = 4 * a_w + 2 * f_w
        out[s, R : R + 1, end : end + a_w] = m_full[1:2, lo:hi].astype(dt)
    for i in range(dp):
        s = order[where_[0] * dp + i]
        lo, hi = i * a_w, (i + 1) * a_w
        flo, fhi = i * f_w, (i + 1) * f_w
        out[s, :R, 3 * a_w : 4 * a_w] = ga_attn[:, lo:hi].astype(dt)
        out[s, :R, 6 * a_w : 6 * a_w + f_w] = ga_d[:, flo:fhi].astype(dt)
        for p in range(3):
            for h, at in pieces_of(lo, hi):
                head, inner = divmod(h, HD)
                src = (head * 3 + p) * HD + inner
                w = at[1] - at[0]
                to = p * a_w + at[0]
                out[s, :R, b_at + to : b_at + to + w] = gb_all[p * R : (p + 1) * R, src : src + w].astype(dt)
                out[s, R : R + 1, to : to + w] = m_qkv[:, src : src + w].astype(dt)
        for p in range(2):
            e = b_at + 4 * a_w + p * f_w
            out[s, :R, e : e + f_w] = gb_gu[p * R : (p + 1) * R, flo:fhi].astype(dt)
            e = 4 * a_w + p * f_w
            out[s, R : R + 1, e : e + f_w] = m_gu[p, :, flo:fhi].astype(dt)


def pick(flags, t, own, parts):
    n = len(parts)
    k = lax.rem(t - flags[1] + n, n)
    w = parts[0]
    for i in range(1, n):
        w = jnp.where(k == i, parts[i], w)
    return jnp.where(flags[0] == 1, own, w)


def own_block(t, f):
    return t * f[0]


def merge_qkv_kernel(n, flags, own, *refs):
    parts = refs[:n]
    at, b, vb, ssq = refs[n:]
    t = pl.program_id(0)

    @pl.when(t == 0)
    def _():
        ssq[...] = jnp.zeros_like(ssq)

    members, _, width = own.shape
    for p in range(members):
        w = pick(flags, t, own[p], [r[p] for r in parts])
        v = w.astype(F32) + FACTOR * mm(at[p * R : (p + 1) * R, :], b[p], 0, 0)
        total = jnp.sum(v * v, axis=0, keepdims=True)
        vb16 = v.astype(BF16)
        for h in range(width // HD):
            to = slice((h * members + p) * HD, (h * members + p + 1) * HD)
            vb[:, to] = vb16[:, h * HD : (h + 1) * HD]
            ssq[:, to] += total[:, h * HD : (h + 1) * HD]


def merge_qkv(flags, own, parts, at_qkv, b_qkv):
    members, rows, width = own.shape
    n = len(parts)
    part_rows = rows // n
    block = (members, part_rows, width)
    return pl.pallas_call(
        functools.partial(merge_qkv_kernel, n),
        grid_spec=pltpu.PrefetchScalarGridSpec(
            num_scalar_prefetch=1,
            grid=(n,),
            in_specs=[pl.BlockSpec(block, lambda t, f: (0, own_block(t, f), 0))]
            + [pl.BlockSpec(block, lambda t, f: (0, 0, 0))] * n
            + [
                pl.BlockSpec((members * R, part_rows), lambda t, f: (0, t)),
                pl.BlockSpec((members, R, width), lambda t, f: (0, 0, 0)),
            ],
            out_specs=[
                pl.BlockSpec((part_rows, members * width), lambda t, f: (t, 0)),
                pl.BlockSpec((1, members * width), lambda t, f: (0, 0)),
            ],
        ),
        out_shape=[
            jax.ShapeDtypeStruct((rows, members * width), BF16),
            jax.ShapeDtypeStruct((1, members * width), F32),
        ],
        compiler_params=params(),
        cost_estimate=cost(2 * rows * width * members * 256, 4 * members * rows * width * 2),
    )(flags, own, *parts, at_qkv, b_qkv)


def merge_gu_kernel(n, flags, own, *refs):
    gates, ups = refs[:n], refs[n : 2 * n]
    at, b, vb, ssq, acc = refs[2 * n :]
    t = pl.program_id(1)
    first = pl.program_id(0) == 0
    w = pick(flags, t, own[0], [jnp.where(first, g[0], u[0]) for g, u in zip(gates, ups)])
    v = w.astype(F32) + FACTOR * mm(b[0], at[0], 0, 0)
    vb[0] = v.astype(BF16)
    sq = v * v
    lanes = sq[:, :HD]
    for i in range(1, sq.shape[1] // HD):
        lanes = lanes + sq[:, i * HD : (i + 1) * HD]

    @pl.when(t == 0)
    def _():
        acc[...] = lanes

    @pl.when(t > 0)
    def _():
        acc[...] += lanes

    @pl.when(t == pl.num_programs(1) - 1)
    def _():
        ssq[0] = mm(jnp.ones((8, HD), F32), acc[...], 1, 1, lax.Precision.HIGHEST)[:1]


def merge_gu(flags, own, gates, ups, at_gu, b_gu):
    members, width, rows = own.shape
    n = len(gates)
    part_rows = rows // n
    block = (1, width, part_rows)
    return pl.pallas_call(
        functools.partial(merge_gu_kernel, n),
        grid_spec=pltpu.PrefetchScalarGridSpec(
            num_scalar_prefetch=1,
            grid=(members, n),
            in_specs=[pl.BlockSpec(block, lambda p, t, f: (p * f[0], 0, own_block(t, f)))]
            + [pl.BlockSpec(block, lambda p, t, f: (0, 0, 0))] * (2 * n)
            + [
                pl.BlockSpec((1, R, part_rows), lambda p, t, f: (p, 0, t)),
                pl.BlockSpec((1, R, width), lambda p, t, f: (p, 0, 0)),
            ],
            out_specs=[
                pl.BlockSpec(block, lambda p, t, f: (p, 0, t)),
                pl.BlockSpec((1, 1, width), lambda p, t, f: (p, 0, 0)),
            ],
            scratch_shapes=[pltpu.VMEM((width, HD), F32)],
        ),
        out_shape=[
            jax.ShapeDtypeStruct((members, width, rows), BF16),
            jax.ShapeDtypeStruct((members, 1, width), F32),
        ],
        compiler_params=params(),
        cost_estimate=cost(2 * rows * width * members * 256, 4 * members * rows * width * 2),
    )(flags, own, *gates, *ups, at_gu, b_gu)


def merge_rows_kernel(n, flags, own, *refs):
    parts = refs[:n]
    at, b, vb = refs[n:]
    w = pick(flags, pl.program_id(0), own[...], [r[...] for r in parts])
    v = w.astype(F32) + FACTOR * mm(at[...], b[...], 0, 0)
    vb[...] = v.astype(BF16)


def merge_rows(flags, own, parts, at, b):
    rows, width = own.shape
    xs = len(parts)
    part = width // xs
    return pl.pallas_call(
        functools.partial(merge_rows_kernel, xs),
        grid_spec=pltpu.PrefetchScalarGridSpec(
            num_scalar_prefetch=1,
            grid=(xs,),
            in_specs=[pl.BlockSpec((rows, part), lambda t, f: (0, own_block(t, f)))]
            + [pl.BlockSpec((rows, part), lambda t, f: (0, 0))] * xs
            + [
                pl.BlockSpec((R, rows), lambda t, f: (0, 0)),
                pl.BlockSpec((R, part), lambda t, f: (0, t)),
            ],
            out_specs=pl.BlockSpec((rows, part), lambda t, f: (0, t)),
        ),
        out_shape=jax.ShapeDtypeStruct((rows, width), BF16),
        compiler_params=params(),
        cost_estimate=cost(2 * rows * width * 256, 4 * rows * width * 2),
    )(flags, own, *parts, at, b)


def merge_down_kernel(n, flags, own, *refs):
    parts = refs[:n]
    at, b, scale, vb, vs = refs[n:]
    w = pick(flags, pl.program_id(0), own[...], [r[...] for r in parts])
    v = (w.astype(F32) + FACTOR * mm(at[...], b[...], 0, 0)).astype(BF16)
    vb[...] = v
    vs[...] = (v.astype(F32) * scale[...]).astype(BF16)


def merge_down(flags, own, parts, at, b, scale):
    rows, width = own.shape
    n = len(parts)
    part = width // n
    return pl.pallas_call(
        functools.partial(merge_down_kernel, n),
        grid_spec=pltpu.PrefetchScalarGridSpec(
            num_scalar_prefetch=1,
            grid=(n,),
            in_specs=[pl.BlockSpec((rows, part), lambda t, f: (0, own_block(t, f)))]
            + [pl.BlockSpec((rows, part), lambda t, f: (0, 0))] * n
            + [
                pl.BlockSpec((R, rows), lambda t, f: (0, 0)),
                pl.BlockSpec((R, part), lambda t, f: (0, t)),
                pl.BlockSpec((1, part), lambda t, f: (0, t)),
            ],
            out_specs=[pl.BlockSpec((rows, part), lambda t, f: (0, t))] * 2,
        ),
        out_shape=[jax.ShapeDtypeStruct((rows, width), BF16)] * 2,
        compiler_params=params(),
        cost_estimate=cost(2 * rows * width * 256, 5 * rows * width * 2),
    )(flags, own, *parts, at, b, scale)


def qkv_kernel(rows, blk, *refs):
    count = len(rows)
    xs = refs[:count]
    w, scale, cos0, cos1, sin0, sin1, out = refs[count:]
    cos = jnp.concatenate([cos0[...], cos1[...]], axis=0)
    sin = jnp.concatenate([sin0[...], sin1[...]], axis=0)
    at = 0
    for x, r in zip(xs, rows):
        z = mm(x[...], w[...]) * scale[...]
        co, si = cos[at : at + r], sin[at : at + r]
        q = z[:, :HD]
        k = z[:, HD : 2 * HD]
        q = (q * co + pltpu.roll(q, HD // 2, 1) * si) * HD ** (-0.5)
        k = k * co + pltpu.roll(k, HD // 2, 1) * si
        out[at : at + r, :HD] = q.astype(BF16)
        out[at : at + r, HD : 2 * HD] = k.astype(BF16)
        out[at : at + r, 2 * HD :] = z[:, 2 * HD :].astype(BF16)
        at += r


def qkv_chunk(blk, chunk, pieces, w, scale, cos, sin):
    rows = [p.shape[0] for p in pieces]
    total = sum(rows)
    tokens = total // 2
    depth, width = w.shape
    heads = width // (3 * HD)

    def table(k):
        return pl.BlockSpec((tokens, HD), lambda h, b: (b[2 * chunk + k], 0))

    return pl.pallas_call(
        functools.partial(qkv_kernel, rows),
        grid_spec=pltpu.PrefetchScalarGridSpec(
            num_scalar_prefetch=1,
            grid=(heads,),
            in_specs=[pl.BlockSpec((r, depth), lambda h, b: (0, 0)) for r in rows]
            + [
                pl.BlockSpec((depth, 3 * HD), lambda h, b: (0, h)),
                pl.BlockSpec((1, 3 * HD), lambda h, b: (0, h)),
                table(0),
                table(1),
                table(0),
                table(1),
            ],
            out_specs=pl.BlockSpec((total, 3 * HD), lambda h, b: (0, h)),
        ),
        out_shape=jax.ShapeDtypeStruct((total, width), BF16),
        compiler_params=params(),
        cost_estimate=cost(2 * total * depth * width, 2 * (depth * width + total * depth)),
    )(blk, *pieces, w, scale, cos, cos, sin, sin)


def masked(scores, low, first_key, first_query, valid_count):
    keys = first_key + lax.broadcasted_iota(jnp.int32, scores.shape, 0)
    queries = first_query + lax.broadcasted_iota(jnp.int32, (1, scores.shape[1]), 1)
    high = jnp.minimum(queries, valid_count - 1)
    allowed = ((keys >= low) & (keys <= high)) | (keys == queries)
    return jnp.where(allowed, scores, NEG)


def attn_fwd_kernel(n_chunks, tokens, bq, info, *refs):
    chunks = refs[:n_chunks]
    low, qkv_abs, att_abs, att_slot, lse, m_sc, l_sc, acc = refs[n_chunks:]
    i = pl.program_id(1)
    last = pl.num_programs(1) - 1
    slots = 2 * n_chunks
    valid_count = info[slots]

    @pl.when(i == 0)
    def _():
        for s in range(slots):
            start = pl.multiple_of(info[s] * tokens, tokens)
            qkv_abs[pl.ds(start, tokens), :] = chunks[s // 2][
                (s % 2) * tokens : (s % 2 + 1) * tokens, :
            ]

    q0 = pl.multiple_of(i * bq, bq)
    q = qkv_abs[pl.ds(q0, bq), :HD]
    lo = low[:, pl.ds(q0, bq)]
    m_sc[...] = jnp.full(m_sc.shape, NEG, F32)
    l_sc[...] = jnp.zeros_like(l_sc)
    acc[...] = jnp.zeros_like(acc)

    def step(j, carry):
        k0 = pl.multiple_of(j * bq, bq)
        k = qkv_abs[pl.ds(k0, bq), HD : 2 * HD]
        v = qkv_abs[pl.ds(k0, bq), 2 * HD :]
        s = masked(mm(k, q, 1, 1), lo, k0, q0, valid_count)
        m_old = m_sc[...]
        m_new = jnp.maximum(m_old, jnp.max(s, axis=0, keepdims=True))
        p = jnp.exp(s - m_new)
        alpha = jnp.exp(m_old - m_new)
        m_sc[...] = m_new
        l_sc[...] = l_sc[...] * alpha + jnp.sum(p, axis=0, keepdims=True)
        acc[...] = acc[...] * alpha + mm(v, p.astype(BF16), 0, 0)
        return carry

    lax.fori_loop(info[slots + 1 + i], i + 1, step, 0)
    total = l_sc[...]
    lse[0, :, pl.ds(q0, bq)] = m_sc[...] + jnp.log(total)
    att_abs[pl.ds(q0, bq), :] = (acc[...] / total).T.astype(BF16)

    @pl.when(i == last)
    def _():
        for s in range(slots):
            start = pl.multiple_of(info[s] * tokens, tokens)
            att_slot[s * tokens : (s + 1) * tokens, :] = att_abs[pl.ds(start, tokens), :]


def attn_fwd(info, chunks, low, tokens, bq):
    rows, width = chunks[0].shape
    heads = width // (3 * HD)
    seq = rows * len(chunks)
    n_blocks = seq // bq
    whole = pl.BlockSpec((seq, HD), lambda h, i, f: (0, h))
    return pl.pallas_call(
        functools.partial(attn_fwd_kernel, len(chunks), tokens, bq),
        grid_spec=pltpu.PrefetchScalarGridSpec(
            num_scalar_prefetch=1,
            grid=(heads, n_blocks),
            in_specs=[pl.BlockSpec((rows, 3 * HD), lambda h, i, f: (0, h))] * len(chunks)
            + [pl.BlockSpec((1, seq), lambda h, i, f: (0, 0))],
            out_specs=[
                pl.BlockSpec((seq, 3 * HD), lambda h, i, f: (0, h)),
                whole,
                whole,
                pl.BlockSpec((1, 1, seq), lambda h, i, f: (h, 0, 0)),
            ],
            scratch_shapes=[
                pltpu.VMEM((1, bq), F32),
                pltpu.VMEM((1, bq), F32),
                pltpu.VMEM((HD, bq), F32),
            ],
        ),
        out_shape=[
            jax.ShapeDtypeStruct((seq, width), BF16),
            jax.ShapeDtypeStruct((seq, heads * HD), BF16),
            jax.ShapeDtypeStruct((seq, heads * HD), BF16),
            jax.ShapeDtypeStruct((heads, 1, seq), F32),
        ],
        compiler_params=params(),
        cost_estimate=cost(
            4 * heads * seq * seq * HD, 2 * seq * width * 3, heads * seq * seq // 2
        ),
    )(info, *chunks, low)


def attn_bwd_kernel(
    n_chunks, tokens, bq, info, qkv, *refs
):
    dos = refs[:n_chunks]
    att, lse, low, cos, sin, scale, dz, dc, do_abs, delta, dq, dk, dv = refs[n_chunks:]
    slots = 2 * n_chunks
    valid_count = info[slots]
    seq = qkv.shape[0]
    n_blocks = seq // bq
    for s in range(slots):
        start = pl.multiple_of(info[s] * tokens, tokens)
        do_abs[pl.ds(start, tokens), :] = dos[s // 2][(s % 2) * tokens : (s % 2 + 1) * tokens, :]
    ones = jnp.ones((8, HD), F32)
    for i in range(n_blocks):
        r = slice(i * bq, (i + 1) * bq)
        prod = do_abs[r, :].astype(F32) * att[r, :].astype(F32)
        delta[:, r] = mm(ones, prod, 1, 1, lax.Precision.HIGHEST)[:1]
    dq[...] = jnp.zeros_like(dq)

    def outer(j, carry):
        k0 = pl.multiple_of(j * bq, bq)
        k = qkv[pl.ds(k0, bq), HD : 2 * HD]
        v = qkv[pl.ds(k0, bq), 2 * HD :]
        krow = pl.ds(k0, bq)
        dk[krow, :] = jnp.zeros((bq, HD), F32)
        dv[krow, :] = jnp.zeros((bq, HD), F32)

        def inner(i, c):
            @pl.when(info[slots + 1 + i] <= j)
            def _():
                q0 = pl.multiple_of(i * bq, bq)
                qrow = pl.ds(q0, bq)
                q = qkv[qrow, :HD]
                do = do_abs[qrow, :]
                s = masked(mm(k, q, 1, 1), low[:, qrow], k0, q0, valid_count)
                p = jnp.exp(s - lse[0, :, qrow])
                dp = mm(v, do, 1, 1)
                ds = (p * (dp - delta[:, qrow])).astype(BF16)
                dv[krow, :] += mm(p.astype(BF16), do)
                dk[krow, :] += mm(ds, q)
                dq[qrow, :] += mm(ds, k, 0, 0)

            return c

        return lax.fori_loop(j, n_blocks, inner, carry)

    lax.fori_loop(0, n_blocks, outer, 0)
    dcq = jnp.zeros((1, HD), F32)
    dck = jnp.zeros((1, HD), F32)
    dcv = jnp.zeros((1, HD), F32)
    half = HD // 2
    for s in range(slots):
        rows = pl.ds(pl.multiple_of(info[s] * tokens, tokens), tokens)
        co, si = cos[rows, :], sin[rows, :]
        out = slice(s * tokens, (s + 1) * tokens)

        def back(u):
            return u * co - pltpu.roll(u, half, 1) * si

        gq = back(dq[rows, :]) * HD ** (-0.5)
        gk = back(dk[rows, :])
        gv = dv[rows, :]
        q = back(qkv[rows, :HD].astype(F32)) * HD**0.5
        k = back(qkv[rows, HD : 2 * HD].astype(F32))
        v = qkv[rows, 2 * HD :].astype(F32)
        dcq += jnp.sum(gq * q, axis=0, keepdims=True)
        dck += jnp.sum(gk * k, axis=0, keepdims=True)
        dcv += jnp.sum(gv * v, axis=0, keepdims=True)
        dz[out, :HD] = (gq * scale[:, :HD]).astype(BF16)
        dz[out, HD : 2 * HD] = (gk * scale[:, HD : 2 * HD]).astype(BF16)
        dz[out, 2 * HD :] = (gv * scale[:, 2 * HD :]).astype(BF16)
    dc[:, :HD] = dcq / scale[:, :HD]
    dc[:, HD : 2 * HD] = dck / scale[:, HD : 2 * HD]
    dc[:, 2 * HD :] = dcv / scale[:, 2 * HD :]


def attn_bwd(info, qkv_abs, do_chunks, att_abs, lse, low, cos, sin, scale, tokens, bq):
    seq, width = qkv_abs.shape
    heads = width // (3 * HD)
    rows = do_chunks[0].shape[0]
    once = lambda h, f: (0, 0)
    head = lambda h, f: (0, h)
    return pl.pallas_call(
        functools.partial(attn_bwd_kernel, len(do_chunks), tokens, bq),
        grid_spec=pltpu.PrefetchScalarGridSpec(
            num_scalar_prefetch=1,
            grid=(heads,),
            in_specs=[pl.BlockSpec((seq, 3 * HD), head)]
            + [pl.BlockSpec((rows, HD), head)] * len(do_chunks)
            + [
                pl.BlockSpec((seq, HD), head),
                pl.BlockSpec((1, 1, seq), lambda h, f: (h, 0, 0)),
                pl.BlockSpec((1, seq), once),
                pl.BlockSpec((seq, HD), once),
                pl.BlockSpec((seq, HD), once),
                pl.BlockSpec((1, 3 * HD), head),
            ],
            out_specs=[
                pl.BlockSpec((seq, 3 * HD), head),
                pl.BlockSpec((1, 3 * HD), head),
            ],
            scratch_shapes=[
                pltpu.VMEM((seq, HD), BF16),
                pltpu.VMEM((1, seq), F32),
                pltpu.VMEM((seq, HD), F32),
                pltpu.VMEM((seq, HD), F32),
                pltpu.VMEM((seq, HD), F32),
            ],
        ),
        out_shape=[
            jax.ShapeDtypeStruct((seq, width), BF16),
            jax.ShapeDtypeStruct((1, width), F32),
        ],
        compiler_params=params(),
        cost_estimate=cost(
            10 * heads * seq * seq * HD, 2 * seq * width * 4, heads * seq * seq // 2
        ),
    )(info, qkv_abs, *do_chunks, att_abs, lse, low, cos, sin, scale)


def mlp_kernel(rows, *refs):
    count = len(rows)
    xs = refs[:count]
    dhid, w, scale, hid, dz, dx_own, dx_mate, dc = refs[count:]
    tokens = dx_own.shape[0]
    sum_gate = jnp.zeros(scale.shape[1:], F32)
    sum_up = jnp.zeros(scale.shape[1:], F32)
    at = 0
    for x, r in zip(xs, rows):
        part = slice(at, at + r)
        xv = x[...]
        zg = mm(xv, w[0], 1, 1)
        zu = mm(xv, w[1], 1, 1)
        gate = zg * scale[0]
        up = zu * scale[1]
        s = 1.0 / (1.0 + jnp.exp(-gate))
        act = gate * s
        hid[part, :] = (act * up).astype(BF16)
        d = dhid[part, :].astype(F32)
        dgate = d * up * s * (1.0 + gate * (1.0 - s))
        dup = d * act
        sum_gate += jnp.sum(dgate * zg, axis=0, keepdims=True)
        sum_up += jnp.sum(dup * zu, axis=0, keepdims=True)
        dzg = (dgate * scale[0]).astype(BF16)
        dzu = (dup * scale[1]).astype(BF16)
        dz[0, part, :] = dzg
        dz[1, part, :] = dzu
        dx = (mm(dzg, w[0]) + mm(dzu, w[1])).astype(BF16)
        if at < tokens:
            dx_own[part, :] = dx
        else:
            dx_mate[at - tokens : at - tokens + r, :] = dx
        at += r
    dc[0] = sum_gate
    dc[1] = sum_up


def mlp_chunk(pieces, dhid, w, scale):
    rows = [p.shape[0] for p in pieces]
    total = sum(rows)
    _, width, depth = w.shape
    half = jax.ShapeDtypeStruct((total // 2, depth), BF16)
    return pl.pallas_call(
        functools.partial(mlp_kernel, rows),
        in_specs=[VM] * (len(pieces) + 3),
        out_specs=[VM] * 5,
        out_shape=[
            jax.ShapeDtypeStruct((total, width), BF16),
            jax.ShapeDtypeStruct((2, total, width), BF16),
            half,
            half,
            jax.ShapeDtypeStruct((2, 1, width), F32),
        ],
        compiler_params=params(),
        cost_estimate=cost(
            8 * total * depth * width, 4 * depth * width + 4 * total * depth, total * width
        ),
    )(*pieces, dhid, w, scale)


def rank_kernel(nx, nd, groups, turned, spans, *refs):
    xs = refs[:nx]
    ds = refs[nx : nx + nd]
    at, b, v, s, c, ga, gb = refs[nx + nd :]
    rank = at.shape[0]
    bs = [(b[g].astype(F32) * c[...]).astype(BF16) for g in range(groups)]
    share = rank // groups
    n_out = b.shape[2]
    ga_sum = None
    gb_sum = [None] * groups
    for xi, xa, di, da, r in spans:
        x = xs[xi][xa : xa + r, :]
        d = [ds[di][g, da : da + r, :] if groups > 1 else ds[di][da : da + r, :] for g in range(groups)]
        u = jnp.concatenate([mm(d[g], bs[g], 1, 1) for g in range(groups)], axis=1).astype(BF16)
        t = mm(x, at[...], 1, 1).astype(BF16)
        a_part = mm(u, x, 0, 0)
        ga_sum = a_part if ga_sum is None else ga_sum + a_part
        for g in range(groups):
            b_part = mm(t, d[g], 0, 0)
            gb_sum[g] = b_part if gb_sum[g] is None else gb_sum[g] + b_part
    for g in range(groups):
        rows = slice(g * share, (g + 1) * share)
        sv = s[g]
        sb = (b[g].astype(F32) * sv).astype(BF16)
        vg = v[g] if groups > 1 else v[...]
        back = mm(sb, vg, 1, 0 if turned else 1)
        ahead = mm(at[rows, :], vg, 1, 1 if turned else 0)
        ga[rows, :] = FACTOR * (ga_sum[rows, :] - back)
        gb[rows, :] = FACTOR * (gb_sum[g][rows, :] * c[...] - ahead * sv)


def rank_grads(xs, ds, at, b, v, s, turned=False, rows=None, scale=None):
    groups = b.shape[0]
    axis = 1 if groups > 1 else 0
    spans = []
    d_rows = used_rows(ds, rows) if rows else [d.shape[axis] for d in ds]
    xi = xa = di = da = 0
    while xi < len(xs):
        r = min(xs[xi].shape[0] - xa, d_rows[di] - da)
        spans.append((xi, xa, di, da, r))
        xa += r
        da += r
        if xa == xs[xi].shape[0]:
            xi, xa = xi + 1, 0
        if da == d_rows[di]:
            di, da = di + 1, 0
    total = sum(x.shape[0] for x in xs)
    rank, n_in = at.shape
    n_out = b.shape[2]
    return pl.pallas_call(
        functools.partial(rank_kernel, len(xs), len(ds), groups, turned, tuple(spans)),
        in_specs=[VM] * (len(xs) + len(ds) + 5),
        out_specs=[VM] * 2,
        out_shape=[
            jax.ShapeDtypeStruct((rank, n_in), F32),
            jax.ShapeDtypeStruct((rank, n_out), F32),
        ],
        compiler_params=params(),
        cost_estimate=cost(
            4 * total * (n_in + n_out * groups) * 256,
            2 * (total * (n_in + n_out * groups) + n_in * n_out * groups),
        ),
    )(*xs, *ds, at, b, v, s, jnp.ones((1, n_out), F32) if scale is None else scale)


def product_kernel(count, turned, spans, *refs):
    xs = refs[:count]
    w = refs[count]
    outs = refs[count + 1 :]
    for xi, oi, at, r in spans:
        outs[oi][at : at + r, :] = mm(xs[xi][...], w[...], 1, 1 if turned else 0).astype(BF16)


def used_rows(xs, tokens):
    rows = []
    left = tokens
    for x in xs:
        r = min(left, x.shape[0])
        rows.append(r)
        left -= r
        if left == 0:
            left = tokens
    return rows


def product(xs, w, turned, n_outs, steps, block=None, tokens=None):
    n = w.shape[0] if turned else w.shape[1]
    depth = w.shape[1] if turned else w.shape[0]
    tn = n // steps
    if block is not None:
        start, rows_in = block
        rows = [rows_in // n_outs] * n_outs
        x_specs = [
            pl.BlockSpec((r, depth), functools.partial(lambda k, i: (k, 0), start * n_outs + j))
            for j, r in enumerate(rows)
        ]
        xs = [xs] * n_outs
    else:
        rows = used_rows(xs, tokens) if tokens else [x.shape[0] for x in xs]
        x_specs = [pl.BlockSpec((r, depth), lambda i: (0, 0)) for r in rows]
    total = sum(rows)
    share = total // n_outs
    spans = []
    at = 0
    for xi, r in enumerate(rows):
        spans.append((xi, at // share, at % share, r))
        at += r
    w_spec = (
        pl.BlockSpec((tn, depth), lambda i: (i, 0))
        if turned
        else pl.BlockSpec((depth, tn), lambda i: (0, i))
    )
    return pl.pallas_call(
        functools.partial(product_kernel, len(xs), turned, tuple(spans)),
        grid=(steps,),
        in_specs=x_specs + [w_spec],
        out_specs=[pl.BlockSpec((share, tn), lambda i: (0, i))] * n_outs,
        out_shape=[jax.ShapeDtypeStruct((share, n), BF16)] * n_outs,
        compiler_params=params(),
        cost_estimate=cost(2 * total * n * depth, 2 * (n * depth + total * (n + depth))),
    )(*xs, w)


def down_kernel(rows, h, w, *refs):
    ds = refs[: len(rows)]
    own, other, dc = refs[len(rows) :]
    tokens = own.shape[0]
    total = jnp.zeros(dc.shape, F32)
    at = 0
    for d, r in zip(ds, rows):
        z = mm(h[at : at + r, :], w[...])
        total += jnp.sum(z * d[...].astype(F32), axis=0, keepdims=True)
        if at < tokens:
            own[at : at + r, :] = z.astype(BF16)
        else:
            other[at - tokens : at - tokens + r, :] = z.astype(BF16)
        at += r
    dc[...] = total


def down_product(h, w, ds):
    rows = [d.shape[0] for d in ds]
    total, depth = h.shape
    n = w.shape[1]
    tn = n // 2
    half = jax.ShapeDtypeStruct((total // 2, n), BF16)
    return pl.pallas_call(
        functools.partial(down_kernel, rows),
        grid=(2,),
        in_specs=[
            pl.BlockSpec((total, depth), lambda i: (0, 0)),
            pl.BlockSpec((depth, tn), lambda i: (0, i)),
        ]
        + [pl.BlockSpec((r, tn), lambda i: (0, i)) for r in rows],
        out_specs=[pl.BlockSpec((total // 2, tn), lambda i: (0, i))] * 2
        + [pl.BlockSpec((1, tn), lambda i: (0, i))],
        out_shape=[half, half, jax.ShapeDtypeStruct((1, n), F32)],
        compiler_params=params(),
        cost_estimate=cost(2 * total * n * depth, 2 * (n * depth + total * (2 * n + depth))),
    )(h, w, *ds)


def norm_forward(values):
    inverse = lax.rsqrt(jnp.mean(values * values, axis=-1, keepdims=True) + EPSILON)
    return values * inverse, inverse


def norm_backward(grad_normed, unit_vals, inverse, gain):
    scaled = grad_normed * gain
    return inverse * (scaled - unit_vals * jnp.mean(scaled * unit_vals, axis=-1, keepdims=True))


def after(value, *others):
    return lax.optimization_barrier((value,) + others)[0]


def on_device(
    sizes,
    layer_input,
    cotangent,
    segment_ids,
    token_valid,
    norm_attn,
    norm_mlp,
    base_qkv,
    base_attn_out,
    base_gate_up,
    base_down,
    rank_in_attn,
    rank_out_attn,
    magnitude_qkv,
    magnitude_out,
    rank_in_mlp,
    rank_out_mlp,
    magnitude_mlp,
    rank_in_down,
    rank_out_down,
    magnitude_down,
):
    X, C, ZH, ZL, Y = (sizes[a] for a in AXES)
    ix, ic, izh, izl, iy = (lax.axis_index(a) for a in AXES)
    dp, mp = X * C, ZH * ZL * Y
    n_dev = dp * mp
    tokens, model = layer_input.shape
    seq_len = segment_ids.shape[0]
    width = base_qkv.shape[2]
    hidden = base_gate_up.shape[2]
    heads = width // HD
    a_w = rank_in_attn.shape[1]
    f_w = rank_in_down.shape[0]
    used = 11 * a_w + 3 * f_w
    packed_w = -(-used // 128) * 128
    bq = min(512, seq_len)
    stay = ic == izh

    def from_offset(a, axis, k):
        n = sizes[axis]
        return lax.ppermute(a, axis, [(s, (s - k) % n) for s in range(n)])

    def to_offset(a, axis, k):
        n = sizes[axis]
        return lax.ppermute(a, axis, [(s, (s + k) % n) for s in range(n)])

    def mate(a):
        return from_offset(a, "c", 1)

    offsets = [(dz, dy) for dz in range(ZL) for dy in range(Y)]
    n_chips = len(offsets)

    def chips(a, off, sign):
        dz, dy = off
        perm = []
        for z in range(ZL):
            for y in range(Y):
                perm.append((z * Y + y, (z + sign * dz) % ZL * Y + (y + sign * dy) % Y))
        return lax.ppermute(a, ("zl", "y"), perm)

    def swap_rows(a):
        return lax.ppermute(a, ("c", "zh"), [(1, 2), (2, 1)])

    last = [None]

    def seq(x):
        return x if last[0] is None else after(x, last[0])

    def mark(x):
        last[0] = x
        return x

    relayed = ZL == 2 and Y == 2

    def gather_start(a):
        if relayed:
            return [[a, mate(a)], [chips(a, (0, 1), -1)], [chips(a, (1, 0), -1)]]
        return [[a, mate(a)]] + [[chips(a, o, -1)] for o in offsets[1:]]

    def gather_next(got):
        py, pz = seq(got[1][0]), seq(got[-1][0])
        if relayed:
            half = tokens // 2
            d0 = chips(pz[:half], (0, 1), -1)
            d1 = chips(py[half:], (1, 0), -1)
            return [got[0], [py, mate(py)], [pz, mate(pz)], [d0, d1]]
        return [got[0]] + [[g[0], mate(seq(g[0]))] for g in got[1:]]

    def gather_last(got):
        if relayed:
            d0, d1 = seq(got[3][0]), seq(got[3][1])
            return got[:3] + [[d0, d1, mate(d0), mate(d1)]]
        return got

    def block_of(own, other, wide=False):
        block = own.astype(F32) + mate(other).astype(F32)
        return block if wide else block.astype(BF16)

    def scatter_end(own, arrived):
        for a in arrived:
            own = own + a.astype(F32)
        return own

    def product_blocks(make, between=None):
        parts = [None] * n_chips
        for o in range(n_chips)[::-1]:
            parts[o] = make(o)
            mark(parts[o][0])
        blocks = [None] * n_chips
        if between is not None:
            blocks.append(between())
        for o in range(n_chips)[::-1]:
            own, other = parts[o]
            blocks[o] = mark(block_of(seq(own), other, wide=o == 0))
        return blocks

    def send_blocks(blocks):
        return [chips(blocks[o], offsets[o], 1) for o in range(1, n_chips)[::-1]]

    def square_sum(a):
        total = a
        for axis in ("c", "zl", "y"):
            total = sum((from_offset(total, axis, k) for k in range(1, sizes[axis])), total)
        return total

    place = np.zeros((n_dev, 2 * n_dev + 4 + 2 * n_chips), np.int32)
    for own in range(n_dev):
        x, c, zh, zl, y = np.unravel_index(own, (X, C, ZH, ZL, Y))
        xs, cs, zhs, zls, ys = np.unravel_index(np.arange(n_dev), (X, C, ZH, ZL, Y))
        order = (cs - c) % C
        order = order * X + (xs - x) % X
        order = order * Y + (ys - y) % Y
        order = order * ZL + (zls - zl) % ZL
        order = order * ZH + (zhs - zh) % ZH
        send = ((((cs - c) % C * X + xs) * ZH + zhs) * ZL + zls) * Y + ys
        blocks = [
            ((c + k) % 2 * ZL + (zl + dz) % ZL) * Y + (y + dy) % Y
            for dz, dy in offsets
            for k in range(2)
        ]
        place[own, :n_dev] = order
        place[own, n_dev : n_dev + 2] = (c * ZL + zl) * Y + y, (zh * ZL + zl) * Y + y
        place[own, n_dev + 2 : n_dev + 4] = int(c == zh), x
        place[own, n_dev + 4 : n_dev + 4 + 2 * n_chips] = blocks
        place[own, n_dev + 4 + 2 * n_chips :] = send
    own_id = (((ix * C + ic) * ZH + izh) * ZL + izl) * Y + iy
    row = lax.dynamic_slice_in_dim(jnp.asarray(place), own_id, 1, 0)[0]
    table = row[: n_dev + 2]
    flags = row[n_dev + 2 : n_dev + 4]
    blk = row[n_dev + 4 : n_dev + 4 + 2 * n_chips]
    send_table = jnp.concatenate([row[n_dev + 4 + 2 * n_chips :], row[n_dev : n_dev + 2]])

    def sds(shape, dtype=BF16):
        return jax.ShapeDtypeStruct(shape, dtype)

    packed = pl.pallas_call(
        functools.partial(pack_kernel, a_w, f_w),
        in_specs=[VM] * 10,
        out_specs=VM,
        out_shape=sds((1, R + 1, packed_w)),
    )(
        jnp.swapaxes(rank_in_attn, 1, 2),
        rank_out_attn,
        magnitude_qkv,
        magnitude_out[None],
        jnp.swapaxes(rank_in_mlp, 1, 2),
        rank_out_mlp,
        magnitude_mlp,
        rank_in_down.T[None],
        rank_out_down[None],
        magnitude_down[None],
    )
    def over_z(a):
        found = []
        for k in range(1, ZL * ZH):
            dl, dh = divmod(k, ZH)
            perm = []
            for zh in range(ZH):
                for zl in range(ZL):
                    perm.append((zh * ZL + zl, (zh - dh) % ZH * ZL + (zl - dl) % ZL))
            found.append(lax.ppermute(a, ("zh", "zl"), perm))
        return found

    gathered = jnp.concatenate([packed] + over_z(packed), axis=0)
    moved_input = swap_rows(after(layer_input, packed))
    for axis in ("y", "x", "c"):
        gathered = jnp.concatenate(
            [gathered] + [from_offset(gathered, axis, k) for k in range(1, sizes[axis])], axis=0
        )
    mark(gathered)

    def fetch(w, axis, gate):
        part = w.shape[axis] // X
        at = after(ix, *gate) if gate else ix
        mine = lax.dynamic_slice_in_dim(w, at * part, part, axis)
        return lax.ppermute(mine, ("c", "zh"), [(0, 1), (3, 2)])

    def fetch_rest(mine):
        mine = seq(mine)
        parts = [mine]
        for k in range(1, X):
            perm = []
            for x in range(X):
                for cz in (1, 2):
                    perm.append((x * 4 + cz, (x - k) % X * 4 + cz))
            parts.append(lax.ppermute(mine, ("x", "c", "zh"), perm))
        return parts

    mine_qkv = fetch(base_qkv, 1, [])
    local_input = jnp.where(stay, layer_input, seq(moved_input))
    gain_one = norm_attn.astype(F32)
    gain_two = norm_mlp.astype(F32)
    input_full = local_input.astype(F32)
    unit_one, inverse_one = norm_forward(input_full)
    normed_one = mark((unit_one * gain_one).astype(BF16))
    one = gather_start(normed_one)

    turned_gu = jnp.swapaxes(base_gate_up, 1, 2)

    (
        at_qkv, at_gu, at_o, at_d, at_o0, at_d0, b_qkv, b_blocks, b_gu, b_o, b_d, mags_qkv, m_o, m_gu, m_d,
    ) = pl.pallas_call(
        functools.partial(unpack_kernel, a_w, f_w, dp),
        in_specs=[SM, VM],
        out_specs=[VM] * 15,
        out_shape=[
            sds((3 * R, model)),
            sds((2, R, model)),
            sds((R, width)),
            sds((R, hidden)),
            sds((R, width)),
            sds((R, hidden)),
            sds((3, R, width)),
            sds((3 * R, 3 * width)),
            sds((2, R, hidden)),
            sds((R, model)),
            sds((R, model)),
            sds((1, 3 * width), F32),
            sds((1, model), F32),
            sds((2, 1, hidden), F32),
            sds((1, model), F32),
        ],
    )(table, seq(gathered))
    mark(at_qkv)

    rows_here = jnp.stack([segment_ids, token_valid])
    rows_here = jnp.where(stay, rows_here, mate(rows_here))
    segments, valid = rows_here[0], rows_here[1]
    steps = jnp.arange(seq_len, dtype=jnp.int32)
    earlier = jnp.concatenate([segments[:1] - 1, segments[:-1]])
    first = lax.cummax(jnp.where(segments != earlier, steps, 0), axis=0)
    low = first[None]
    positions = seq(steps - first)
    frequency = ROPE_BASE ** (-(2.0 * jnp.arange(HD // 2, dtype=F32)) / HD)
    sign = jnp.concatenate([-jnp.ones(HD // 2, F32), jnp.ones(HD // 2, F32)])
    angle = positions.astype(F32)[:, None] * jnp.concatenate([frequency, frequency])[None, :]
    cos, sin = jnp.cos(angle), jnp.sin(angle) * sign[None, :]
    info = jnp.concatenate([blk, jnp.sum(valid)[None].astype(jnp.int32), first[::bq] // bq])
    mark(cos)

    def rows_square(base, at0, b):
        v = base.astype(F32) + FACTOR * mm(at0, b, 0, 0)
        return jnp.sum(v * v, axis=0)

    squares = jnp.stack(
        [rows_square(base_attn_out, seq(at_o0), b_o), rows_square(base_down, seq(at_d0), b_d)]
    )
    mark(squares)

    def add_over(a, axis):
        return sum((from_offset(a, axis, k) for k in range(1, sizes[axis])), a)

    one = gather_next(one)
    parts_qkv = fetch_rest(mine_qkv)
    mine_o = fetch(base_attn_out, 1, [parts_qkv[0]])
    moved_cot = swap_rows(after(cotangent, parts_qkv[0]))
    one = gather_last(one)
    mine_gate = fetch(turned_gu[:1], 2, [one[-1][0]])
    v_qkv, square_qkv = merge_qkv(flags, base_qkv, parts_qkv, seq(at_qkv), b_qkv)
    mark(square_qkv)
    norms_qkv = jnp.sqrt(square_qkv)
    scale_qkv = mark(mags_qkv / norms_qkv)

    qkv = []
    for o in range(n_chips):
        qkv.append(mark(qkv_chunk(blk, o, one[o], v_qkv, seq(scale_qkv), cos, sin)))
    local_cot = mark(jnp.where(stay, cotangent, seq(moved_cot)))
    grad_output = local_cot.astype(F32)
    parts_o = fetch_rest(mine_o)
    rest_gate = fetch_rest(mine_gate)
    down = [[local_cot, mate(local_cot)]] + [[chips(local_cot, o, -1)] for o in offsets[1 : Y + 1]]
    mine_up = fetch(turned_gu[1:], 2, [local_cot])
    column = over_z(squares)
    qkv_abs, att_abs, att_slot, lse = attn_fwd(info, qkv, seq(low), tokens, bq)
    mark(lse)
    for i in range(1, Y + 1):
        down[i] = [mark(seq(down[i][0]))]
    v_o = mark(merge_rows(flags, base_attn_out, parts_o, seq(at_o), b_o))
    rest_up = fetch_rest(mine_up)
    squares = add_over(sum(column, seq(squares)), "y")
    blocks = product_blocks(
        lambda o: product(att_slot, seq(v_o), False, 2, 2, block=(o, 2 * tokens))
    )
    arrived = send_blocks(blocks)
    down += [[chips(seq(down[Y][0]), o, -1)] for o in offsets[1:Y]]
    down[1:] = [[p[0], mate(seq(p[0]))] for p in down[1 : Y + 1]] + down[Y + 1 :]
    mine_d = fetch(base_down, 1, [blocks[1]])
    v_gu, square_gu = merge_gu(flags, turned_gu, rest_gate, rest_up, seq(at_gu), b_gu)
    norms_gu = jnp.sqrt(square_gu)
    scale_gu = mark(m_gu / norms_gu)
    norms_rows = jnp.sqrt(squares)
    norms_o, norms_d = norms_rows[0:1], norms_rows[1:2]
    scale_o = m_o / norms_o
    scale_d = m_d / norms_d
    summed_out = scatter_end(seq(blocks[0]), arrived)
    residual = input_full + summed_out * scale_o
    unit_two, inverse_two = norm_forward(residual)
    normed_two = mark((unit_two * gain_two).astype(BF16))
    two = gather_start(normed_two)

    parts_d = fetch_rest(mine_d)
    for i in range(Y + 1, n_chips):
        down[i].append(mate(seq(down[i][0])))
    v_d, v_ds = merge_down(flags, base_down, parts_d, seq(at_d), b_d, scale_d)
    mark(v_d)
    dhid = []
    for o in range(n_chips):
        dhid.append(mark(product(down[o], seq(v_ds), True, 1, 1)[0]))
    two = gather_next(two)

    hid, dz_gu, parts, dc_gu = [], [], [], 0.0
    blocks = [None] * n_chips
    for o in range(n_chips):
        if o == n_chips - 1:
            two = gather_last(two)
        h, dz, own, other, dc = mlp_chunk(two[o], dhid[o], v_gu, seq(scale_gu))
        mark(h)
        hid.append(h)
        dz_gu.append(dz)
        parts.append((own, other))
        dc_gu = dc_gu + dc
    blocks = [None] * n_chips
    for o in list(range(1, n_chips)) + [0]:
        blocks[o] = mark(block_of(seq(parts[o][0]), parts[o][1], wide=o == 0))
    arrived = send_blocks(blocks)
    down_parts = []
    dc_down = 0.0
    for o in range(n_chips):
        own, other, dc = down_product(hid[o], seq(v_d), down[o])
        mark(dc)
        dc_down = dc_down + dc
        down_parts.append((own, other))
    def shrink(col, mags, norms):
        return col * mags / (norms * norms * norms)

    def flat(lists):
        return [p for pieces in lists for p in pieces]

    ga_gu, gb_gu = rank_grads(
        flat(two),
        dz_gu,
        seq(at_gu).reshape(2 * R, model),
        b_gu,
        v_gu,
        shrink(dc_gu, m_gu, norms_gu),
        turned=True,
    )
    mark(ga_gu)
    grad_normed_two = scatter_end(seq(blocks[0]), arrived)
    grad_residual = grad_output + norm_backward(grad_normed_two, unit_two, inverse_two, gain_two)
    col_out = jnp.sum(grad_residual * summed_out, axis=0, keepdims=True)
    extra = jnp.concatenate([col_out, dc_down, jnp.zeros((14, model), F32)], axis=0)
    low_out = mark(
        jnp.concatenate([(grad_residual * scale_o).astype(BF16), extra.astype(BF16)], axis=0)
    )
    out = gather_start(low_out)

    down_blocks = [block_of(seq(p[0]), p[1], wide=o == 0) for o, p in enumerate(down_parts)]
    mark(down_blocks[-1])
    out = gather_next(out)

    def tails(lists):
        found = []
        for pieces in lists:
            n = len(pieces) // 2
            found += [pieces[n - 1][-16:], pieces[-1][-16:]]
        return found

    do_chunks = []
    for o in range(n_chips):
        if o == n_chips - 1:
            out = gather_last(out)
        do_chunks.append(mark(product(out[o], seq(v_o), True, 1, 1, tokens=tokens)[0]))
    cols = sum(p[:2].astype(F32) for p in tails(out))
    arrived_down = send_blocks([seq(b) for b in down_blocks])
    dz_qkv, dc_qkv = attn_bwd(
        info, qkv_abs, do_chunks, att_abs, lse, seq(low), cos, sin, scale_qkv, tokens, bq
    )
    mark(dc_qkv)
    summed_down = scatter_end(seq(down_blocks[0]), arrived_down)
    output_here = mark((residual + summed_down * scale_d).astype(BF16))
    moved_output = swap_rows(output_here)
    blocks = product_blocks(
        lambda o: product(dz_qkv, seq(v_qkv), True, 2, 2, block=(o, 2 * tokens)),
        lambda: mark(jnp.where(stay, output_here, seq(moved_output))),
    )
    layer_output = blocks.pop()
    arrived = send_blocks(blocks)

    ga_qkv, gb_all = rank_grads(
        flat(one),
        [dz_qkv],
        seq(at_qkv),
        b_blocks[None],
        v_qkv,
        shrink(dc_qkv, mags_qkv, norms_qkv)[None],
    )
    mark(ga_qkv)
    ga_o, gb_o = rank_grads(
        [att_slot],
        flat(out),
        seq(at_o),
        b_o[None],
        v_o,
        shrink(cols[0:1], m_o, norms_o)[None],
        rows=tokens,
    )
    mark(ga_o)
    ga_d, gb_d = rank_grads(
        hid,
        flat(down),
        seq(at_d),
        b_d[None],
        v_d,
        shrink(cols[1:2], m_d, norms_d)[None],
        scale=scale_d,
    )
    mark(ga_d)
    grad_normed_one = scatter_end(seq(blocks[0]), arrived)
    grad_here = grad_residual + norm_backward(grad_normed_one, unit_one, inverse_one, gain_one)
    low_here = mark(grad_here.astype(BF16))
    input_grad = jnp.where(stay, grad_here, swap_rows(low_here).astype(F32))
    mag_full = jnp.concatenate([col_out / norms_o, dc_down / norms_d], axis=0)
    grads = pl.pallas_call(
        functools.partial(pack_grads_kernel, a_w, f_w, dp),
        in_specs=[SM] + [VM] * 11,
        out_specs=VM,
        out_shape=sds((n_dev, R + 1, packed_w)),
    )(
        send_table,
        seq(ga_qkv),
        ga_gu,
        gb_o,
        gb_d,
        mag_full,
        ga_o,
        ga_d,
        gb_all,
        gb_gu,
        dc_qkv / norms_qkv,
        dc_gu / norms_gu,
    )
    half = n_dev // 2
    grads = grads[:half].astype(F32) + mate(grads[half:]).astype(F32)
    pieces = lax.all_to_all(
        grads.astype(BF16), ("x", "zh", "zl", "y"), split_axis=0, concat_axis=0, tiled=True
    )
    grads = jnp.sum(pieces.astype(F32), axis=0, keepdims=True)
    a1, b1, mq, mo, a2, b2, mm_, a3, b3, md = pl.pallas_call(
        functools.partial(unpack_grads_kernel, a_w, f_w),
        in_specs=[VM],
        out_specs=[VM] * 10,
        out_shape=[
            sds((4, R, a_w), F32),
            sds((4, R, a_w), F32),
            sds((3, a_w), F32),
            sds((1, a_w), F32),
            sds((2, R, a_w), F32),
            sds((2, R, f_w), F32),
            sds((2, f_w), F32),
            sds((1, R, f_w), F32),
            sds((1, R, a_w), F32),
            sds((1, a_w), F32),
        ],
    )(grads)
    return (
        layer_output,
        input_grad,
        jnp.swapaxes(a1, 1, 2),
        b1,
        mq,
        mo[0],
        jnp.swapaxes(a2, 1, 2),
        b2,
        mm_,
        a3[0].T,
        b3[0],
        md[0],
    )


def solution(mesh):
    dp, mp = mesh.shape["dp"], mesh.shape["mp"]
    shape = (dp // 2, 2, 2, 2, mp // 4)
    fine = Mesh(mesh.devices.reshape(shape), AXES)
    rows, cols = ("x", "c"), ("zh", "zl", "y")
    both = rows + cols
    return jax.shard_map(
        functools.partial(on_device, dict(zip(AXES, shape))),
        mesh=fine,
        in_specs=(
            P(both, None),
            P(both, None),
            P(rows),
            P(rows),
            P(),
            P(),
            P(None, None, cols),
            P(cols, None),
            P(None, None, cols),
            P(cols, None),
            P(None, both, None),
            P(None, None, both),
            P(None, both),
            P(both),
            P(None, both, None),
            P(None, None, both),
            P(None, both),
            P(both, None),
            P(None, both),
            P(both),
        ),
        out_specs=(
            P(both, None),
            P(both, None),
            P(None, both, None),
            P(None, None, both),
            P(None, both),
            P(both),
            P(None, both, None),
            P(None, None, both),
            P(None, both),
            P(both, None),
            P(None, both),
            P(both),
        ),
        check_vma=False,
    )
```

```python
import functools

import jax
import jax.numpy as jnp
import numpy as np
from jax import lax
from jax.experimental import pallas as pl
from jax.experimental.pallas import tpu as pltpu
from jax.sharding import Mesh
from jax.sharding import PartitionSpec as P

HD = 128
R = 16
ALPHA = 32
FACTOR = ALPHA / R
EPSILON = 1e-05
ROPE_BASE = 10000.0
BF16 = jnp.bfloat16
F32 = jnp.float32
NEG = -1e30
LOG2E = 1.4426950408889634
AXES = ("x", "c", "zh", "zl", "y")
VM = pl.BlockSpec(memory_space=pltpu.VMEM)
SM = pl.BlockSpec(memory_space=pltpu.SMEM)


def mm(left, right, lc=1, rc=0, precision=None):
    return lax.dot_general(
        left,
        right,
        (((lc,), (rc,)), ((), ())),
        preferred_element_type=F32,
        precision=precision,
    )


def params(mib=18):
    return pltpu.CompilerParams(vmem_limit_bytes=mib * 1024 * 1024)


def cost(flops, nbytes, trans=0):
    scale = 10**6
    return pl.CostEstimate(
        flops=int(flops) // scale,
        bytes_accessed=int(nbytes) // scale,
        transcendentals=int(trans) // scale,
    )


class Shift:
    def __init__(self, ref, at):
        self.ref, self.at = ref, at

    def __getitem__(self, i):
        return self.ref[self.at + i]


def pack_kernel(a_w, f_w, a1, b1, mq, mo, a2, b2, mm_, a3, b3, md, out):
    out[...] = jnp.zeros(out.shape, out.dtype)
    at = 0
    for ref, count, w in ((a1, 4, a_w), (a2, 2, a_w), (a3, 1, f_w), (b1, 4, a_w), (b2, 2, f_w), (b3, 1, a_w)):
        for p in range(count):
            out[0, :R, at : at + w] = ref[p].astype(BF16)
            at += w
    at = 0
    for ref, count, w in ((mq, 3, a_w), (mo, 1, a_w), (mm_, 2, f_w), (md, 1, a_w)):
        for p in range(count):
            out[0, R : R + 1, at : at + w] = ref[p : p + 1, :].astype(BF16)
            at += w


def unpack_grads_kernel(a_w, f_w, g, a1, b1, mq, mo, a2, b2, mm_, a3, b3, md):
    at = 0
    for ref, count, w in ((a1, 4, a_w), (a2, 2, a_w), (a3, 1, f_w), (b1, 4, a_w), (b2, 2, f_w), (b3, 1, a_w)):
        for p in range(count):
            ref[p] = g[0, :R, at : at + w]
            at += w
    at = 0
    for ref, count, w in ((mq, 3, a_w), (mo, 1, a_w), (mm_, 2, f_w), (md, 1, a_w)):
        for p in range(count):
            ref[p : p + 1, :] = g[0, R : R + 1, at : at + w]
            at += w


def unpack_kernel(
    a_w, f_w, dp, table, g, at_qkv, at_gu, at_o, at_d, at_o0, at_d0,
    b_qkv, b_blocks, b_gu, b_o, b_d, m_qkv, m_o, m_gu, m_d,
):
    b_blocks[...] = jnp.zeros(b_blocks.shape, b_blocks.dtype)
    n = g.shape[0]
    order, where_ = Shift(table, 0), Shift(table, n)
    b_at = 6 * a_w + f_w
    for d in range(n):
        s = order[d]
        lo, hi = d * a_w, (d + 1) * a_w
        for p in range(3):
            at_qkv[p * R : (p + 1) * R, lo:hi] = g[s, :R, p * a_w : (p + 1) * a_w]
        for p in range(2):
            at_gu[p, :, lo:hi] = g[s, :R, (4 + p) * a_w : (5 + p) * a_w]
        b_o[:, lo:hi] = g[s, :R, b_at + 3 * a_w : b_at + 4 * a_w]
        end = b_at + 4 * a_w + 2 * f_w
        b_d[:, lo:hi] = g[s, :R, end : end + a_w]
        m_o[:, lo:hi] = g[s, R : R + 1, 3 * a_w : 4 * a_w].astype(F32)
        end = 4 * a_w + 2 * f_w
        m_d[:, lo:hi] = g[s, R : R + 1, end : end + a_w].astype(F32)
    for i in range(dp):
        s = order[where_[0] * dp + i]
        lo, hi = i * a_w, (i + 1) * a_w
        flo, fhi = i * f_w, (i + 1) * f_w
        at_o[:, lo:hi] = g[s, :R, 3 * a_w : 4 * a_w]
        at_d[:, flo:fhi] = g[s, :R, 6 * a_w : 6 * a_w + f_w]
        for p in range(3):
            b_qkv[p, :, lo:hi] = g[s, :R, b_at + p * a_w : b_at + (p + 1) * a_w]
            for h, at in pieces_of(lo, hi):
                head, inner = divmod(h, HD)
                to = (head * 3 + p) * HD + inner
                w = at[1] - at[0]
                src = p * a_w + at[0]
                b_blocks[p * R : (p + 1) * R, to : to + w] = g[s, :R, b_at + src : b_at + src + w]
                m_qkv[:, to : to + w] = g[s, R : R + 1, src : src + w].astype(F32)
        for p in range(2):
            e = b_at + 4 * a_w + p * f_w
            b_gu[p, :, flo:fhi] = g[s, :R, e : e + f_w]
            e = 4 * a_w + p * f_w
            m_gu[p, :, flo:fhi] = g[s, R : R + 1, e : e + f_w].astype(F32)
        s = order[where_[1] * dp + i]
        at_o0[:, lo:hi] = g[s, :R, 3 * a_w : 4 * a_w]
        at_d0[:, flo:fhi] = g[s, :R, 6 * a_w : 6 * a_w + f_w]


def pieces_of(lo, hi):
    found = []
    at = lo
    while at < hi:
        end = min(hi, (at // HD + 1) * HD)
        found.append((at, (at - lo, end - lo)))
        at = end
    return found


def pack_grads_kernel(
    a_w, f_w, dp, table, ga_qkv, ga_gu, gb_o, gb_d, m_full, ga_attn, ga_d, gb_all, gb_gu,
    m_qkv, m_gu, out
):
    n = out.shape[0]
    order, where_ = Shift(table, 0), Shift(table, n)
    heads = m_qkv.shape[1] // (3 * HD)
    out[...] = jnp.zeros(out.shape, out.dtype)
    b_at = 6 * a_w + f_w
    dt = out.dtype
    for d in range(n):
        s = order[d]
        lo, hi = d * a_w, (d + 1) * a_w
        for p in range(3):
            out[s, :R, p * a_w : (p + 1) * a_w] = ga_qkv[p * R : (p + 1) * R, lo:hi].astype(dt)
        for p in range(2):
            e = (4 + p) * a_w
            out[s, :R, e : e + a_w] = ga_gu[p * R : (p + 1) * R, lo:hi].astype(dt)
        out[s, :R, b_at + 3 * a_w : b_at + 4 * a_w] = gb_o[:, lo:hi].astype(dt)
        end = b_at + 4 * a_w + 2 * f_w
        out[s, :R, end : end + a_w] = gb_d[:, lo:hi].astype(dt)
        out[s, R : R + 1, 3 * a_w : 4 * a_w] = m_full[0:1, lo:hi].astype(dt)
        end = 4 * a_w + 2 * f_w
        out[s, R : R + 1, end : end + a_w] = m_full[1:2, lo:hi].astype(dt)
    for i in range(dp):
        s = order[where_[0] * dp + i]
        lo, hi = i * a_w, (i + 1) * a_w
        flo, fhi = i * f_w, (i + 1) * f_w
        out[s, :R, 3 * a_w : 4 * a_w] = ga_attn[:, lo:hi].astype(dt)
        out[s, :R, 6 * a_w : 6 * a_w + f_w] = ga_d[:, flo:fhi].astype(dt)
        for p in range(3):
            for h, at in pieces_of(lo, hi):
                head, inner = divmod(h, HD)
                src = (head * 3 + p) * HD + inner
                w = at[1] - at[0]
                to = p * a_w + at[0]
                out[s, :R, b_at + to : b_at + to + w] = gb_all[p * R : (p + 1) * R, src : src + w].astype(dt)
                out[s, R : R + 1, to : to + w] = m_qkv[:, src : src + w].astype(dt)
        for p in range(2):
            e = b_at + 4 * a_w + p * f_w
            out[s, :R, e : e + f_w] = gb_gu[p * R : (p + 1) * R, flo:fhi].astype(dt)
            e = 4 * a_w + p * f_w
            out[s, R : R + 1, e : e + f_w] = m_gu[p, :, flo:fhi].astype(dt)


def pick(flags, t, own, parts):
    n = len(parts)
    k = lax.rem(t - flags[1] + n, n)
    w = parts[0]
    for i in range(1, n):
        w = jnp.where(k == i, parts[i], w)
    return jnp.where(flags[0] == 1, own, w)


def own_block(t, f):
    return t * f[0]


def merge_qkv_kernel(n, flags, own, *refs):
    parts = refs[:n]
    at, b, vb, ssq = refs[n:]
    t = pl.program_id(0)

    @pl.when(t == 0)
    def _():
        ssq[...] = jnp.zeros_like(ssq)

    members, _, width = own.shape
    for p in range(members):
        w = pick(flags, t, own[p], [r[p] for r in parts])
        v = w.astype(F32) + FACTOR * mm(at[p * R : (p + 1) * R, :], b[p], 0, 0)
        total = jnp.sum(v * v, axis=0, keepdims=True)
        vb16 = v.astype(BF16)
        for h in range(width // HD):
            to = slice((h * members + p) * HD, (h * members + p + 1) * HD)
            vb[:, to] = vb16[:, h * HD : (h + 1) * HD]
            ssq[:, to] += total[:, h * HD : (h + 1) * HD]


def merge_qkv(flags, own, parts, at_qkv, b_qkv):
    members, rows, width = own.shape
    n = len(parts)
    part_rows = rows // n
    block = (members, part_rows, width)
    return pl.pallas_call(
        functools.partial(merge_qkv_kernel, n),
        grid_spec=pltpu.PrefetchScalarGridSpec(
            num_scalar_prefetch=1,
            grid=(n,),
            in_specs=[pl.BlockSpec(block, lambda t, f: (0, own_block(t, f), 0))]
            + [pl.BlockSpec(block, lambda t, f: (0, 0, 0))] * n
            + [
                pl.BlockSpec((members * R, part_rows), lambda t, f: (0, t)),
                pl.BlockSpec((members, R, width), lambda t, f: (0, 0, 0)),
            ],
            out_specs=[
                pl.BlockSpec((part_rows, members * width), lambda t, f: (t, 0)),
                pl.BlockSpec((1, members * width), lambda t, f: (0, 0)),
            ],
        ),
        out_shape=[
            jax.ShapeDtypeStruct((rows, members * width), BF16),
            jax.ShapeDtypeStruct((1, members * width), F32),
        ],
        compiler_params=params(),
        cost_estimate=cost(2 * rows * width * members * 256, 4 * members * rows * width * 2),
    )(flags, own, *parts, at_qkv, b_qkv)


def merge_gu_kernel(n, flags, own, *refs):
    gates, ups = refs[:n], refs[n : 2 * n]
    at, b, vb, ssq, acc = refs[2 * n :]
    t = pl.program_id(1)
    first = pl.program_id(0) == 0
    w = pick(flags, t, own[0], [jnp.where(first, g[0], u[0]) for g, u in zip(gates, ups)])
    v = w.astype(F32) + FACTOR * mm(b[0], at[0], 0, 0)
    vb[0] = v.astype(BF16)
    sq = v * v
    lanes = sq[:, :HD]
    for i in range(1, sq.shape[1] // HD):
        lanes = lanes + sq[:, i * HD : (i + 1) * HD]

    @pl.when(t == 0)
    def _():
        acc[...] = lanes

    @pl.when(t > 0)
    def _():
        acc[...] += lanes

    @pl.when(t == pl.num_programs(1) - 1)
    def _():
        ssq[0] = mm(jnp.ones((8, HD), F32), acc[...], 1, 1, lax.Precision.HIGHEST)[:1]


def merge_gu(flags, own, gates, ups, at_gu, b_gu):
    members, width, rows = own.shape
    n = len(gates)
    part_rows = rows // n
    block = (1, width, part_rows)
    return pl.pallas_call(
        functools.partial(merge_gu_kernel, n),
        grid_spec=pltpu.PrefetchScalarGridSpec(
            num_scalar_prefetch=1,
            grid=(members, n),
            in_specs=[pl.BlockSpec(block, lambda p, t, f: (p * f[0], 0, own_block(t, f)))]
            + [pl.BlockSpec(block, lambda p, t, f: (0, 0, 0))] * (2 * n)
            + [
                pl.BlockSpec((1, R, part_rows), lambda p, t, f: (p, 0, t)),
                pl.BlockSpec((1, R, width), lambda p, t, f: (p, 0, 0)),
            ],
            out_specs=[
                pl.BlockSpec(block, lambda p, t, f: (p, 0, t)),
                pl.BlockSpec((1, 1, width), lambda p, t, f: (p, 0, 0)),
            ],
            scratch_shapes=[pltpu.VMEM((width, HD), F32)],
        ),
        out_shape=[
            jax.ShapeDtypeStruct((members, width, rows), BF16),
            jax.ShapeDtypeStruct((members, 1, width), F32),
        ],
        compiler_params=params(),
        cost_estimate=cost(2 * rows * width * members * 256, 4 * members * rows * width * 2),
    )(flags, own, *gates, *ups, at_gu, b_gu)


def merge_rows_kernel(n, flags, own, *refs):
    parts = refs[:n]
    at, b, vb = refs[n:]
    w = pick(flags, pl.program_id(0), own[...], [r[...] for r in parts])
    v = w.astype(F32) + FACTOR * mm(at[...], b[...], 0, 0)
    vb[...] = v.astype(BF16)


def merge_rows(flags, own, parts, at, b):
    rows, width = own.shape
    xs = len(parts)
    part = width // xs
    return pl.pallas_call(
        functools.partial(merge_rows_kernel, xs),
        grid_spec=pltpu.PrefetchScalarGridSpec(
            num_scalar_prefetch=1,
            grid=(xs,),
            in_specs=[pl.BlockSpec((rows, part), lambda t, f: (0, own_block(t, f)))]
            + [pl.BlockSpec((rows, part), lambda t, f: (0, 0))] * xs
            + [
                pl.BlockSpec((R, rows), lambda t, f: (0, 0)),
                pl.BlockSpec((R, part), lambda t, f: (0, t)),
            ],
            out_specs=pl.BlockSpec((rows, part), lambda t, f: (0, t)),
        ),
        out_shape=jax.ShapeDtypeStruct((rows, width), BF16),
        compiler_params=params(),
        cost_estimate=cost(2 * rows * width * 256, 4 * rows * width * 2),
    )(flags, own, *parts, at, b)


def merge_down_kernel(n, flags, own, *refs):
    parts = refs[:n]
    at, b, scale, vb, vs = refs[n:]
    w = pick(flags, pl.program_id(0), own[...], [r[...] for r in parts])
    v = (w.astype(F32) + FACTOR * mm(at[...], b[...], 0, 0)).astype(BF16)
    vb[...] = v
    vs[...] = (v.astype(F32) * scale[...]).astype(BF16)


def merge_down(flags, own, parts, at, b, scale):
    rows, width = own.shape
    n = len(parts)
    part = width // n
    return pl.pallas_call(
        functools.partial(merge_down_kernel, n),
        grid_spec=pltpu.PrefetchScalarGridSpec(
            num_scalar_prefetch=1,
            grid=(n,),
            in_specs=[pl.BlockSpec((rows, part), lambda t, f: (0, own_block(t, f)))]
            + [pl.BlockSpec((rows, part), lambda t, f: (0, 0))] * n
            + [
                pl.BlockSpec((R, rows), lambda t, f: (0, 0)),
                pl.BlockSpec((R, part), lambda t, f: (0, t)),
                pl.BlockSpec((1, part), lambda t, f: (0, t)),
            ],
            out_specs=[pl.BlockSpec((rows, part), lambda t, f: (0, t))] * 2,
        ),
        out_shape=[jax.ShapeDtypeStruct((rows, width), BF16)] * 2,
        compiler_params=params(),
        cost_estimate=cost(2 * rows * width * 256, 5 * rows * width * 2),
    )(flags, own, *parts, at, b, scale)


def qkv_kernel(rows, blk, *refs):
    count = len(rows)
    xs = refs[:count]
    w, scale, cos0, cos1, sin0, sin1, out = refs[count:]
    cos = jnp.concatenate([cos0[...], cos1[...]], axis=0)
    sin = jnp.concatenate([sin0[...], sin1[...]], axis=0)
    at = 0
    for x, r in zip(xs, rows):
        z = mm(x[...], w[...]) * scale[...]
        co, si = cos[at : at + r], sin[at : at + r]
        q = z[:, :HD]
        k = z[:, HD : 2 * HD]
        q = (q * co + pltpu.roll(q, HD // 2, 1) * si) * (LOG2E * HD ** (-0.5))
        k = k * co + pltpu.roll(k, HD // 2, 1) * si
        out[at : at + r, :HD] = q.astype(BF16)
        out[at : at + r, HD : 2 * HD] = k.astype(BF16)
        out[at : at + r, 2 * HD :] = z[:, 2 * HD :].astype(BF16)
        at += r


def qkv_chunk(blk, chunk, pieces, w, scale, cos, sin):
    rows = [p.shape[0] for p in pieces]
    total = sum(rows)
    tokens = total // 2
    depth, width = w.shape
    heads = width // (3 * HD)

    def table(k):
        return pl.BlockSpec((tokens, HD), lambda h, b: (b[2 * chunk + k], 0))

    return pl.pallas_call(
        functools.partial(qkv_kernel, rows),
        grid_spec=pltpu.PrefetchScalarGridSpec(
            num_scalar_prefetch=1,
            grid=(heads,),
            in_specs=[pl.BlockSpec((r, depth), lambda h, b: (0, 0)) for r in rows]
            + [
                pl.BlockSpec((depth, 3 * HD), lambda h, b: (0, h)),
                pl.BlockSpec((1, 3 * HD), lambda h, b: (0, h)),
                table(0),
                table(1),
                table(0),
                table(1),
            ],
            out_specs=pl.BlockSpec((total, 3 * HD), lambda h, b: (0, h)),
        ),
        out_shape=jax.ShapeDtypeStruct((total, width), BF16),
        compiler_params=params(),
        cost_estimate=cost(2 * total * depth * width, 2 * (depth * width + total * depth)),
    )(blk, *pieces, w, scale, cos, cos, sin, sin)


def masked(scores, low, first_key, first_query, valid_count, diagonal):
    keys = first_key + lax.broadcasted_iota(jnp.int32, (scores.shape[0], 1), 0)
    if not diagonal:
        allowed = (keys >= low) & (keys < valid_count)
        return jnp.where(allowed, scores, NEG)
    queries = first_query + lax.broadcasted_iota(jnp.int32, (1, scores.shape[1]), 1)
    high = jnp.minimum(queries, valid_count - 1)
    allowed = ((keys >= low) & (keys <= high)) | (keys == queries)
    return jnp.where(allowed, scores, NEG)


def attn_fwd_kernel(n_chunks, tokens, bq, info, *refs):
    chunks = refs[:n_chunks]
    low, qkv_abs, att_abs, att_slot, lse, m_sc, l_sc, acc = refs[n_chunks:]
    i = pl.program_id(0)
    last = pl.num_programs(0) - 1
    heads = m_sc.shape[0]
    slots = 2 * n_chunks
    valid_count = info[slots]

    @pl.when(i == 0)
    def _():
        for s in range(slots):
            start = pl.multiple_of(info[s] * tokens, tokens)
            qkv_abs[pl.ds(start, tokens), :] = chunks[s // 2][
                (s % 2) * tokens : (s % 2 + 1) * tokens, :
            ]

    q0 = pl.multiple_of(i * bq, bq)
    rows = pl.ds(q0, bq)
    lo = low[:, rows]
    m_sc[...] = jnp.full(m_sc.shape, NEG, F32)
    l_sc[...] = jnp.zeros_like(l_sc)
    acc[...] = jnp.zeros_like(acc)

    def step(j, diagonal):
        k0 = pl.multiple_of(j * bq, bq)
        keys = pl.ds(k0, bq)
        for h in range(heads):
            at = 3 * HD * h
            q = qkv_abs[rows, at : at + HD]
            k = qkv_abs[keys, at + HD : at + 2 * HD]
            v = qkv_abs[keys, at + 2 * HD : at + 3 * HD]
            s = masked(mm(k, q, 1, 1), lo, k0, q0, valid_count, diagonal)
            m_old = m_sc[h]
            m_new = jnp.maximum(m_old, jnp.max(s, axis=0, keepdims=True))
            p = jnp.exp2(s - m_new)
            alpha = jnp.exp2(m_old - m_new)
            m_sc[h] = m_new
            l_sc[h] = l_sc[h] * alpha + jnp.sum(p, axis=0, keepdims=True)
            acc[h] = acc[h] * alpha + mm(v, p.astype(BF16), 0, 0)

    def full(j, carry):
        step(j, False)
        return carry

    lax.fori_loop(info[slots + 1 + i], i, full, 0)
    step(i, True)
    for h in range(heads):
        total = l_sc[h]
        lse[h, :, rows] = m_sc[h] + jnp.log2(total)
        att_abs[rows, h * HD : (h + 1) * HD] = (acc[h] / total).T.astype(BF16)

    @pl.when(i == last)
    def _():
        for s in range(slots):
            start = pl.multiple_of(info[s] * tokens, tokens)
            att_slot[s * tokens : (s + 1) * tokens, :] = att_abs[pl.ds(start, tokens), :]


def attn_fwd(info, chunks, low, tokens, bq):
    rows, width = chunks[0].shape
    heads = width // (3 * HD)
    seq = rows * len(chunks)
    n_blocks = seq // bq
    whole = pl.BlockSpec((seq, heads * HD), lambda i, f: (0, 0))
    return pl.pallas_call(
        functools.partial(attn_fwd_kernel, len(chunks), tokens, bq),
        grid_spec=pltpu.PrefetchScalarGridSpec(
            num_scalar_prefetch=1,
            grid=(n_blocks,),
            in_specs=[pl.BlockSpec((rows, width), lambda i, f: (0, 0))] * len(chunks)
            + [pl.BlockSpec((1, seq), lambda i, f: (0, 0))],
            out_specs=[
                pl.BlockSpec((seq, width), lambda i, f: (0, 0)),
                whole,
                whole,
                pl.BlockSpec((heads, 1, seq), lambda i, f: (0, 0, 0)),
            ],
            scratch_shapes=[
                pltpu.VMEM((heads, 1, bq), F32),
                pltpu.VMEM((heads, 1, bq), F32),
                pltpu.VMEM((heads, HD, bq), F32),
            ],
        ),
        out_shape=[
            jax.ShapeDtypeStruct((seq, width), BF16),
            jax.ShapeDtypeStruct((seq, heads * HD), BF16),
            jax.ShapeDtypeStruct((seq, heads * HD), BF16),
            jax.ShapeDtypeStruct((heads, 1, seq), F32),
        ],
        compiler_params=params(40),
        cost_estimate=cost(
            4 * heads * seq * seq * HD, 2 * seq * width * 3, heads * seq * seq // 2
        ),
    )(info, *chunks, low)


def attn_bwd_kernel(n_chunks, tokens, bq, info, qkv, *refs):
    dos = refs[:n_chunks]
    att, lse, low, cos, sin, scale, dz, dc, do_abs, delta, dq, dk, dv = refs[n_chunks:]
    slots = 2 * n_chunks
    valid_count = info[slots]
    seq = qkv.shape[0]
    heads = dq.shape[0]
    n_blocks = seq // bq
    for s in range(slots):
        start = pl.multiple_of(info[s] * tokens, tokens)
        do_abs[pl.ds(start, tokens), :] = dos[s // 2][(s % 2) * tokens : (s % 2 + 1) * tokens, :]
    ones = jnp.ones((8, HD), F32)

    def sums(i, c):
        r = pl.ds(pl.multiple_of(i * bq, bq), bq)
        for h in range(heads):
            cols = slice(h * HD, (h + 1) * HD)
            prod = do_abs[r, cols].astype(F32) * att[r, cols].astype(F32)
            delta[h, :, r] = mm(ones, prod, 1, 1, lax.Precision.HIGHEST)[:1]
        return c

    lax.fori_loop(0, n_blocks, sums, 0)

    def outer(j, carry):
        k0 = pl.multiple_of(j * bq, bq)
        krow = pl.ds(k0, bq)

        def pair(i, diagonal):
            q0 = pl.multiple_of(i * bq, bq)
            qrow = pl.ds(q0, bq)
            lo = low[:, qrow]
            for h in range(heads):
                at = 3 * HD * h
                k = qkv[krow, at + HD : at + 2 * HD]
                v = qkv[krow, at + 2 * HD : at + 3 * HD]
                q = qkv[qrow, at : at + HD]
                do = do_abs[qrow, h * HD : (h + 1) * HD]
                s = masked(mm(k, q, 1, 1), lo, k0, q0, valid_count, diagonal)
                p = jnp.exp2(s - lse[h, :, qrow])
                dp = mm(v, do, 1, 1)
                ds = (p * (dp - delta[h, :, qrow])).astype(BF16)
                if diagonal:
                    dv[h, krow, :] = mm(p.astype(BF16), do)
                    dk[h, krow, :] = mm(ds, q)
                else:
                    dv[h, krow, :] += mm(p.astype(BF16), do)
                    dk[h, krow, :] += mm(ds, q)
                part = mm(ds, k, 0, 0)

                @pl.when(j == info[slots + 1 + i])
                def _():
                    dq[h, qrow, :] = part

                @pl.when(j > info[slots + 1 + i])
                def _():
                    dq[h, qrow, :] += part

        pair(j, True)

        def inner(i, c):
            @pl.when(info[slots + 1 + i] <= j)
            def _():
                pair(i, False)

            return c

        return lax.fori_loop(j + 1, n_blocks, inner, carry)

    lax.fori_loop(0, n_blocks, outer, 0)
    half = HD // 2
    dc[...] = jnp.zeros_like(dc)

    def finish(s, c):
        rows = pl.ds(pl.multiple_of(info[s] * tokens, tokens), tokens)
        out = pl.ds(pl.multiple_of(s * tokens, tokens), tokens)
        co, si = cos[rows, :], sin[rows, :]

        def back(u):
            return u * co - pltpu.roll(u, half, 1) * si

        for h in range(heads):
            at = 3 * HD * h
            qc, kc, vc = (slice(at + n * HD, at + (n + 1) * HD) for n in range(3))
            gq = back(dq[h, rows, :]) * HD ** (-0.5)
            gk = back(dk[h, rows, :]) * (1 / LOG2E)
            gv = dv[h, rows, :]
            q = back(qkv[rows, qc].astype(F32)) * (HD**0.5 / LOG2E)
            k = back(qkv[rows, kc].astype(F32))
            v = qkv[rows, vc].astype(F32)
            dc[:, qc] += jnp.sum(gq * q, axis=0, keepdims=True)
            dc[:, kc] += jnp.sum(gk * k, axis=0, keepdims=True)
            dc[:, vc] += jnp.sum(gv * v, axis=0, keepdims=True)
            dz[out, qc] = (gq * scale[:, qc]).astype(BF16)
            dz[out, kc] = (gk * scale[:, kc]).astype(BF16)
            dz[out, vc] = (gv * scale[:, vc]).astype(BF16)
        return c

    lax.fori_loop(0, slots, finish, 0)
    dc[...] = dc[...] / scale[...]


def attn_bwd(info, qkv_abs, do_chunks, att_abs, lse, low, cos, sin, scale, tokens, bq):
    seq, width = qkv_abs.shape
    heads = width // (3 * HD)
    return pl.pallas_call(
        functools.partial(attn_bwd_kernel, len(do_chunks), tokens, bq),
        in_specs=[SM] + [VM] * (len(do_chunks) + 7),
        out_specs=[VM] * 2,
        scratch_shapes=[
            pltpu.VMEM((seq, heads * HD), BF16),
            pltpu.VMEM((heads, 1, seq), F32),
            pltpu.VMEM((heads, seq, HD), F32),
            pltpu.VMEM((heads, seq, HD), F32),
            pltpu.VMEM((heads, seq, HD), F32),
        ],
        out_shape=[
            jax.ShapeDtypeStruct((seq, width), BF16),
            jax.ShapeDtypeStruct((1, width), F32),
        ],
        compiler_params=params(44),
        cost_estimate=cost(
            10 * heads * seq * seq * HD, 2 * seq * width * 4, heads * seq * seq // 2
        ),
    )(info, qkv_abs, *do_chunks, att_abs, lse, low, cos, sin, scale)


def mlp_kernel(rows, *refs):
    count = len(rows)
    xs = refs[:count]
    dhid, w, scale, hid, dz, dx_own, dx_mate, dc = refs[count:]
    tokens = dx_own.shape[0]
    sum_gate = jnp.zeros(scale.shape[1:], F32)
    sum_up = jnp.zeros(scale.shape[1:], F32)
    at = 0
    for x, r in zip(xs, rows):
        part = slice(at, at + r)
        xv = x[...]
        zg = mm(xv, w[0], 1, 1)
        zu = mm(xv, w[1], 1, 1)
        gate = zg * scale[0]
        up = zu * scale[1]
        s = 1.0 / (1.0 + jnp.exp(-gate))
        act = gate * s
        hid[part, :] = (act * up).astype(BF16)
        d = dhid[part, :].astype(F32)
        dgate = d * up * s * (1.0 + gate * (1.0 - s))
        dup = d * act
        sum_gate += jnp.sum(dgate * zg, axis=0, keepdims=True)
        sum_up += jnp.sum(dup * zu, axis=0, keepdims=True)
        dzg = (dgate * scale[0]).astype(BF16)
        dzu = (dup * scale[1]).astype(BF16)
        dz[0, part, :] = dzg
        dz[1, part, :] = dzu
        dx = (mm(dzg, w[0]) + mm(dzu, w[1])).astype(BF16)
        if at < tokens:
            dx_own[part, :] = dx
        else:
            dx_mate[at - tokens : at - tokens + r, :] = dx
        at += r
    dc[0] = sum_gate
    dc[1] = sum_up


def mlp_chunk(pieces, dhid, w, scale):
    rows = [p.shape[0] for p in pieces]
    total = sum(rows)
    _, width, depth = w.shape
    half = jax.ShapeDtypeStruct((total // 2, depth), BF16)
    return pl.pallas_call(
        functools.partial(mlp_kernel, rows),
        in_specs=[VM] * (len(pieces) + 3),
        out_specs=[VM] * 5,
        out_shape=[
            jax.ShapeDtypeStruct((total, width), BF16),
            jax.ShapeDtypeStruct((2, total, width), BF16),
            half,
            half,
            jax.ShapeDtypeStruct((2, 1, width), F32),
        ],
        compiler_params=params(),
        cost_estimate=cost(
            8 * total * depth * width, 4 * depth * width + 4 * total * depth, total * width
        ),
    )(*pieces, dhid, w, scale)


def rank_kernel(nx, nd, groups, turned, spans, *refs):
    xs = refs[:nx]
    ds = refs[nx : nx + nd]
    at, b, v, s, c, ga, gb = refs[nx + nd :]
    rank = at.shape[0]
    bs = [(b[g].astype(F32) * c[...]).astype(BF16) for g in range(groups)]
    share = rank // groups
    n_out = b.shape[2]
    ga_sum = None
    gb_sum = [None] * groups
    for xi, xa, di, da, r in spans:
        x = xs[xi][xa : xa + r, :]
        d = [ds[di][g, da : da + r, :] if groups > 1 else ds[di][da : da + r, :] for g in range(groups)]
        u = jnp.concatenate([mm(d[g], bs[g], 1, 1) for g in range(groups)], axis=1).astype(BF16)
        t = mm(x, at[...], 1, 1).astype(BF16)
        a_part = mm(u, x, 0, 0)
        ga_sum = a_part if ga_sum is None else ga_sum + a_part
        for g in range(groups):
            b_part = mm(t, d[g], 0, 0)
            gb_sum[g] = b_part if gb_sum[g] is None else gb_sum[g] + b_part
    for g in range(groups):
        rows = slice(g * share, (g + 1) * share)
        sv = s[g]
        sb = (b[g].astype(F32) * sv).astype(BF16)
        vg = v[g] if groups > 1 else v[...]
        back = mm(sb, vg, 1, 0 if turned else 1)
        ahead = mm(at[rows, :], vg, 1, 1 if turned else 0)
        ga[rows, :] = FACTOR * (ga_sum[rows, :] - back)
        gb[rows, :] = FACTOR * (gb_sum[g][rows, :] * c[...] - ahead * sv)


def rank_grads(xs, ds, at, b, v, s, turned=False, rows=None, scale=None):
    groups = b.shape[0]
    axis = 1 if groups > 1 else 0
    spans = []
    d_rows = used_rows(ds, rows) if rows else [d.shape[axis] for d in ds]
    xi = xa = di = da = 0
    while xi < len(xs):
        r = min(xs[xi].shape[0] - xa, d_rows[di] - da)
        spans.append((xi, xa, di, da, r))
        xa += r
        da += r
        if xa == xs[xi].shape[0]:
            xi, xa = xi + 1, 0
        if da == d_rows[di]:
            di, da = di + 1, 0
    total = sum(x.shape[0] for x in xs)
    rank, n_in = at.shape
    n_out = b.shape[2]
    return pl.pallas_call(
        functools.partial(rank_kernel, len(xs), len(ds), groups, turned, tuple(spans)),
        in_specs=[VM] * (len(xs) + len(ds) + 5),
        out_specs=[VM] * 2,
        out_shape=[
            jax.ShapeDtypeStruct((rank, n_in), F32),
            jax.ShapeDtypeStruct((rank, n_out), F32),
        ],
        compiler_params=params(),
        cost_estimate=cost(
            4 * total * (n_in + n_out * groups) * 256,
            2 * (total * (n_in + n_out * groups) + n_in * n_out * groups),
        ),
    )(*xs, *ds, at, b, v, s, jnp.ones((1, n_out), F32) if scale is None else scale)


def product_kernel(count, turned, spans, *refs):
    xs = refs[:count]
    w = refs[count]
    outs = refs[count + 1 :]
    for xi, oi, at, r in spans:
        outs[oi][at : at + r, :] = mm(xs[xi][...], w[...], 1, 1 if turned else 0).astype(BF16)


def used_rows(xs, tokens):
    rows = []
    left = tokens
    for x in xs:
        r = min(left, x.shape[0])
        rows.append(r)
        left -= r
        if left == 0:
            left = tokens
    return rows


def product(xs, w, turned, n_outs, steps, block=None, tokens=None):
    n = w.shape[0] if turned else w.shape[1]
    depth = w.shape[1] if turned else w.shape[0]
    tn = n // steps
    if block is not None:
        start, rows_in = block
        rows = [rows_in // n_outs] * n_outs
        x_specs = [
            pl.BlockSpec((r, depth), functools.partial(lambda k, i: (k, 0), start * n_outs + j))
            for j, r in enumerate(rows)
        ]
        xs = [xs] * n_outs
    else:
        rows = used_rows(xs, tokens) if tokens else [x.shape[0] for x in xs]
        x_specs = [pl.BlockSpec((r, depth), lambda i: (0, 0)) for r in rows]
    total = sum(rows)
    share = total // n_outs
    spans = []
    at = 0
    for xi, r in enumerate(rows):
        spans.append((xi, at // share, at % share, r))
        at += r
    w_spec = (
        pl.BlockSpec((tn, depth), lambda i: (i, 0))
        if turned
        else pl.BlockSpec((depth, tn), lambda i: (0, i))
    )
    return pl.pallas_call(
        functools.partial(product_kernel, len(xs), turned, tuple(spans)),
        grid=(steps,),
        in_specs=x_specs + [w_spec],
        out_specs=[pl.BlockSpec((share, tn), lambda i: (0, i))] * n_outs,
        out_shape=[jax.ShapeDtypeStruct((share, n), BF16)] * n_outs,
        compiler_params=params(),
        cost_estimate=cost(2 * total * n * depth, 2 * (n * depth + total * (n + depth))),
    )(*xs, w)


def down_kernel(rows, h, w, *refs):
    ds = refs[: len(rows)]
    own, other, dc = refs[len(rows) :]
    tokens = own.shape[0]
    total = jnp.zeros(dc.shape, F32)
    at = 0
    for d, r in zip(ds, rows):
        z = mm(h[at : at + r, :], w[...])
        total += jnp.sum(z * d[...].astype(F32), axis=0, keepdims=True)
        if at < tokens:
            own[at : at + r, :] = z.astype(BF16)
        else:
            other[at - tokens : at - tokens + r, :] = z.astype(BF16)
        at += r
    dc[...] = total


def down_product(h, w, ds):
    rows = [d.shape[0] for d in ds]
    total, depth = h.shape
    n = w.shape[1]
    tn = n // 2
    half = jax.ShapeDtypeStruct((total // 2, n), BF16)
    return pl.pallas_call(
        functools.partial(down_kernel, rows),
        grid=(2,),
        in_specs=[
            pl.BlockSpec((total, depth), lambda i: (0, 0)),
            pl.BlockSpec((depth, tn), lambda i: (0, i)),
        ]
        + [pl.BlockSpec((r, tn), lambda i: (0, i)) for r in rows],
        out_specs=[pl.BlockSpec((total // 2, tn), lambda i: (0, i))] * 2
        + [pl.BlockSpec((1, tn), lambda i: (0, i))],
        out_shape=[half, half, jax.ShapeDtypeStruct((1, n), F32)],
        compiler_params=params(),
        cost_estimate=cost(2 * total * n * depth, 2 * (n * depth + total * (2 * n + depth))),
    )(h, w, *ds)


def norm_forward(values):
    inverse = lax.rsqrt(jnp.mean(values * values, axis=-1, keepdims=True) + EPSILON)
    return values * inverse, inverse


def norm_backward(grad_normed, unit_vals, inverse, gain):
    scaled = grad_normed * gain
    return inverse * (scaled - unit_vals * jnp.mean(scaled * unit_vals, axis=-1, keepdims=True))


def after(value, *others):
    return lax.optimization_barrier((value,) + others)[0]


def on_device(
    sizes,
    layer_input,
    cotangent,
    segment_ids,
    token_valid,
    norm_attn,
    norm_mlp,
    base_qkv,
    base_attn_out,
    base_gate_up,
    base_down,
    rank_in_attn,
    rank_out_attn,
    magnitude_qkv,
    magnitude_out,
    rank_in_mlp,
    rank_out_mlp,
    magnitude_mlp,
    rank_in_down,
    rank_out_down,
    magnitude_down,
):
    X, C, ZH, ZL, Y = (sizes[a] for a in AXES)
    ix, ic, izh, izl, iy = (lax.axis_index(a) for a in AXES)
    dp, mp = X * C, ZH * ZL * Y
    n_dev = dp * mp
    tokens, model = layer_input.shape
    seq_len = segment_ids.shape[0]
    width = base_qkv.shape[2]
    hidden = base_gate_up.shape[2]
    heads = width // HD
    a_w = rank_in_attn.shape[1]
    f_w = rank_in_down.shape[0]
    used = 11 * a_w + 3 * f_w
    packed_w = -(-used // 128) * 128
    bq = min(512, seq_len)
    stay = ic == izh

    def from_offset(a, axis, k):
        n = sizes[axis]
        return lax.ppermute(a, axis, [(s, (s - k) % n) for s in range(n)])

    def to_offset(a, axis, k):
        n = sizes[axis]
        return lax.ppermute(a, axis, [(s, (s + k) % n) for s in range(n)])

    def mate(a):
        return from_offset(a, "c", 1)

    offsets = [(dz, dy) for dz in range(ZL) for dy in range(Y)]
    n_chips = len(offsets)

    def chips(a, off, sign):
        dz, dy = off
        perm = []
        for z in range(ZL):
            for y in range(Y):
                perm.append((z * Y + y, (z + sign * dz) % ZL * Y + (y + sign * dy) % Y))
        return lax.ppermute(a, ("zl", "y"), perm)

    def swap_rows(a):
        return lax.ppermute(a, ("c", "zh"), [(1, 2), (2, 1)])

    last = [None]

    def seq(x):
        return x if last[0] is None else after(x, last[0])

    def mark(x):
        last[0] = x
        return x

    relayed = ZL == 2 and Y == 2

    def gather_start(a):
        if relayed:
            return [[a, mate(a)], [chips(a, (0, 1), -1)], [chips(a, (1, 0), -1)]]
        return [[a, mate(a)]] + [[chips(a, o, -1)] for o in offsets[1:]]

    def gather_next(got):
        py, pz = seq(got[1][0]), seq(got[-1][0])
        if relayed:
            half = tokens // 2
            d0 = chips(pz[:half], (0, 1), -1)
            d1 = chips(py[half:], (1, 0), -1)
            return [got[0], [py, mate(py)], [pz, mate(pz)], [d0, d1]]
        return [got[0]] + [[g[0], mate(seq(g[0]))] for g in got[1:]]

    def gather_last(got):
        if relayed:
            d0, d1 = seq(got[3][0]), seq(got[3][1])
            return got[:3] + [[d0, d1, mate(d0), mate(d1)]]
        return got

    def block_of(own, other, wide=False):
        block = own.astype(F32) + mate(other).astype(F32)
        return block if wide else block.astype(BF16)

    def scatter_end(own, arrived):
        for a in arrived:
            own = own + a.astype(F32)
        return own

    def product_blocks(make, between=None):
        parts = [None] * n_chips
        for o in range(n_chips)[::-1]:
            parts[o] = make(o)
            mark(parts[o][0])
        blocks = [None] * n_chips
        if between is not None:
            blocks.append(between())
        here = last[0]

        def gated(x):
            return x if between is None else after(x, here)

        for o in range(n_chips)[::-1]:
            own, other = parts[o]
            blocks[o] = mark(block_of(seq(own), gated(other), wide=o == 0))
        return blocks

    def send_blocks(blocks):
        return [chips(blocks[o], offsets[o], 1) for o in range(1, n_chips)[::-1]]

    def square_sum(a):
        total = a
        for axis in ("c", "zl", "y"):
            total = sum((from_offset(total, axis, k) for k in range(1, sizes[axis])), total)
        return total

    place = np.zeros((n_dev, 2 * n_dev + 4 + 2 * n_chips), np.int32)
    for own in range(n_dev):
        x, c, zh, zl, y = np.unravel_index(own, (X, C, ZH, ZL, Y))
        xs, cs, zhs, zls, ys = np.unravel_index(np.arange(n_dev), (X, C, ZH, ZL, Y))
        order = (cs - c) % C
        order = order * X + (xs - x) % X
        order = order * Y + (ys - y) % Y
        order = order * ZL + (zls - zl) % ZL
        order = order * ZH + (zhs - zh) % ZH
        send = ((((cs - c) % C * X + xs) * ZH + zhs) * ZL + zls) * Y + ys
        blocks = [
            ((c + k) % 2 * ZL + (zl + dz) % ZL) * Y + (y + dy) % Y
            for dz, dy in offsets
            for k in range(2)
        ]
        place[own, :n_dev] = order
        place[own, n_dev : n_dev + 2] = (c * ZL + zl) * Y + y, (zh * ZL + zl) * Y + y
        place[own, n_dev + 2 : n_dev + 4] = int(c == zh), x
        place[own, n_dev + 4 : n_dev + 4 + 2 * n_chips] = blocks
        place[own, n_dev + 4 + 2 * n_chips :] = send
    own_id = (((ix * C + ic) * ZH + izh) * ZL + izl) * Y + iy
    row = lax.dynamic_slice_in_dim(jnp.asarray(place), own_id, 1, 0)[0]
    table = row[: n_dev + 2]
    flags = row[n_dev + 2 : n_dev + 4]
    blk = row[n_dev + 4 : n_dev + 4 + 2 * n_chips]
    send_table = jnp.concatenate([row[n_dev + 4 + 2 * n_chips :], row[n_dev : n_dev + 2]])

    def sds(shape, dtype=BF16):
        return jax.ShapeDtypeStruct(shape, dtype)

    packed = pl.pallas_call(
        functools.partial(pack_kernel, a_w, f_w),
        in_specs=[VM] * 10,
        out_specs=VM,
        out_shape=sds((1, R + 1, packed_w)),
    )(
        jnp.swapaxes(rank_in_attn, 1, 2),
        rank_out_attn,
        magnitude_qkv,
        magnitude_out[None],
        jnp.swapaxes(rank_in_mlp, 1, 2),
        rank_out_mlp,
        magnitude_mlp,
        rank_in_down.T[None],
        rank_out_down[None],
        magnitude_down[None],
    )
    def over_z(a):
        found = []
        for k in range(1, ZL * ZH):
            dl, dh = divmod(k, ZH)
            perm = []
            for zh in range(ZH):
                for zl in range(ZL):
                    perm.append((zh * ZL + zl, (zh - dh) % ZH * ZL + (zl - dl) % ZL))
            found.append(lax.ppermute(a, ("zh", "zl"), perm))
        return found

    gathered = jnp.concatenate([packed] + over_z(packed), axis=0)
    moved_input = swap_rows(after(layer_input, packed))
    for axis in ("y", "x", "c"):
        gathered = jnp.concatenate(
            [gathered] + [from_offset(gathered, axis, k) for k in range(1, sizes[axis])], axis=0
        )
    mark(gathered)

    def cut(w, axis, member=None):
        part = w.shape[axis] // X
        start = [0] * w.ndim
        size = list(w.shape)
        start[axis] = ix * part
        size[axis] = part
        if member is not None:
            start[0], size[0] = member, 1
        return lax.dynamic_slice(w, start, size)

    def fetch(mine, *gate):
        mine = after(mine, *gate) if gate else mine
        return lax.ppermute(mine, ("c", "zh"), [(0, 1), (3, 2)])

    def fetch_rest(mine):
        mine = seq(mine)
        parts = [mine]
        for k in range(1, X):
            perm = []
            for x in range(X):
                for cz in (1, 2):
                    perm.append((x * 4 + cz, (x - k) % X * 4 + cz))
            parts.append(lax.ppermute(mine, ("x", "c", "zh"), perm))
        return parts

    turned_gu = jnp.swapaxes(base_gate_up, 1, 2)
    mine_qkv = fetch(cut(base_qkv, 1))
    cuts = [
        cut(base_attn_out, 1),
        cut(turned_gu, 2, 0),
        cut(turned_gu, 2, 1),
        cut(base_down, 1),
    ]
    local_input = jnp.where(stay, layer_input, seq(moved_input))
    gain_one = norm_attn.astype(F32)
    gain_two = norm_mlp.astype(F32)
    input_full = local_input.astype(F32)
    unit_one, inverse_one = norm_forward(input_full)
    normed_one = mark((unit_one * gain_one).astype(BF16))
    one = gather_start(normed_one)

    gathered = after(gathered, *cuts)

    (
        at_qkv, at_gu, at_o, at_d, at_o0, at_d0, b_qkv, b_blocks, b_gu, b_o, b_d, mags_qkv, m_o, m_gu, m_d,
    ) = pl.pallas_call(
        functools.partial(unpack_kernel, a_w, f_w, dp),
        in_specs=[SM, VM],
        out_specs=[VM] * 15,
        out_shape=[
            sds((3 * R, model)),
            sds((2, R, model)),
            sds((R, width)),
            sds((R, hidden)),
            sds((R, width)),
            sds((R, hidden)),
            sds((3, R, width)),
            sds((3 * R, 3 * width)),
            sds((2, R, hidden)),
            sds((R, model)),
            sds((R, model)),
            sds((1, 3 * width), F32),
            sds((1, model), F32),
            sds((2, 1, hidden), F32),
            sds((1, model), F32),
        ],
    )(table, seq(gathered))
    mark(at_qkv)

    rows_here = jnp.stack([segment_ids, token_valid])
    rows_here = jnp.where(stay, rows_here, mate(rows_here))
    segments, valid = rows_here[0], rows_here[1]
    steps = jnp.arange(seq_len, dtype=jnp.int32)
    earlier = jnp.concatenate([segments[:1] - 1, segments[:-1]])
    first = lax.cummax(jnp.where(segments != earlier, steps, 0), axis=0)
    low = first[None]
    positions = seq(steps - first)
    frequency = ROPE_BASE ** (-(2.0 * jnp.arange(HD // 2, dtype=F32)) / HD)
    sign = jnp.concatenate([-jnp.ones(HD // 2, F32), jnp.ones(HD // 2, F32)])
    angle = positions.astype(F32)[:, None] * jnp.concatenate([frequency, frequency])[None, :]
    cos, sin = jnp.cos(angle), jnp.sin(angle) * sign[None, :]
    info = jnp.concatenate([blk, jnp.sum(valid)[None].astype(jnp.int32), first[::bq] // bq])
    mark(cos)

    def rows_square(base, at0, b):
        v = base.astype(F32) + FACTOR * mm(at0, b, 0, 0)
        return jnp.sum(v * v, axis=0)

    squares = jnp.stack(
        [rows_square(base_attn_out, seq(at_o0), b_o), rows_square(base_down, seq(at_d0), b_d)]
    )
    mark(squares)

    def add_over(a, axis):
        return sum((from_offset(a, axis, k) for k in range(1, sizes[axis])), a)

    one = gather_next(one)
    column = over_z(squares)
    parts_qkv = fetch_rest(mine_qkv)
    mine_o = fetch(cuts[0], parts_qkv[0])
    moved_cot = swap_rows(after(cotangent, parts_qkv[0]))
    one = gather_last(one)
    mine_gate = fetch(cuts[1], one[-1][0])
    v_qkv, square_qkv = merge_qkv(flags, base_qkv, parts_qkv, seq(at_qkv), b_qkv)
    mark(square_qkv)
    norms_qkv = jnp.sqrt(square_qkv)
    scale_qkv = mark(mags_qkv / norms_qkv)

    qkv = []
    for o in range(n_chips):
        qkv.append(mark(qkv_chunk(blk, o, one[o], v_qkv, seq(scale_qkv), cos, sin)))
        if o == 0:
            squares = add_over(sum(column, seq(squares)), "y")
    mark(squares)
    local_cot = mark(jnp.where(stay, cotangent, seq(moved_cot)))
    grad_output = local_cot.astype(F32)
    parts_o = fetch_rest(mine_o)
    rest_gate = fetch_rest(mine_gate)
    down = [[local_cot, mate(local_cot)]] + [[chips(local_cot, o, -1)] for o in offsets[1 : Y + 1]]
    mine_up = fetch(cuts[2], local_cot)
    qkv_abs, att_abs, att_slot, lse = attn_fwd(info, qkv, seq(low), tokens, bq)
    mark(lse)
    for i in range(1, Y + 1):
        down[i] = [mark(seq(down[i][0]))]
    v_o = mark(merge_rows(flags, base_attn_out, parts_o, seq(at_o), b_o))
    rest_up = fetch_rest(mine_up)
    blocks = product_blocks(
        lambda o: product(att_slot, seq(v_o), False, 2, 2, block=(o, 2 * tokens))
    )
    arrived = send_blocks(blocks)
    down += [[chips(seq(down[Y][0]), o, -1)] for o in offsets[1:Y]]
    down[1:] = [[p[0], mate(seq(p[0]))] for p in down[1 : Y + 1]] + down[Y + 1 :]
    mine_d = fetch(cuts[3], blocks[1])
    v_gu, square_gu = merge_gu(flags, turned_gu, rest_gate, rest_up, seq(at_gu), b_gu)
    norms_gu = jnp.sqrt(square_gu)
    scale_gu = mark(m_gu / norms_gu)
    norms_rows = jnp.sqrt(squares)
    norms_o, norms_d = norms_rows[0:1], norms_rows[1:2]
    scale_o = m_o / norms_o
    scale_d = m_d / norms_d
    summed_out = scatter_end(seq(blocks[0]), arrived)
    residual = input_full + summed_out * scale_o
    unit_two, inverse_two = norm_forward(residual)
    normed_two = mark((unit_two * gain_two).astype(BF16))
    two = gather_start(normed_two)

    parts_d = fetch_rest(mine_d)
    for i in range(Y + 1, n_chips):
        down[i].append(mate(seq(down[i][0])))
    v_d, v_ds = merge_down(flags, base_down, parts_d, seq(at_d), b_d, scale_d)
    mark(v_d)
    dhid = []
    for o in range(n_chips):
        dhid.append(mark(product(down[o], seq(v_ds), True, 1, 1)[0]))
    two = gather_next(two)

    hid, dz_gu, parts, dc_gu = [], [], [], 0.0
    blocks = [None] * n_chips
    for o in range(n_chips):
        if o == n_chips - 1:
            two = gather_last(two)
        h, dz, own, other, dc = mlp_chunk(two[o], dhid[o], v_gu, seq(scale_gu))
        mark(h)
        hid.append(h)
        dz_gu.append(dz)
        parts.append((own, other))
        dc_gu = dc_gu + dc
    blocks = [None] * n_chips
    for o in list(range(1, n_chips)) + [0]:
        blocks[o] = mark(block_of(seq(parts[o][0]), parts[o][1], wide=o == 0))
    arrived = send_blocks(blocks)
    down_parts = []
    dc_down = 0.0
    for o in range(n_chips):
        own, other, dc = down_product(hid[o], seq(v_d), down[o])
        mark(dc)
        dc_down = dc_down + dc
        down_parts.append((own, other))
    def shrink(col, mags, norms):
        return col * mags / (norms * norms * norms)

    def flat(lists):
        return [p for pieces in lists for p in pieces]

    ga_gu, gb_gu = rank_grads(
        flat(two),
        dz_gu,
        seq(at_gu).reshape(2 * R, model),
        b_gu,
        v_gu,
        shrink(dc_gu, m_gu, norms_gu),
        turned=True,
    )
    mark(ga_gu)
    grad_normed_two = scatter_end(seq(blocks[0]), arrived)
    grad_residual = grad_output + norm_backward(grad_normed_two, unit_two, inverse_two, gain_two)
    col_out = jnp.sum(grad_residual * summed_out, axis=0, keepdims=True)
    extra = jnp.concatenate([col_out, dc_down, jnp.zeros((14, model), F32)], axis=0)
    low_out = mark(
        jnp.concatenate([(grad_residual * scale_o).astype(BF16), extra.astype(BF16)], axis=0)
    )
    out = gather_start(low_out)

    down_blocks = [block_of(seq(p[0]), p[1], wide=o == 0) for o, p in enumerate(down_parts)]
    mark(down_blocks[-1])
    out = gather_next(out)

    def tails(lists):
        found = []
        for pieces in lists:
            n = len(pieces) // 2
            found += [pieces[n - 1][-16:], pieces[-1][-16:]]
        return found

    do_chunks = []
    for o in range(n_chips):
        if o == n_chips - 1:
            out = gather_last(out)
        do_chunks.append(mark(product(out[o], seq(v_o), True, 1, 1, tokens=tokens)[0]))
    cols = sum(p[:2].astype(F32) for p in tails(out))
    arrived_down = send_blocks([seq(b) for b in down_blocks])
    dz_qkv, dc_qkv = attn_bwd(
        info, qkv_abs, do_chunks, att_abs, lse, seq(low), cos, sin, scale_qkv, tokens, bq
    )
    mark(dc_qkv)
    blocks = product_blocks(
        lambda o: product(dz_qkv, seq(v_qkv), True, 2, 2, block=(o, 2 * tokens)),
        lambda: mark(
            (residual + scatter_end(seq(down_blocks[0]), arrived_down) * scale_d).astype(BF16)
        ),
    )
    output_here = blocks.pop()
    moved_output = swap_rows(output_here)
    arrived = send_blocks(blocks)

    ga_qkv, gb_all = rank_grads(
        flat(one),
        [dz_qkv],
        seq(at_qkv),
        b_blocks[None],
        v_qkv,
        shrink(dc_qkv, mags_qkv, norms_qkv)[None],
    )
    mark(ga_qkv)
    ga_o, gb_o = rank_grads(
        [att_slot],
        flat(out),
        seq(at_o),
        b_o[None],
        v_o,
        shrink(cols[0:1], m_o, norms_o)[None],
        rows=tokens,
    )
    mark(ga_o)
    ga_d, gb_d = rank_grads(
        hid,
        flat(down),
        seq(at_d),
        b_d[None],
        v_d,
        shrink(cols[1:2], m_d, norms_d)[None],
        scale=scale_d,
    )
    mark(ga_d)
    mag_full = jnp.concatenate([col_out / norms_o, dc_down / norms_d], axis=0)
    grads = pl.pallas_call(
        functools.partial(pack_grads_kernel, a_w, f_w, dp),
        in_specs=[SM] + [VM] * 11,
        out_specs=VM,
        out_shape=sds((n_dev, R + 1, packed_w)),
    )(
        send_table,
        seq(ga_qkv),
        ga_gu,
        gb_o,
        gb_d,
        mag_full,
        ga_o,
        ga_d,
        gb_all,
        gb_gu,
        dc_qkv / norms_qkv,
        dc_gu / norms_gu,
    )
    mark(grads)
    layer_output = mark(jnp.where(stay, output_here, seq(moved_output)))
    grad_normed_one = scatter_end(seq(blocks[0]), arrived)
    grad_here = grad_residual + norm_backward(grad_normed_one, unit_one, inverse_one, gain_one)
    low_here = mark(grad_here.astype(BF16))
    input_grad = jnp.where(stay, grad_here, swap_rows(low_here).astype(F32))
    half = n_dev // 2
    grads = seq(grads)
    grads = grads[:half].astype(F32) + mate(grads[half:]).astype(F32)
    pieces = lax.all_to_all(
        grads.astype(BF16), ("x", "zh", "zl", "y"), split_axis=0, concat_axis=0, tiled=True
    )
    grads = jnp.sum(pieces.astype(F32), axis=0, keepdims=True)
    a1, b1, mq, mo, a2, b2, mm_, a3, b3, md = pl.pallas_call(
        functools.partial(unpack_grads_kernel, a_w, f_w),
        in_specs=[VM],
        out_specs=[VM] * 10,
        out_shape=[
            sds((4, R, a_w), F32),
            sds((4, R, a_w), F32),
            sds((3, a_w), F32),
            sds((1, a_w), F32),
            sds((2, R, a_w), F32),
            sds((2, R, f_w), F32),
            sds((2, f_w), F32),
            sds((1, R, f_w), F32),
            sds((1, R, a_w), F32),
            sds((1, a_w), F32),
        ],
    )(grads)
    return (
        layer_output,
        input_grad,
        jnp.swapaxes(a1, 1, 2),
        b1,
        mq,
        mo[0],
        jnp.swapaxes(a2, 1, 2),
        b2,
        mm_,
        a3[0].T,
        b3[0],
        md[0],
    )


def solution(mesh):
    dp, mp = mesh.shape["dp"], mesh.shape["mp"]
    shape = (dp // 2, 2, 2, 2, mp // 4)
    fine = Mesh(mesh.devices.reshape(shape), AXES)
    rows, cols = ("x", "c"), ("zh", "zl", "y")
    both = rows + cols
    return jax.shard_map(
        functools.partial(on_device, dict(zip(AXES, shape))),
        mesh=fine,
        in_specs=(
            P(both, None),
            P(both, None),
            P(rows),
            P(rows),
            P(),
            P(),
            P(None, None, cols),
            P(cols, None),
            P(None, None, cols),
            P(cols, None),
            P(None, both, None),
            P(None, None, both),
            P(None, both),
            P(both),
            P(None, both, None),
            P(None, None, both),
            P(None, both),
            P(both, None),
            P(None, both),
            P(both),
        ),
        out_specs=(
            P(both, None),
            P(both, None),
            P(None, both, None),
            P(None, None, both),
            P(None, both),
            P(both),
            P(None, both, None),
            P(None, None, both),
            P(None, both),
            P(both, None),
            P(None, both),
            P(both),
        ),
        check_vma=False,
    )
```

```python
import functools

import jax
import jax.numpy as jnp
import numpy as np
from jax import lax
from jax.experimental import pallas as pl
from jax.experimental.pallas import tpu as pltpu
from jax.sharding import Mesh
from jax.sharding import PartitionSpec as P

HD = 128
R = 16
ALPHA = 32
FACTOR = ALPHA / R
EPSILON = 1e-05
ROPE_BASE = 10000.0
BF16 = jnp.bfloat16
F32 = jnp.float32
NEG = -1e30
LOG2E = 1.4426950408889634
AXES = ("x", "c", "zh", "zl", "y")
VM = pl.BlockSpec(memory_space=pltpu.VMEM)
SM = pl.BlockSpec(memory_space=pltpu.SMEM)


def mm(left, right, lc=1, rc=0, precision=None):
    return lax.dot_general(
        left,
        right,
        (((lc,), (rc,)), ((), ())),
        preferred_element_type=F32,
        precision=precision,
    )


def params(mib=18):
    return pltpu.CompilerParams(vmem_limit_bytes=mib * 1024 * 1024)


def cost(flops, nbytes, trans=0, scale=10**6):
    return pl.CostEstimate(
        flops=int(flops) // scale,
        bytes_accessed=int(nbytes) // scale,
        transcendentals=int(trans) // scale,
    )


class Shift:
    def __init__(self, ref, at):
        self.ref, self.at = ref, at

    def __getitem__(self, i):
        return self.ref[self.at + i]


def pack_kernel(a_w, f_w, a1, b1, mq, mo, a2, b2, mm_, a3, b3, md, out):
    out[...] = jnp.zeros(out.shape, out.dtype)
    at = 0
    for ref, count, w in ((a1, 4, a_w), (a2, 2, a_w), (a3, 1, f_w), (b1, 4, a_w), (b2, 2, f_w), (b3, 1, a_w)):
        for p in range(count):
            out[0, :R, at : at + w] = ref[p].astype(BF16)
            at += w
    at = 0
    for ref, count, w in ((mq, 3, a_w), (mo, 1, a_w), (mm_, 2, f_w), (md, 1, a_w)):
        for p in range(count):
            out[0, R : R + 1, at : at + w] = ref[p : p + 1, :].astype(BF16)
            at += w


def unpack_grads_kernel(a_w, f_w, g, a1, b1, mq, mo, a2, b2, mm_, a3, b3, md):
    at = 0
    for ref, count, w in ((a1, 4, a_w), (a2, 2, a_w), (a3, 1, f_w), (b1, 4, a_w), (b2, 2, f_w), (b3, 1, a_w)):
        for p in range(count):
            ref[p] = g[0, :R, at : at + w]
            at += w
    at = 0
    for ref, count, w in ((mq, 3, a_w), (mo, 1, a_w), (mm_, 2, f_w), (md, 1, a_w)):
        for p in range(count):
            ref[p : p + 1, :] = g[0, R : R + 1, at : at + w]
            at += w


def unpack_kernel(
    a_w, f_w, dp, table, g, at_qkv, at_gu, at_o, at_d, at_o0, at_d0,
    b_qkv, b_blocks, b_gu, b_o, b_d, m_qkv, m_o, m_gu, m_d,
):
    b_blocks[...] = jnp.zeros(b_blocks.shape, b_blocks.dtype)
    n = g.shape[0]
    order, where_ = Shift(table, 0), Shift(table, n)
    b_at = 6 * a_w + f_w
    for d in range(n):
        s = order[d]
        lo, hi = d * a_w, (d + 1) * a_w
        for p in range(3):
            at_qkv[p * R : (p + 1) * R, lo:hi] = g[s, :R, p * a_w : (p + 1) * a_w]
        for p in range(2):
            at_gu[p, :, lo:hi] = g[s, :R, (4 + p) * a_w : (5 + p) * a_w]
        b_o[:, lo:hi] = g[s, :R, b_at + 3 * a_w : b_at + 4 * a_w]
        end = b_at + 4 * a_w + 2 * f_w
        b_d[:, lo:hi] = g[s, :R, end : end + a_w]
        m_o[:, lo:hi] = g[s, R : R + 1, 3 * a_w : 4 * a_w].astype(F32)
        end = 4 * a_w + 2 * f_w
        m_d[:, lo:hi] = g[s, R : R + 1, end : end + a_w].astype(F32)
    for i in range(dp):
        s = order[where_[0] * dp + i]
        lo, hi = i * a_w, (i + 1) * a_w
        flo, fhi = i * f_w, (i + 1) * f_w
        at_o[:, lo:hi] = g[s, :R, 3 * a_w : 4 * a_w]
        at_d[:, flo:fhi] = g[s, :R, 6 * a_w : 6 * a_w + f_w]
        for p in range(3):
            b_qkv[p, :, lo:hi] = g[s, :R, b_at + p * a_w : b_at + (p + 1) * a_w]
            for h, at in pieces_of(lo, hi):
                head, inner = divmod(h, HD)
                to = (head * 3 + p) * HD + inner
                w = at[1] - at[0]
                src = p * a_w + at[0]
                b_blocks[p * R : (p + 1) * R, to : to + w] = g[s, :R, b_at + src : b_at + src + w]
                m_qkv[:, to : to + w] = g[s, R : R + 1, src : src + w].astype(F32)
        for p in range(2):
            e = b_at + 4 * a_w + p * f_w
            b_gu[p, :, flo:fhi] = g[s, :R, e : e + f_w]
            e = 4 * a_w + p * f_w
            m_gu[p, :, flo:fhi] = g[s, R : R + 1, e : e + f_w].astype(F32)
        s = order[where_[1] * dp + i]
        at_o0[:, lo:hi] = g[s, :R, 3 * a_w : 4 * a_w]
        at_d0[:, flo:fhi] = g[s, :R, 6 * a_w : 6 * a_w + f_w]


def pieces_of(lo, hi):
    found = []
    at = lo
    while at < hi:
        end = min(hi, (at // HD + 1) * HD)
        found.append((at, (at - lo, end - lo)))
        at = end
    return found


def pack_grads_kernel(
    a_w, f_w, dp, table, ga_qkv, ga_gu, gb_o, gb_d, m_full, ga_attn, ga_d, gb_all, gb_gu,
    m_qkv, m_gu, out
):
    n = out.shape[0]
    order, where_ = Shift(table, 0), Shift(table, n)
    heads = m_qkv.shape[1] // (3 * HD)
    out[...] = jnp.zeros(out.shape, out.dtype)
    b_at = 6 * a_w + f_w
    dt = out.dtype
    for d in range(n):
        s = order[d]
        lo, hi = d * a_w, (d + 1) * a_w
        for p in range(3):
            out[s, :R, p * a_w : (p + 1) * a_w] = ga_qkv[p * R : (p + 1) * R, lo:hi].astype(dt)
        for p in range(2):
            e = (4 + p) * a_w
            out[s, :R, e : e + a_w] = ga_gu[p * R : (p + 1) * R, lo:hi].astype(dt)
        out[s, :R, b_at + 3 * a_w : b_at + 4 * a_w] = gb_o[:, lo:hi].astype(dt)
        end = b_at + 4 * a_w + 2 * f_w
        out[s, :R, end : end + a_w] = gb_d[:, lo:hi].astype(dt)
        out[s, R : R + 1, 3 * a_w : 4 * a_w] = m_full[0:1, lo:hi].astype(dt)
        end = 4 * a_w + 2 * f_w
        out[s, R : R + 1, end : end + a_w] = m_full[1:2, lo:hi].astype(dt)
    for i in range(dp):
        s = order[where_[0] * dp + i]
        lo, hi = i * a_w, (i + 1) * a_w
        flo, fhi = i * f_w, (i + 1) * f_w
        out[s, :R, 3 * a_w : 4 * a_w] = ga_attn[:, lo:hi].astype(dt)
        out[s, :R, 6 * a_w : 6 * a_w + f_w] = ga_d[:, flo:fhi].astype(dt)
        for p in range(3):
            for h, at in pieces_of(lo, hi):
                head, inner = divmod(h, HD)
                src = (head * 3 + p) * HD + inner
                w = at[1] - at[0]
                to = p * a_w + at[0]
                out[s, :R, b_at + to : b_at + to + w] = gb_all[p * R : (p + 1) * R, src : src + w].astype(dt)
                out[s, R : R + 1, to : to + w] = m_qkv[:, src : src + w].astype(dt)
        for p in range(2):
            e = b_at + 4 * a_w + p * f_w
            out[s, :R, e : e + f_w] = gb_gu[p * R : (p + 1) * R, flo:fhi].astype(dt)
            e = 4 * a_w + p * f_w
            out[s, R : R + 1, e : e + f_w] = m_gu[p, :, flo:fhi].astype(dt)


def pick(flags, t, own, parts):
    n = len(parts)
    k = lax.rem(t - flags[1] + n, n)
    w = parts[0]
    for i in range(1, n):
        w = jnp.where(k == i, parts[i], w)
    return jnp.where(flags[0] == 1, own, w)


def own_block(t, f):
    return t * f[0]


def merge_qkv_kernel(n, flags, own, *refs):
    parts = refs[:n]
    at, b, vb, ssq = refs[n:]
    t = pl.program_id(0)

    @pl.when(t == 0)
    def _():
        ssq[...] = jnp.zeros_like(ssq)

    members, _, width = own.shape
    for p in range(members):
        w = pick(flags, t, own[p], [r[p] for r in parts])
        v = w.astype(F32) + FACTOR * mm(at[p * R : (p + 1) * R, :], b[p], 0, 0)
        total = jnp.sum(v * v, axis=0, keepdims=True)
        vb16 = v.astype(BF16)
        for h in range(width // HD):
            to = slice((h * members + p) * HD, (h * members + p + 1) * HD)
            vb[:, to] = vb16[:, h * HD : (h + 1) * HD]
            ssq[:, to] += total[:, h * HD : (h + 1) * HD]


def merge_qkv(flags, own, parts, at_qkv, b_qkv):
    members, rows, width = own.shape
    n = len(parts)
    part_rows = rows // n
    block = (members, part_rows, width)
    return pl.pallas_call(
        functools.partial(merge_qkv_kernel, n),
        grid_spec=pltpu.PrefetchScalarGridSpec(
            num_scalar_prefetch=1,
            grid=(n,),
            in_specs=[pl.BlockSpec(block, lambda t, f: (0, own_block(t, f), 0))]
            + [pl.BlockSpec(block, lambda t, f: (0, 0, 0))] * n
            + [
                pl.BlockSpec((members * R, part_rows), lambda t, f: (0, t)),
                pl.BlockSpec((members, R, width), lambda t, f: (0, 0, 0)),
            ],
            out_specs=[
                pl.BlockSpec((part_rows, members * width), lambda t, f: (t, 0)),
                pl.BlockSpec((1, members * width), lambda t, f: (0, 0)),
            ],
        ),
        out_shape=[
            jax.ShapeDtypeStruct((rows, members * width), BF16),
            jax.ShapeDtypeStruct((1, members * width), F32),
        ],
        compiler_params=params(),
        cost_estimate=cost(2 * rows * width * members * 256, 4 * members * rows * width * 2),
    )(flags, own, *parts, at_qkv, b_qkv)


def merge_gu_kernel(n, flags, own, *refs):
    gates, ups = refs[:n], refs[n : 2 * n]
    at, b, vb, ssq, acc = refs[2 * n :]
    t = pl.program_id(1)
    first = pl.program_id(0) == 0
    w = pick(flags, t, own[0], [jnp.where(first, g[0], u[0]) for g, u in zip(gates, ups)])
    v = w.astype(F32) + FACTOR * mm(b[0], at[0], 0, 0)
    vb[0] = v.astype(BF16)
    sq = v * v
    lanes = sq[:, :HD]
    for i in range(1, sq.shape[1] // HD):
        lanes = lanes + sq[:, i * HD : (i + 1) * HD]

    @pl.when(t == 0)
    def _():
        acc[...] = lanes

    @pl.when(t > 0)
    def _():
        acc[...] += lanes

    @pl.when(t == pl.num_programs(1) - 1)
    def _():
        ssq[0] = mm(jnp.ones((8, HD), F32), acc[...], 1, 1, lax.Precision.HIGHEST)[:1]


def merge_gu(flags, own, gates, ups, at_gu, b_gu):
    members, width, rows = own.shape
    n = len(gates)
    part_rows = rows // n
    block = (1, width, part_rows)
    return pl.pallas_call(
        functools.partial(merge_gu_kernel, n),
        grid_spec=pltpu.PrefetchScalarGridSpec(
            num_scalar_prefetch=1,
            grid=(members, n),
            in_specs=[pl.BlockSpec(block, lambda p, t, f: (p * f[0], 0, own_block(t, f)))]
            + [pl.BlockSpec(block, lambda p, t, f: (0, 0, 0))] * (2 * n)
            + [
                pl.BlockSpec((1, R, part_rows), lambda p, t, f: (p, 0, t)),
                pl.BlockSpec((1, R, width), lambda p, t, f: (p, 0, 0)),
            ],
            out_specs=[
                pl.BlockSpec(block, lambda p, t, f: (p, 0, t)),
                pl.BlockSpec((1, 1, width), lambda p, t, f: (p, 0, 0)),
            ],
            scratch_shapes=[pltpu.VMEM((width, HD), F32)],
        ),
        out_shape=[
            jax.ShapeDtypeStruct((members, width, rows), BF16),
            jax.ShapeDtypeStruct((members, 1, width), F32),
        ],
        compiler_params=params(),
        cost_estimate=cost(2 * rows * width * members * 256, 4 * members * rows * width * 2),
    )(flags, own, *gates, *ups, at_gu, b_gu)


def merge_rows_kernel(n, flags, own, *refs):
    parts = refs[:n]
    at, b, vb = refs[n:]
    w = pick(flags, pl.program_id(0), own[...], [r[...] for r in parts])
    v = w.astype(F32) + FACTOR * mm(at[...], b[...], 0, 0)
    vb[...] = v.astype(BF16)


def merge_rows(flags, own, parts, at, b):
    rows, width = own.shape
    xs = len(parts)
    part = width // xs
    return pl.pallas_call(
        functools.partial(merge_rows_kernel, xs),
        grid_spec=pltpu.PrefetchScalarGridSpec(
            num_scalar_prefetch=1,
            grid=(xs,),
            in_specs=[pl.BlockSpec((rows, part), lambda t, f: (0, own_block(t, f)))]
            + [pl.BlockSpec((rows, part), lambda t, f: (0, 0))] * xs
            + [
                pl.BlockSpec((R, rows), lambda t, f: (0, 0)),
                pl.BlockSpec((R, part), lambda t, f: (0, t)),
            ],
            out_specs=pl.BlockSpec((rows, part), lambda t, f: (0, t)),
        ),
        out_shape=jax.ShapeDtypeStruct((rows, width), BF16),
        compiler_params=params(),
        cost_estimate=cost(2 * rows * width * 256, 4 * rows * width * 2),
    )(flags, own, *parts, at, b)


def merge_down_kernel(n, flags, own, *refs):
    parts = refs[:n]
    at, b, scale, vb, vs = refs[n:]
    w = pick(flags, pl.program_id(0), own[...], [r[...] for r in parts])
    v = (w.astype(F32) + FACTOR * mm(at[...], b[...], 0, 0)).astype(BF16)
    vb[...] = v
    vs[...] = (v.astype(F32) * scale[...]).astype(BF16)


def merge_down(flags, own, parts, at, b, scale):
    rows, width = own.shape
    n = len(parts)
    part = width // n
    return pl.pallas_call(
        functools.partial(merge_down_kernel, n),
        grid_spec=pltpu.PrefetchScalarGridSpec(
            num_scalar_prefetch=1,
            grid=(n,),
            in_specs=[pl.BlockSpec((rows, part), lambda t, f: (0, own_block(t, f)))]
            + [pl.BlockSpec((rows, part), lambda t, f: (0, 0))] * n
            + [
                pl.BlockSpec((R, rows), lambda t, f: (0, 0)),
                pl.BlockSpec((R, part), lambda t, f: (0, t)),
                pl.BlockSpec((1, part), lambda t, f: (0, t)),
            ],
            out_specs=[pl.BlockSpec((rows, part), lambda t, f: (0, t))] * 2,
        ),
        out_shape=[jax.ShapeDtypeStruct((rows, width), BF16)] * 2,
        compiler_params=params(),
        cost_estimate=cost(2 * rows * width * 256, 5 * rows * width * 2),
    )(flags, own, *parts, at, b, scale)


def qkv_kernel(rows, blk, *refs):
    count = len(rows)
    xs = refs[:count]
    w, scale, cos0, cos1, sin0, sin1, out = refs[count:]
    cos = jnp.concatenate([cos0[...], cos1[...]], axis=0)
    sin = jnp.concatenate([sin0[...], sin1[...]], axis=0)
    at = 0
    for x, r in zip(xs, rows):
        z = mm(x[...], w[...]) * scale[...]
        co, si = cos[at : at + r], sin[at : at + r]
        q = z[:, :HD]
        k = z[:, HD : 2 * HD]
        q = (q * co + pltpu.roll(q, HD // 2, 1) * si) * (LOG2E * HD ** (-0.5))
        k = k * co + pltpu.roll(k, HD // 2, 1) * si
        out[at : at + r, :HD] = q.astype(BF16)
        out[at : at + r, HD : 2 * HD] = k.astype(BF16)
        out[at : at + r, 2 * HD :] = z[:, 2 * HD :].astype(BF16)
        at += r


def qkv_chunk(blk, chunk, pieces, w, scale, cos, sin):
    rows = [p.shape[0] for p in pieces]
    total = sum(rows)
    tokens = total // 2
    depth, width = w.shape
    heads = width // (3 * HD)

    def table(k):
        return pl.BlockSpec((tokens, HD), lambda h, b: (b[2 * chunk + k], 0))

    return pl.pallas_call(
        functools.partial(qkv_kernel, rows),
        grid_spec=pltpu.PrefetchScalarGridSpec(
            num_scalar_prefetch=1,
            grid=(heads,),
            in_specs=[pl.BlockSpec((r, depth), lambda h, b: (0, 0)) for r in rows]
            + [
                pl.BlockSpec((depth, 3 * HD), lambda h, b: (0, h)),
                pl.BlockSpec((1, 3 * HD), lambda h, b: (0, h)),
                table(0),
                table(1),
                table(0),
                table(1),
            ],
            out_specs=pl.BlockSpec((total, 3 * HD), lambda h, b: (0, h)),
        ),
        out_shape=jax.ShapeDtypeStruct((total, width), BF16),
        compiler_params=params(),
        cost_estimate=cost(2 * total * depth * width, 2 * (depth * width + total * depth)),
    )(blk, *pieces, w, scale, cos, cos, sin, sin)


def masked(scores, low, first_key, first_query, valid_count, diagonal):
    keys = first_key + lax.broadcasted_iota(jnp.int32, (scores.shape[0], 1), 0)
    if not diagonal:
        allowed = (keys >= low) & (keys < valid_count)
        return jnp.where(allowed, scores, NEG)
    queries = first_query + lax.broadcasted_iota(jnp.int32, (1, scores.shape[1]), 1)
    high = jnp.minimum(queries, valid_count - 1)
    allowed = ((keys >= low) & (keys <= high)) | (keys == queries)
    return jnp.where(allowed, scores, NEG)


def attn_fwd_kernel(n_chunks, tokens, bq, info, *refs):
    chunks = refs[:n_chunks]
    low, qkv_abs, att_abs, att_slot, lse, m_sc, l_sc, acc = refs[n_chunks:]
    i = pl.program_id(0)
    last = pl.num_programs(0) - 1
    heads = m_sc.shape[0]
    slots = 2 * n_chunks
    valid_count = info[slots]

    @pl.when(i == 0)
    def _():
        for s in range(slots):
            start = pl.multiple_of(info[s] * tokens, tokens)
            qkv_abs[pl.ds(start, tokens), :] = chunks[s // 2][
                (s % 2) * tokens : (s % 2 + 1) * tokens, :
            ]

    q0 = pl.multiple_of(i * bq, bq)
    rows = pl.ds(q0, bq)
    lo = low[:, rows]
    m_sc[...] = jnp.full(m_sc.shape, NEG, F32)
    l_sc[...] = jnp.zeros_like(l_sc)
    acc[...] = jnp.zeros_like(acc)

    def step(j, diagonal):
        k0 = pl.multiple_of(j * bq, bq)
        keys = pl.ds(k0, bq)
        for h in range(heads):
            at = 3 * HD * h
            q = qkv_abs[rows, at : at + HD]
            k = qkv_abs[keys, at + HD : at + 2 * HD]
            v = qkv_abs[keys, at + 2 * HD : at + 3 * HD]
            s = masked(mm(k, q, 1, 1), lo, k0, q0, valid_count, diagonal)
            m_old = m_sc[h]
            m_new = jnp.maximum(m_old, jnp.max(s, axis=0, keepdims=True))
            p = jnp.exp2(s - m_new)
            alpha = jnp.exp2(m_old - m_new)
            m_sc[h] = m_new
            l_sc[h] = l_sc[h] * alpha + jnp.sum(p, axis=0, keepdims=True)
            acc[h] = acc[h] * alpha + mm(v, p.astype(BF16), 0, 0)

    def full(j, carry):
        step(j, False)
        return carry

    lax.fori_loop(info[slots + 1 + i], i, full, 0)
    step(i, True)
    for h in range(heads):
        total = l_sc[h]
        lse[h, :, rows] = m_sc[h] + jnp.log2(total)
        att_abs[rows, h * HD : (h + 1) * HD] = (acc[h] / total).T.astype(BF16)

    @pl.when(i == last)
    def _():
        for s in range(slots):
            start = pl.multiple_of(info[s] * tokens, tokens)
            att_slot[s * tokens : (s + 1) * tokens, :] = att_abs[pl.ds(start, tokens), :]


def attn_fwd(info, chunks, low, tokens, bq):
    rows, width = chunks[0].shape
    heads = width // (3 * HD)
    seq = rows * len(chunks)
    n_blocks = seq // bq
    whole = pl.BlockSpec((seq, heads * HD), lambda i, f: (0, 0))
    return pl.pallas_call(
        functools.partial(attn_fwd_kernel, len(chunks), tokens, bq),
        grid_spec=pltpu.PrefetchScalarGridSpec(
            num_scalar_prefetch=1,
            grid=(n_blocks,),
            in_specs=[pl.BlockSpec((rows, width), lambda i, f: (0, 0))] * len(chunks)
            + [pl.BlockSpec((1, seq), lambda i, f: (0, 0))],
            out_specs=[
                pl.BlockSpec((seq, width), lambda i, f: (0, 0)),
                whole,
                whole,
                pl.BlockSpec((heads, 1, seq), lambda i, f: (0, 0, 0)),
            ],
            scratch_shapes=[
                pltpu.VMEM((heads, 1, bq), F32),
                pltpu.VMEM((heads, 1, bq), F32),
                pltpu.VMEM((heads, HD, bq), F32),
            ],
        ),
        out_shape=[
            jax.ShapeDtypeStruct((seq, width), BF16),
            jax.ShapeDtypeStruct((seq, heads * HD), BF16),
            jax.ShapeDtypeStruct((seq, heads * HD), BF16),
            jax.ShapeDtypeStruct((heads, 1, seq), F32),
        ],
        compiler_params=params(40),
        cost_estimate=cost(
            4 * heads * seq * seq * HD, 2 * seq * width * 3, heads * seq * seq // 2, 1
        ),
    )(info, *chunks, low)


def attn_bwd_kernel(n_chunks, tokens, bq, info, qkv, *refs):
    dos = refs[:n_chunks]
    att, lse, low, cos, sin, scale, dz, dc, do_abs, delta, dq, dk, dv = refs[n_chunks:]
    slots = 2 * n_chunks
    valid_count = info[slots]
    seq = qkv.shape[0]
    heads = dq.shape[0]
    n_blocks = seq // bq
    for s in range(slots):
        start = pl.multiple_of(info[s] * tokens, tokens)
        do_abs[pl.ds(start, tokens), :] = dos[s // 2][(s % 2) * tokens : (s % 2 + 1) * tokens, :]
    ones = jnp.ones((8, HD), F32)

    def sums(i, c):
        r = pl.ds(pl.multiple_of(i * bq, bq), bq)
        for h in range(heads):
            cols = slice(h * HD, (h + 1) * HD)
            prod = do_abs[r, cols].astype(F32) * att[r, cols].astype(F32)
            delta[h, :, r] = mm(ones, prod, 1, 1, lax.Precision.HIGHEST)[:1]
        return c

    lax.fori_loop(0, n_blocks, sums, 0)

    def outer(j, carry):
        k0 = pl.multiple_of(j * bq, bq)
        krow = pl.ds(k0, bq)

        def pair(i, diagonal):
            q0 = pl.multiple_of(i * bq, bq)
            qrow = pl.ds(q0, bq)
            lo = low[:, qrow]
            for h in range(heads):
                at = 3 * HD * h
                k = qkv[krow, at + HD : at + 2 * HD]
                v = qkv[krow, at + 2 * HD : at + 3 * HD]
                q = qkv[qrow, at : at + HD]
                do = do_abs[qrow, h * HD : (h + 1) * HD]
                s = masked(mm(k, q, 1, 1), lo, k0, q0, valid_count, diagonal)
                p = jnp.exp2(s - lse[h, :, qrow])
                dp = mm(v, do, 1, 1)
                ds = (p * (dp - delta[h, :, qrow])).astype(BF16)
                if diagonal:
                    dv[h, krow, :] = mm(p.astype(BF16), do)
                    dk[h, krow, :] = mm(ds, q)
                else:
                    dv[h, krow, :] += mm(p.astype(BF16), do)
                    dk[h, krow, :] += mm(ds, q)
                part = mm(ds, k, 0, 0)

                @pl.when(j == info[slots + 1 + i])
                def _():
                    dq[h, qrow, :] = part

                @pl.when(j > info[slots + 1 + i])
                def _():
                    dq[h, qrow, :] += part

        pair(j, True)

        def inner(i, c):
            @pl.when(info[slots + 1 + i] <= j)
            def _():
                pair(i, False)

            return c

        return lax.fori_loop(j + 1, n_blocks, inner, carry)

    lax.fori_loop(0, n_blocks, outer, 0)
    half = HD // 2
    dc[...] = jnp.zeros_like(dc)

    def finish(s, c):
        rows = pl.ds(pl.multiple_of(info[s] * tokens, tokens), tokens)
        out = pl.ds(pl.multiple_of(s * tokens, tokens), tokens)
        co, si = cos[rows, :], sin[rows, :]

        def back(u):
            return u * co - pltpu.roll(u, half, 1) * si

        for h in range(heads):
            at = 3 * HD * h
            qc, kc, vc = (slice(at + n * HD, at + (n + 1) * HD) for n in range(3))
            gq = back(dq[h, rows, :]) * HD ** (-0.5)
            gk = back(dk[h, rows, :]) * (1 / LOG2E)
            gv = dv[h, rows, :]
            q = back(qkv[rows, qc].astype(F32)) * (HD**0.5 / LOG2E)
            k = back(qkv[rows, kc].astype(F32))
            v = qkv[rows, vc].astype(F32)
            dc[:, qc] += jnp.sum(gq * q, axis=0, keepdims=True)
            dc[:, kc] += jnp.sum(gk * k, axis=0, keepdims=True)
            dc[:, vc] += jnp.sum(gv * v, axis=0, keepdims=True)
            dz[out, qc] = (gq * scale[:, qc]).astype(BF16)
            dz[out, kc] = (gk * scale[:, kc]).astype(BF16)
            dz[out, vc] = (gv * scale[:, vc]).astype(BF16)
        return c

    lax.fori_loop(0, slots, finish, 0)
    dc[...] = dc[...] / scale[...]


def attn_bwd(info, qkv_abs, do_chunks, att_abs, lse, low, cos, sin, scale, tokens, bq):
    seq, width = qkv_abs.shape
    heads = width // (3 * HD)
    return pl.pallas_call(
        functools.partial(attn_bwd_kernel, len(do_chunks), tokens, bq),
        in_specs=[SM] + [VM] * (len(do_chunks) + 7),
        out_specs=[VM] * 2,
        scratch_shapes=[
            pltpu.VMEM((seq, heads * HD), BF16),
            pltpu.VMEM((heads, 1, seq), F32),
            pltpu.VMEM((heads, seq, HD), F32),
            pltpu.VMEM((heads, seq, HD), F32),
            pltpu.VMEM((heads, seq, HD), F32),
        ],
        out_shape=[
            jax.ShapeDtypeStruct((seq, width), BF16),
            jax.ShapeDtypeStruct((1, width), F32),
        ],
        compiler_params=params(44),
        cost_estimate=cost(
            10 * heads * seq * seq * HD, 2 * seq * width * 4, heads * seq * seq // 2
        ),
    )(info, qkv_abs, *do_chunks, att_abs, lse, low, cos, sin, scale)


def mlp_kernel(rows, *refs):
    count = len(rows)
    xs = refs[:count]
    dhid, w, scale, hid, dz, dx_own, dx_mate, dc = refs[count:]
    tokens = dx_own.shape[0]
    sum_gate = jnp.zeros(scale.shape[1:], F32)
    sum_up = jnp.zeros(scale.shape[1:], F32)
    at = 0
    for x, r in zip(xs, rows):
        part = slice(at, at + r)
        xv = x[...]
        zg = mm(xv, w[0], 1, 1)
        zu = mm(xv, w[1], 1, 1)
        gate = zg * scale[0]
        up = zu * scale[1]
        s = 1.0 / (1.0 + jnp.exp(-gate))
        act = gate * s
        hid[part, :] = (act * up).astype(BF16)
        d = dhid[part, :].astype(F32)
        dgate = d * up * s * (1.0 + gate * (1.0 - s))
        dup = d * act
        sum_gate += jnp.sum(dgate * zg, axis=0, keepdims=True)
        sum_up += jnp.sum(dup * zu, axis=0, keepdims=True)
        dzg = (dgate * scale[0]).astype(BF16)
        dzu = (dup * scale[1]).astype(BF16)
        dz[0, part, :] = dzg
        dz[1, part, :] = dzu
        dx = (mm(dzg, w[0]) + mm(dzu, w[1])).astype(BF16)
        if at < tokens:
            dx_own[part, :] = dx
        else:
            dx_mate[at - tokens : at - tokens + r, :] = dx
        at += r
    dc[0] = sum_gate
    dc[1] = sum_up


def mlp_chunk(pieces, dhid, w, scale):
    rows = [p.shape[0] for p in pieces]
    total = sum(rows)
    _, width, depth = w.shape
    half = jax.ShapeDtypeStruct((total // 2, depth), BF16)
    return pl.pallas_call(
        functools.partial(mlp_kernel, rows),
        in_specs=[VM] * (len(pieces) + 3),
        out_specs=[VM] * 5,
        out_shape=[
            jax.ShapeDtypeStruct((total, width), BF16),
            jax.ShapeDtypeStruct((2, total, width), BF16),
            half,
            half,
            jax.ShapeDtypeStruct((2, 1, width), F32),
        ],
        compiler_params=params(),
        cost_estimate=cost(
            8 * total * depth * width, 4 * depth * width + 4 * total * depth, total * width
        ),
    )(*pieces, dhid, w, scale)


def rank_kernel(nx, nd, groups, turned, spans, *refs):
    xs = refs[:nx]
    ds = refs[nx : nx + nd]
    at, b, v, s, c, ga, gb = refs[nx + nd :]
    rank = at.shape[0]
    bs = [(b[g].astype(F32) * c[...]).astype(BF16) for g in range(groups)]
    share = rank // groups
    n_out = b.shape[2]
    ga_sum = None
    gb_sum = [None] * groups
    for xi, xa, di, da, r in spans:
        x = xs[xi][xa : xa + r, :]
        d = [ds[di][g, da : da + r, :] if groups > 1 else ds[di][da : da + r, :] for g in range(groups)]
        u = jnp.concatenate([mm(d[g], bs[g], 1, 1) for g in range(groups)], axis=1).astype(BF16)
        t = mm(x, at[...], 1, 1).astype(BF16)
        a_part = mm(u, x, 0, 0)
        ga_sum = a_part if ga_sum is None else ga_sum + a_part
        for g in range(groups):
            b_part = mm(t, d[g], 0, 0)
            gb_sum[g] = b_part if gb_sum[g] is None else gb_sum[g] + b_part
    for g in range(groups):
        rows = slice(g * share, (g + 1) * share)
        sv = s[g]
        sb = (b[g].astype(F32) * sv).astype(BF16)
        vg = v[g] if groups > 1 else v[...]
        back = mm(sb, vg, 1, 0 if turned else 1)
        ahead = mm(at[rows, :], vg, 1, 1 if turned else 0)
        ga[rows, :] = FACTOR * (ga_sum[rows, :] - back)
        gb[rows, :] = FACTOR * (gb_sum[g][rows, :] * c[...] - ahead * sv)


def rank_grads(xs, ds, at, b, v, s, turned=False, rows=None, scale=None):
    groups = b.shape[0]
    axis = 1 if groups > 1 else 0
    spans = []
    d_rows = used_rows(ds, rows) if rows else [d.shape[axis] for d in ds]
    xi = xa = di = da = 0
    while xi < len(xs):
        r = min(xs[xi].shape[0] - xa, d_rows[di] - da)
        spans.append((xi, xa, di, da, r))
        xa += r
        da += r
        if xa == xs[xi].shape[0]:
            xi, xa = xi + 1, 0
        if da == d_rows[di]:
            di, da = di + 1, 0
    total = sum(x.shape[0] for x in xs)
    rank, n_in = at.shape
    n_out = b.shape[2]
    return pl.pallas_call(
        functools.partial(rank_kernel, len(xs), len(ds), groups, turned, tuple(spans)),
        in_specs=[VM] * (len(xs) + len(ds) + 5),
        out_specs=[VM] * 2,
        out_shape=[
            jax.ShapeDtypeStruct((rank, n_in), F32),
            jax.ShapeDtypeStruct((rank, n_out), F32),
        ],
        compiler_params=params(),
        cost_estimate=cost(
            4 * total * (n_in + n_out * groups) * 256,
            2 * (total * (n_in + n_out * groups) + n_in * n_out * groups),
        ),
    )(*xs, *ds, at, b, v, s, jnp.ones((1, n_out), F32) if scale is None else scale)


def product_kernel(count, turned, spans, *refs):
    xs = refs[:count]
    w = refs[count]
    outs = refs[count + 1 :]
    for xi, oi, at, r in spans:
        outs[oi][at : at + r, :] = mm(xs[xi][...], w[...], 1, 1 if turned else 0).astype(BF16)


def used_rows(xs, tokens):
    rows = []
    left = tokens
    for x in xs:
        r = min(left, x.shape[0])
        rows.append(r)
        left -= r
        if left == 0:
            left = tokens
    return rows


def product(xs, w, turned, n_outs, steps, block=None, tokens=None):
    n = w.shape[0] if turned else w.shape[1]
    depth = w.shape[1] if turned else w.shape[0]
    tn = n // steps
    if block is not None:
        start, rows_in = block
        rows = [rows_in // n_outs] * n_outs
        x_specs = [
            pl.BlockSpec((r, depth), functools.partial(lambda k, i: (k, 0), start * n_outs + j))
            for j, r in enumerate(rows)
        ]
        xs = [xs] * n_outs
    else:
        rows = used_rows(xs, tokens) if tokens else [x.shape[0] for x in xs]
        x_specs = [pl.BlockSpec((r, depth), lambda i: (0, 0)) for r in rows]
    total = sum(rows)
    share = total // n_outs
    spans = []
    at = 0
    for xi, r in enumerate(rows):
        spans.append((xi, at // share, at % share, r))
        at += r
    w_spec = (
        pl.BlockSpec((tn, depth), lambda i: (i, 0))
        if turned
        else pl.BlockSpec((depth, tn), lambda i: (0, i))
    )
    return pl.pallas_call(
        functools.partial(product_kernel, len(xs), turned, tuple(spans)),
        grid=(steps,),
        in_specs=x_specs + [w_spec],
        out_specs=[pl.BlockSpec((share, tn), lambda i: (0, i))] * n_outs,
        out_shape=[jax.ShapeDtypeStruct((share, n), BF16)] * n_outs,
        compiler_params=params(),
        cost_estimate=cost(2 * total * n * depth, 2 * (n * depth + total * (n + depth))),
    )(*xs, w)


def down_kernel(rows, h, w, *refs):
    ds = refs[: len(rows)]
    own, other, dc = refs[len(rows) :]
    tokens = own.shape[0]
    total = jnp.zeros(dc.shape, F32)
    at = 0
    for d, r in zip(ds, rows):
        z = mm(h[at : at + r, :], w[...])
        total += jnp.sum(z * d[...].astype(F32), axis=0, keepdims=True)
        if at < tokens:
            own[at : at + r, :] = z.astype(BF16)
        else:
            other[at - tokens : at - tokens + r, :] = z.astype(BF16)
        at += r
    dc[...] = total


def down_product(h, w, ds):
    rows = [d.shape[0] for d in ds]
    total, depth = h.shape
    n = w.shape[1]
    tn = n // 2
    half = jax.ShapeDtypeStruct((total // 2, n), BF16)
    return pl.pallas_call(
        functools.partial(down_kernel, rows),
        grid=(2,),
        in_specs=[
            pl.BlockSpec((total, depth), lambda i: (0, 0)),
            pl.BlockSpec((depth, tn), lambda i: (0, i)),
        ]
        + [pl.BlockSpec((r, tn), lambda i: (0, i)) for r in rows],
        out_specs=[pl.BlockSpec((total // 2, tn), lambda i: (0, i))] * 2
        + [pl.BlockSpec((1, tn), lambda i: (0, i))],
        out_shape=[half, half, jax.ShapeDtypeStruct((1, n), F32)],
        compiler_params=params(),
        cost_estimate=cost(2 * total * n * depth, 2 * (n * depth + total * (2 * n + depth))),
    )(h, w, *ds)


def norm_forward(values):
    inverse = lax.rsqrt(jnp.mean(values * values, axis=-1, keepdims=True) + EPSILON)
    return values * inverse, inverse


def norm_backward(grad_normed, unit_vals, inverse, gain):
    scaled = grad_normed * gain
    return inverse * (scaled - unit_vals * jnp.mean(scaled * unit_vals, axis=-1, keepdims=True))


def after(value, *others):
    return lax.optimization_barrier((value,) + others)[0]


def on_device(
    sizes,
    layer_input,
    cotangent,
    segment_ids,
    token_valid,
    norm_attn,
    norm_mlp,
    base_qkv,
    base_attn_out,
    base_gate_up,
    base_down,
    rank_in_attn,
    rank_out_attn,
    magnitude_qkv,
    magnitude_out,
    rank_in_mlp,
    rank_out_mlp,
    magnitude_mlp,
    rank_in_down,
    rank_out_down,
    magnitude_down,
):
    X, C, ZH, ZL, Y = (sizes[a] for a in AXES)
    ix, ic, izh, izl, iy = (lax.axis_index(a) for a in AXES)
    dp, mp = X * C, ZH * ZL * Y
    n_dev = dp * mp
    tokens, model = layer_input.shape
    seq_len = segment_ids.shape[0]
    width = base_qkv.shape[2]
    hidden = base_gate_up.shape[2]
    heads = width // HD
    a_w = rank_in_attn.shape[1]
    f_w = rank_in_down.shape[0]
    used = 11 * a_w + 3 * f_w
    packed_w = -(-used // 128) * 128
    bq = min(512, seq_len)
    stay = ic == izh

    def from_offset(a, axis, k):
        n = sizes[axis]
        return lax.ppermute(a, axis, [(s, (s - k) % n) for s in range(n)])

    def to_offset(a, axis, k):
        n = sizes[axis]
        return lax.ppermute(a, axis, [(s, (s + k) % n) for s in range(n)])

    def mate(a):
        return from_offset(a, "c", 1)

    offsets = [(dz, dy) for dz in range(ZL) for dy in range(Y)]
    n_chips = len(offsets)

    def chips(a, off, sign):
        dz, dy = off
        perm = []
        for z in range(ZL):
            for y in range(Y):
                perm.append((z * Y + y, (z + sign * dz) % ZL * Y + (y + sign * dy) % Y))
        return lax.ppermute(a, ("zl", "y"), perm)

    def swap_rows(a):
        return lax.ppermute(a, ("c", "zh"), [(1, 2), (2, 1)])

    last = [None]

    def seq(x):
        return x if last[0] is None else after(x, last[0])

    def mark(x):
        last[0] = x
        return x

    relayed = ZL == 2 and Y == 2

    def gather_start(a):
        if relayed:
            return [[a, mate(a)], [chips(a, (0, 1), -1)], [chips(a, (1, 0), -1)]]
        return [[a, mate(a)]] + [[chips(a, o, -1)] for o in offsets[1:]]

    def gather_next(got):
        py, pz = seq(got[1][0]), seq(got[-1][0])
        if relayed:
            half = tokens // 2
            d0 = chips(pz[:half], (0, 1), -1)
            d1 = chips(py[half:], (1, 0), -1)
            return [got[0], [py, mate(py)], [pz, mate(pz)], [d0, d1]]
        return [got[0]] + [[g[0], mate(seq(g[0]))] for g in got[1:]]

    def gather_last(got):
        if relayed:
            d0, d1 = seq(got[3][0]), seq(got[3][1])
            return got[:3] + [[d0, d1, mate(d0), mate(d1)]]
        return got

    def block_of(own, other, wide=False):
        block = own.astype(F32) + mate(other).astype(F32)
        return block if wide else block.astype(BF16)

    def scatter_end(own, arrived):
        for a in arrived:
            own = own + a.astype(F32)
        return own

    def product_blocks(make, between=None):
        parts = [None] * n_chips
        for o in range(n_chips)[::-1]:
            parts[o] = make(o)
            mark(parts[o][0])
        blocks = [None] * n_chips
        if between is not None:
            blocks.append(between())
        here = last[0]

        def gated(x):
            return x if between is None else after(x, here)

        for o in range(n_chips)[::-1]:
            own, other = parts[o]
            blocks[o] = mark(block_of(seq(own), gated(other), wide=o == 0))
        return blocks

    def send_blocks(blocks):
        return [chips(blocks[o], offsets[o], 1) for o in range(1, n_chips)[::-1]]

    def square_sum(a):
        total = a
        for axis in ("c", "zl", "y"):
            total = sum((from_offset(total, axis, k) for k in range(1, sizes[axis])), total)
        return total

    place = np.zeros((n_dev, 2 * n_dev + 4 + 2 * n_chips), np.int32)
    for own in range(n_dev):
        x, c, zh, zl, y = np.unravel_index(own, (X, C, ZH, ZL, Y))
        xs, cs, zhs, zls, ys = np.unravel_index(np.arange(n_dev), (X, C, ZH, ZL, Y))
        order = (cs - c) % C
        order = order * X + (xs - x) % X
        order = order * Y + (ys - y) % Y
        order = order * ZL + (zls - zl) % ZL
        order = order * ZH + (zhs - zh) % ZH
        send = ((((cs - c) % C * X + xs) * ZH + zhs) * ZL + zls) * Y + ys
        blocks = [
            ((c + k) % 2 * ZL + (zl + dz) % ZL) * Y + (y + dy) % Y
            for dz, dy in offsets
            for k in range(2)
        ]
        place[own, :n_dev] = order
        place[own, n_dev : n_dev + 2] = (c * ZL + zl) * Y + y, (zh * ZL + zl) * Y + y
        place[own, n_dev + 2 : n_dev + 4] = int(c == zh), x
        place[own, n_dev + 4 : n_dev + 4 + 2 * n_chips] = blocks
        place[own, n_dev + 4 + 2 * n_chips :] = send
    own_id = (((ix * C + ic) * ZH + izh) * ZL + izl) * Y + iy
    row = lax.dynamic_slice_in_dim(jnp.asarray(place), own_id, 1, 0)[0]
    table = row[: n_dev + 2]
    flags = row[n_dev + 2 : n_dev + 4]
    blk = row[n_dev + 4 : n_dev + 4 + 2 * n_chips]
    send_table = jnp.concatenate([row[n_dev + 4 + 2 * n_chips :], row[n_dev : n_dev + 2]])

    def sds(shape, dtype=BF16):
        return jax.ShapeDtypeStruct(shape, dtype)

    packed = pl.pallas_call(
        functools.partial(pack_kernel, a_w, f_w),
        in_specs=[VM] * 10,
        out_specs=VM,
        out_shape=sds((1, R + 1, packed_w)),
    )(
        jnp.swapaxes(rank_in_attn, 1, 2),
        rank_out_attn,
        magnitude_qkv,
        magnitude_out[None],
        jnp.swapaxes(rank_in_mlp, 1, 2),
        rank_out_mlp,
        magnitude_mlp,
        rank_in_down.T[None],
        rank_out_down[None],
        magnitude_down[None],
    )
    def over_z(a):
        found = []
        for k in range(1, ZL * ZH):
            dl, dh = divmod(k, ZH)
            perm = []
            for zh in range(ZH):
                for zl in range(ZL):
                    perm.append((zh * ZL + zl, (zh - dh) % ZH * ZL + (zl - dl) % ZL))
            found.append(lax.ppermute(a, ("zh", "zl"), perm))
        return found

    gathered = jnp.concatenate([packed] + over_z(packed), axis=0)
    moved_input = swap_rows(after(layer_input, packed))
    for axis in ("y", "x", "c"):
        gathered = jnp.concatenate(
            [gathered] + [from_offset(gathered, axis, k) for k in range(1, sizes[axis])], axis=0
        )
    mark(gathered)

    def cut(w, axis, member=None):
        part = w.shape[axis] // X
        start = [0] * w.ndim
        size = list(w.shape)
        start[axis] = ix * part
        size[axis] = part
        if member is not None:
            start[0], size[0] = member, 1
        return lax.dynamic_slice(w, start, size)

    def fetch(mine, *gate):
        mine = after(mine, *gate) if gate else mine
        return lax.ppermute(mine, ("c", "zh"), [(0, 1), (3, 2)])

    def fetch_rest(mine):
        mine = seq(mine)
        parts = [mine]
        for k in range(1, X):
            perm = []
            for x in range(X):
                for cz in (1, 2):
                    perm.append((x * 4 + cz, (x - k) % X * 4 + cz))
            parts.append(lax.ppermute(mine, ("x", "c", "zh"), perm))
        return parts

    turned_gu = jnp.swapaxes(base_gate_up, 1, 2)
    mine_qkv = fetch(cut(base_qkv, 1))
    cuts = [
        cut(base_attn_out, 1),
        cut(turned_gu, 2, 0),
        cut(turned_gu, 2, 1),
        cut(base_down, 1),
    ]
    local_input = jnp.where(stay, layer_input, seq(moved_input))
    gain_one = norm_attn.astype(F32)
    gain_two = norm_mlp.astype(F32)
    input_full = local_input.astype(F32)
    unit_one, inverse_one = norm_forward(input_full)
    normed_one = mark((unit_one * gain_one).astype(BF16))
    one = gather_start(normed_one)

    gathered = after(gathered, *cuts)

    (
        at_qkv, at_gu, at_o, at_d, at_o0, at_d0, b_qkv, b_blocks, b_gu, b_o, b_d, mags_qkv, m_o, m_gu, m_d,
    ) = pl.pallas_call(
        functools.partial(unpack_kernel, a_w, f_w, dp),
        in_specs=[SM, VM],
        out_specs=[VM] * 15,
        out_shape=[
            sds((3 * R, model)),
            sds((2, R, model)),
            sds((R, width)),
            sds((R, hidden)),
            sds((R, width)),
            sds((R, hidden)),
            sds((3, R, width)),
            sds((3 * R, 3 * width)),
            sds((2, R, hidden)),
            sds((R, model)),
            sds((R, model)),
            sds((1, 3 * width), F32),
            sds((1, model), F32),
            sds((2, 1, hidden), F32),
            sds((1, model), F32),
        ],
    )(table, seq(gathered))
    mark(at_qkv)

    rows_here = jnp.stack([segment_ids, token_valid])
    rows_here = jnp.where(stay, rows_here, mate(rows_here))
    segments, valid = rows_here[0], rows_here[1]
    steps = jnp.arange(seq_len, dtype=jnp.int32)
    earlier = jnp.concatenate([segments[:1] - 1, segments[:-1]])
    first = lax.cummax(jnp.where(segments != earlier, steps, 0), axis=0)
    low = first[None]
    positions = seq(steps - first)
    frequency = ROPE_BASE ** (-(2.0 * jnp.arange(HD // 2, dtype=F32)) / HD)
    sign = jnp.concatenate([-jnp.ones(HD // 2, F32), jnp.ones(HD // 2, F32)])
    angle = positions.astype(F32)[:, None] * jnp.concatenate([frequency, frequency])[None, :]
    cos, sin = jnp.cos(angle), jnp.sin(angle) * sign[None, :]
    info = jnp.concatenate([blk, jnp.sum(valid)[None].astype(jnp.int32), first[::bq] // bq])
    mark(cos)

    def rows_square(base, at0, b):
        v = base.astype(F32) + FACTOR * mm(at0, b, 0, 0)
        return jnp.sum(v * v, axis=0)

    squares = jnp.stack(
        [rows_square(base_attn_out, seq(at_o0), b_o), rows_square(base_down, seq(at_d0), b_d)]
    )
    mark(squares)

    def add_over(a, axis):
        return sum((from_offset(a, axis, k) for k in range(1, sizes[axis])), a)

    one = gather_next(one)
    parts_qkv = fetch_rest(mine_qkv)
    mine_o = fetch(cuts[0], parts_qkv[0])
    moved_cot = swap_rows(after(cotangent, parts_qkv[0]))
    one = gather_last(one)
    mine_gate = fetch(cuts[1], one[-1][0])
    v_qkv, square_qkv = merge_qkv(flags, base_qkv, parts_qkv, seq(at_qkv), b_qkv)
    mark(square_qkv)
    norms_qkv = jnp.sqrt(square_qkv)
    scale_qkv = mark(mags_qkv / norms_qkv)

    qkv = []
    for o in range(n_chips):
        qkv.append(mark(qkv_chunk(blk, o, one[o], v_qkv, seq(scale_qkv), cos, sin)))
        if o == 1:
            mine_o = mark(seq(mine_o))
            parts_o = fetch_rest(mine_o)
    local_cot = mark(jnp.where(stay, cotangent, seq(moved_cot)))
    grad_output = local_cot.astype(F32)
    rest_gate = fetch_rest(mine_gate)
    down = [[local_cot, mate(local_cot)]] + [[chips(local_cot, o, -1)] for o in offsets[1 : Y + 1]]
    mine_up = fetch(cuts[2], local_cot)
    column = over_z(squares)
    qkv_abs, att_abs, att_slot, lse = attn_fwd(info, qkv, seq(low), tokens, bq)
    mark(lse)
    for i in range(1, Y + 1):
        down[i] = [mark(seq(down[i][0]))]
    squares = add_over(mark(sum(column, seq(squares))), "y")
    v_o = mark(merge_rows(flags, base_attn_out, parts_o, seq(at_o), b_o))
    rest_up = fetch_rest(mine_up)
    blocks = product_blocks(
        lambda o: product(att_slot, seq(v_o), False, 2, 2, block=(o, 2 * tokens))
    )
    arrived = send_blocks(blocks)
    down += [[chips(seq(down[Y][0]), o, -1)] for o in offsets[1:Y]]
    down[1:] = [[p[0], mate(seq(p[0]))] for p in down[1 : Y + 1]] + down[Y + 1 :]
    mine_d = fetch(cuts[3], blocks[1])
    v_gu, square_gu = merge_gu(flags, turned_gu, rest_gate, rest_up, seq(at_gu), b_gu)
    norms_gu = jnp.sqrt(square_gu)
    scale_gu = mark(m_gu / norms_gu)
    norms_rows = jnp.sqrt(squares)
    norms_o, norms_d = norms_rows[0:1], norms_rows[1:2]
    scale_o = m_o / norms_o
    scale_d = m_d / norms_d
    summed_out = scatter_end(seq(blocks[0]), arrived)
    residual = input_full + summed_out * scale_o
    unit_two, inverse_two = norm_forward(residual)
    normed_two = mark((unit_two * gain_two).astype(BF16))
    two = gather_start(normed_two)

    parts_d = fetch_rest(mine_d)
    for i in range(Y + 1, n_chips):
        down[i].append(mate(seq(down[i][0])))
    v_d, v_ds = merge_down(flags, base_down, parts_d, seq(at_d), b_d, scale_d)
    mark(v_d)
    dhid = []
    for o in range(n_chips):
        dhid.append(mark(product(down[o], seq(v_ds), True, 1, 1)[0]))
    two = gather_next(two)

    hid, dz_gu, parts, dc_gu = [], [], [], 0.0
    blocks = [None] * n_chips
    for o in range(n_chips):
        if o == n_chips - 1:
            two = gather_last(two)
        h, dz, own, other, dc = mlp_chunk(two[o], dhid[o], v_gu, seq(scale_gu))
        mark(h)
        hid.append(h)
        dz_gu.append(dz)
        parts.append((own, other))
        dc_gu = dc_gu + dc
    blocks = [None] * n_chips
    for o in list(range(1, n_chips)) + [0]:
        blocks[o] = mark(block_of(seq(parts[o][0]), parts[o][1], wide=o == 0))
    arrived = send_blocks(blocks)
    down_parts = []
    dc_down = 0.0
    for o in range(n_chips):
        own, other, dc = down_product(hid[o], seq(v_d), down[o])
        mark(dc)
        dc_down = dc_down + dc
        down_parts.append((own, other))
    def shrink(col, mags, norms):
        return col * mags / (norms * norms * norms)

    def flat(lists):
        return [p for pieces in lists for p in pieces]

    ga_gu, gb_gu = rank_grads(
        flat(two),
        dz_gu,
        seq(at_gu).reshape(2 * R, model),
        b_gu,
        v_gu,
        shrink(dc_gu, m_gu, norms_gu),
        turned=True,
    )
    mark(ga_gu)
    grad_normed_two = scatter_end(seq(blocks[0]), arrived)
    grad_residual = grad_output + norm_backward(grad_normed_two, unit_two, inverse_two, gain_two)
    col_out = jnp.sum(grad_residual * summed_out, axis=0, keepdims=True)
    extra = jnp.concatenate([col_out, dc_down, jnp.zeros((14, model), F32)], axis=0)
    low_out = mark(
        jnp.concatenate([(grad_residual * scale_o).astype(BF16), extra.astype(BF16)], axis=0)
    )
    out = gather_start(low_out)

    down_blocks = [block_of(seq(p[0]), p[1], wide=o == 0) for o, p in enumerate(down_parts)]
    mark(down_blocks[-1])
    out = gather_next(out)

    def tails(lists):
        found = []
        for pieces in lists:
            n = len(pieces) // 2
            found += [pieces[n - 1][-16:], pieces[-1][-16:]]
        return found

    do_chunks = []
    for o in range(n_chips):
        if o == n_chips - 1:
            out = gather_last(out)
        do_chunks.append(mark(product(out[o], seq(v_o), True, 1, 1, tokens=tokens)[0]))
    cols = sum(p[:2].astype(F32) for p in tails(out))
    arrived_down = send_blocks([seq(b) for b in down_blocks])
    dz_qkv, dc_qkv = attn_bwd(
        info, qkv_abs, do_chunks, att_abs, lse, seq(low), cos, sin, scale_qkv, tokens, bq
    )
    mark(dc_qkv)
    blocks = product_blocks(
        lambda o: product(dz_qkv, seq(v_qkv), True, 2, 2, block=(o, 2 * tokens)),
        lambda: mark(
            (residual + scatter_end(seq(down_blocks[0]), arrived_down) * scale_d).astype(BF16)
        ),
    )
    output_here = blocks.pop()
    moved_output = swap_rows(output_here)
    arrived = send_blocks(blocks)

    ga_qkv, gb_all = rank_grads(
        flat(one),
        [dz_qkv],
        seq(at_qkv),
        b_blocks[None],
        v_qkv,
        shrink(dc_qkv, mags_qkv, norms_qkv)[None],
    )
    mark(ga_qkv)
    ga_o, gb_o = rank_grads(
        [att_slot],
        flat(out),
        seq(at_o),
        b_o[None],
        v_o,
        shrink(cols[0:1], m_o, norms_o)[None],
        rows=tokens,
    )
    mark(ga_o)
    ga_d, gb_d = rank_grads(
        hid,
        flat(down),
        seq(at_d),
        b_d[None],
        v_d,
        shrink(cols[1:2], m_d, norms_d)[None],
        scale=scale_d,
    )
    mark(ga_d)
    mag_full = jnp.concatenate([col_out / norms_o, dc_down / norms_d], axis=0)
    grads = pl.pallas_call(
        functools.partial(pack_grads_kernel, a_w, f_w, dp),
        in_specs=[SM] + [VM] * 11,
        out_specs=VM,
        out_shape=sds((n_dev, R + 1, packed_w)),
    )(
        send_table,
        seq(ga_qkv),
        ga_gu,
        gb_o,
        gb_d,
        mag_full,
        ga_o,
        ga_d,
        gb_all,
        gb_gu,
        dc_qkv / norms_qkv,
        dc_gu / norms_gu,
    )
    mark(grads)
    layer_output = mark(jnp.where(stay, output_here, seq(moved_output)))
    grad_normed_one = scatter_end(seq(blocks[0]), arrived)
    grad_here = grad_residual + norm_backward(grad_normed_one, unit_one, inverse_one, gain_one)
    low_here = mark(grad_here.astype(BF16))
    input_grad = jnp.where(stay, grad_here, swap_rows(low_here).astype(F32))
    half = n_dev // 2
    grads = seq(grads)
    grads = grads[:half].astype(F32) + mate(grads[half:]).astype(F32)
    pieces = lax.all_to_all(
        grads.astype(BF16), ("x", "zh", "zl", "y"), split_axis=0, concat_axis=0, tiled=True
    )
    grads = jnp.sum(pieces.astype(F32), axis=0, keepdims=True)
    a1, b1, mq, mo, a2, b2, mm_, a3, b3, md = pl.pallas_call(
        functools.partial(unpack_grads_kernel, a_w, f_w),
        in_specs=[VM],
        out_specs=[VM] * 10,
        out_shape=[
            sds((4, R, a_w), F32),
            sds((4, R, a_w), F32),
            sds((3, a_w), F32),
            sds((1, a_w), F32),
            sds((2, R, a_w), F32),
            sds((2, R, f_w), F32),
            sds((2, f_w), F32),
            sds((1, R, f_w), F32),
            sds((1, R, a_w), F32),
            sds((1, a_w), F32),
        ],
    )(grads)
    return (
        layer_output,
        input_grad,
        jnp.swapaxes(a1, 1, 2),
        b1,
        mq,
        mo[0],
        jnp.swapaxes(a2, 1, 2),
        b2,
        mm_,
        a3[0].T,
        b3[0],
        md[0],
    )


def solution(mesh):
    dp, mp = mesh.shape["dp"], mesh.shape["mp"]
    shape = (dp // 2, 2, 2, 2, mp // 4)
    fine = Mesh(mesh.devices.reshape(shape), AXES)
    rows, cols = ("x", "c"), ("zh", "zl", "y")
    both = rows + cols
    return jax.shard_map(
        functools.partial(on_device, dict(zip(AXES, shape))),
        mesh=fine,
        in_specs=(
            P(both, None),
            P(both, None),
            P(rows),
            P(rows),
            P(),
            P(),
            P(None, None, cols),
            P(cols, None),
            P(None, None, cols),
            P(cols, None),
            P(None, both, None),
            P(None, None, both),
            P(None, both),
            P(both),
            P(None, both, None),
            P(None, None, both),
            P(None, both),
            P(both, None),
            P(None, both),
            P(both),
        ),
        out_specs=(
            P(both, None),
            P(both, None),
            P(None, both, None),
            P(None, None, both),
            P(None, both),
            P(both),
            P(None, both, None),
            P(None, None, both),
            P(None, both),
            P(both, None),
            P(None, both),
            P(both),
        ),
        check_vma=False,
    )
```
